256 devices in a mesh: row: 16 (over z_lo, x), col: 16 (over y, z_hi, core).
Axes of the slice: x: 4, y: 4, z: 8 (z_hi: 2, z_lo: 4; z = z_hi * 4 + z_lo), core: 2. Of those that a mesh axis runs over, the one named last changes fastest.
Arguments:
- offsets: int32 [16, 16, 2], P('row', 'col'), may hold values from 1 to 3
- targets: float32 [3, 3, 512, 2048], P(None, None, 'row', 'col'), may hold values from -60 to 60
- grid_fine: float32 [32, 512, 2048], P(None, 'row', 'col'), may hold values from -6 to 6
- grid_coarse: float32 [32, 128, 512], P(None, 'row', 'col'), may hold values from -6 to 6
- weight_in: float32 [512, 64], replicated, may hold values from -0.75 to 0.75
- weight_mid: float32 [1, 512, 512], replicated, may hold values from -0.25 to 0.25
- weight_out: float32 [3, 512], replicated, may hold values from -0.397747564 to 0.397747564
- fine_first: float32 [32, 512, 2048], P(None, 'row', 'col'), may hold values from -0.012 to 0.012
- fine_second: float32 [32, 512, 2048], P(None, 'row', 'col'), may hold values from 1e-06 to 0.0001
- coarse_first: float32 [32, 128, 512], P(None, 'row', 'col'), may hold values from -0.012 to 0.012
- coarse_second: float32 [32, 128, 512], P(None, 'row', 'col'), may hold values from 1e-06 to 0.0001
- in_first: float32 [512, 64], replicated, may hold values from -0.012 to 0.012
- in_second: float32 [512, 64], replicated, may hold values from 1e-06 to 0.0001
- mid_first: float32 [1, 512, 512], replicated, may hold values from -0.012 to 0.012
- mid_second: float32 [1, 512, 512], replicated, may hold values from 1e-06 to 0.0001
- out_first: float32 [3, 512], replicated, may hold values from -0.012 to 0.012
- out_second: float32 [3, 512], replicated, may hold values from 1e-06 to 0.0001
Outputs:
- fine_step: float32 [32, 512, 2048], P(None, 'row', 'col')
- coarse_step: float32 [32, 128, 512], P(None, 'row', 'col')
- input_step: float32 [512, 64], replicated
- middle_step: float32 [1, 512, 512], replicated
- output_step: float32 [3, 512], replicated
The draws below stay inside these ranges and needn't reach their ends.
All inputs are finite; a program needn't handle non-finite values.
Results may differ from the reference program's by a relative error of at most 0.0014.
The reference program's roundings to bfloat16 on the way count: a program that leaves them out, or rounds other values in their place, can miss the bound.
Values sent between devices are 32-bit elements; how exact they have to be, the bound alone decides.
No kernel may reach another device: no remote copies, remote signals or barrier semaphores. Data moves between devices by JAX's collectives and lax.ppermute only.
A program may use at most 64 MiB of HBM per device.

```python
import math
import jax
import jax.numpy as jnp
from jax import lax

CH = 32
HID = 512
MID = 1
OUT = 3
SUB = 4
RATIO = 4
ADAM_STEP = 10
SR = 32
SC = 128
TILE_ROWS = 16
TILE_COLS = 16
ROWS = 512
COLS = 2048
CROWS = 128
CCOLS = 512
N_ROW = 16
N_COL = 16


def draw_targets(key, part):
    row_level = jnp.arange(ROWS, dtype=jnp.float32) / ROWS
    col_level = jnp.arange(COLS, dtype=jnp.float32) / COLS
    exponent = 0.5 * (row_level[:, None] + col_level[None, :])
    noise = jnp.clip(jax.random.normal(key, (3, OUT, ROWS, COLS), jnp.float32), -4.0, 4.0)
    return noise * 10.0 ** exponent


def draw_weight_out(key, part):
    column_level = 0.3 * 10.0 ** (jnp.arange(HID, dtype=jnp.float32) / (HID - 1))
    noise = jnp.clip(jax.random.normal(key, (OUT, HID), jnp.float32), -3.0, 3.0)
    return noise * column_level[None, :] / HID ** 0.5


def set_ends(values, key, least, top_value):
    extent = values.shape
    index_at = [jax.random.randint(jax.random.fold_in(key, axis), (), 0, extent[axis]) for axis in range(len(extent))]
    values = values.at[tuple(index_at)].set(least)
    longest = extent.index(max(extent))
    index_at[longest] = (index_at[longest] + 1) % extent[longest]
    return values.at[tuple(index_at)].set(top_value)


def block_levels(key, extent, pieces, smallest, top_value):
    level = 1.0
    for axis_at, parts in pieces:
        steps = jax.random.uniform(jax.random.fold_in(jax.random.fold_in(key, 6), axis_at), (parts,), jnp.float32, smallest / len(pieces), top_value / len(pieces))
        level = level * jnp.repeat(jnp.exp(steps), extent[axis_at] // parts).reshape((-1,) + (1,) * (len(extent) - 1 - axis_at))
    return level


def scatter_about(own_key, dims, deviation, reach, split=(), held_as=jnp.bfloat16):
    result = deviation * jax.random.normal(own_key, dims, jnp.float32)
    if split:
        result = result * block_levels(own_key, dims, split, -0.22, 0.18)
    return jnp.clip(result, -reach, reach).astype(held_as)


def setup_inputs(seed: int = 0) -> dict:
    key_of = jax.random.split(jax.random.key(seed), 18)
    return {
        "offsets": set_ends(jax.random.randint(key_of[0], (TILE_ROWS, TILE_COLS, 2), 1, SUB), jax.random.fold_in(key_of[0], 1), 1, SUB - 1).astype(jnp.int32),
        "targets": draw_targets(jax.random.fold_in(key_of[17], 71), 0),
        "grid_fine": scatter_about(key_of[2], (CH, ROWS, COLS), 1.0, 6.0, ((1, 16), (2, 16)), jnp.float32),
        "grid_coarse": scatter_about(key_of[3], (CH, CROWS, CCOLS), 1.0, 6.0, ((1, 16), (2, 16)), jnp.float32),
        "weight_in": scatter_about(key_of[4], (HID, 2 * CH), (2 * CH) ** -0.5, 0.75, (), jnp.float32),
        "weight_mid": scatter_about(key_of[5], (MID, HID, HID), HID ** -0.5, 0.25, (), jnp.float32),
        "weight_out": draw_weight_out(jax.random.fold_in(key_of[17], 71), 0),
        "fine_first": scatter_about(key_of[7], (CH, ROWS, COLS), 0.002, 0.012, ((1, 16), (2, 16)), jnp.float32),
        "fine_second": jnp.clip(jnp.exp(math.log(0.0001) - 4.6051702 * jax.random.uniform(key_of[8], (CH, ROWS, COLS), jnp.float32) ** block_levels(key_of[8], (CH, ROWS, COLS), ((1, 16), (2, 16)), -0.2, 0.2)), 9.999999974752427e-07, 0.0001),
        "coarse_first": scatter_about(key_of[9], (CH, CROWS, CCOLS), 0.002, 0.012, ((1, 16), (2, 16)), jnp.float32),
        "coarse_second": jnp.clip(jnp.exp(math.log(0.0001) - 4.6051702 * jax.random.uniform(key_of[10], (CH, CROWS, CCOLS), jnp.float32) ** block_levels(key_of[10], (CH, CROWS, CCOLS), ((1, 16), (2, 16)), -0.2, 0.2)), 9.999999974752427e-07, 0.0001),
        "in_first": scatter_about(key_of[11], (HID, 2 * CH), 0.002, 0.012, (), jnp.float32),
        "in_second": jnp.clip(jnp.exp(jax.random.uniform(key_of[12], (HID, 2 * CH), jnp.float32, math.log(9.999999974752427e-07), math.log(0.0001))), 9.999999974752427e-07, 0.0001),
        "mid_first": scatter_about(key_of[13], (MID, HID, HID), 0.002, 0.012, (), jnp.float32),
        "mid_second": jnp.clip(jnp.exp(jax.random.uniform(key_of[14], (MID, HID, HID), jnp.float32, math.log(9.999999974752427e-07), math.log(0.0001))), 9.999999974752427e-07, 0.0001),
        "out_first": scatter_about(key_of[15], (OUT, HID), 0.002, 0.012, (), jnp.float32),
        "out_second": jnp.clip(jnp.exp(jax.random.uniform(key_of[16], (OUT, HID), jnp.float32, math.log(9.999999974752427e-07), math.log(0.0001))), 9.999999974752427e-07, 0.0001),
    }


BETA_ONE = 0.9
BETA_TWO = 0.99
ADAM_EPSILON = 1e-08
CLIP_RMS = 0.01
LOSS_VALUE = 0.25
MEAN_EPSILON = 1e-06

def interp_table(samples, level_ratio, offset):
    positions = jnp.arange(samples, dtype=jnp.int32)
    base_index = positions // level_ratio
    fraction = ((positions % level_ratio).astype(jnp.float32) + offset.astype(jnp.float32) / SUB) / level_ratio
    column = jnp.arange(samples // level_ratio + 1, dtype=jnp.int32)
    lower_hit = (column[None, :] == base_index[:, None]).astype(jnp.float32)
    upper_hit = (column[None, :] == base_index[:, None] + 1).astype(jnp.float32)
    return lower_hit * (1.0 - fraction)[:, None] + upper_hit * fraction[:, None]

def level_tables(row_count, col_count, shift_y, shift_x):
    return (interp_table(row_count, 1, shift_y), interp_table(col_count, 1, shift_x), interp_table(row_count, RATIO, shift_y), interp_table(col_count, RATIO, shift_x))

def sample_level(extended, row_table, col_table):
    across = jnp.einsum('kjl,ml->kjm', extended, col_table, precision=lax.Precision.HIGHEST)
    return jnp.einsum('ij,kjm->kim', row_table, across, precision=lax.Precision.HIGHEST)

def spread_level(cotangent, row_table, col_table):
    backward = jnp.einsum('ij,kim->kjm', row_table, cotangent, precision=lax.Precision.HIGHEST)
    return jnp.einsum('kjm,ml->kjl', backward, col_table, precision=lax.Precision.HIGHEST)

def sample_features(fine_ext, coarse_ext, tables):
    fine_feat = sample_level(fine_ext, tables[0], tables[1])
    coarse_feat = sample_level(coarse_ext, tables[2], tables[3])
    channels, row_count, col_count = fine_feat.shape
    return jnp.concatenate([fine_feat.reshape(channels, row_count * col_count), coarse_feat.reshape(channels, row_count * col_count)], axis=0).astype(jnp.bfloat16)

def spread_features(feature_grad, tables):
    channels = feature_grad.shape[0] // 2
    row_count = tables[0].shape[0]
    col_count = tables[1].shape[0]
    fine_cot = feature_grad[:channels].reshape(channels, row_count, col_count)
    coarse_cot = feature_grad[channels:].reshape(channels, row_count, col_count)
    return (spread_level(fine_cot, tables[0], tables[1]), spread_level(coarse_cot, tables[2], tables[3]))

def matmul(former, latter):
    return jnp.dot(former, latter, preferred_element_type=jnp.float32)

def contract_rows(former, latter):
    return lax.dot_general(former, latter, (((0,), (0,)), ((), ())), preferred_element_type=jnp.float32)

def contract_cols(former, latter):
    return lax.dot_general(former, latter, (((1,), (1,)), ((), ())), preferred_element_type=jnp.float32)

def silu_slope(pre_act):
    sigmoid = jax.nn.sigmoid(pre_act)
    return sigmoid * (1.0 + pre_act * (1.0 - sigmoid))

def decoder_forward(features, low_in, low_mid, low_out):
    pre_acts = [matmul(low_in, features)]
    activations = [jax.nn.silu(pre_acts[0]).astype(jnp.bfloat16)]
    for layer_index in range(low_mid.shape[0]):
        pre_acts.append(matmul(low_mid[layer_index], activations[-1]))
        activations.append(jax.nn.silu(pre_acts[-1]).astype(jnp.bfloat16))
    return (matmul(low_out, activations[-1]), pre_acts, activations)

def decoder_backward(features, pre_acts, activations, cotangent, low_in, low_mid, low_out):
    out_cotangent = cotangent.astype(jnp.bfloat16)
    grad_out = contract_cols(out_cotangent, activations[-1])
    upward = contract_rows(low_out, out_cotangent)
    grads_mid = []
    for layer_index in range(low_mid.shape[0] - 1, -1, -1):
        delta_low = (upward * silu_slope(pre_acts[layer_index + 1])).astype(jnp.bfloat16)
        grads_mid.insert(0, contract_cols(delta_low, activations[layer_index]))
        upward = contract_rows(low_mid[layer_index], delta_low)
    delta_low = (upward * silu_slope(pre_acts[0])).astype(jnp.bfloat16)
    grad_in = contract_cols(delta_low, features)
    feature_grad = contract_rows(low_in, delta_low)
    return (grad_in, jnp.stack(grads_mid), grad_out, feature_grad)

def pixel_cotangent(value_error, row_error, row_prior, col_error, col_prior):
    return 2.0 * LOSS_VALUE * value_error + 2.0 * (row_prior - row_error) + 2.0 * (col_prior - col_error)

def clip_factor(total, entries):
    return jnp.minimum(1.0, CLIP_RMS / jnp.sqrt(total / entries + MEAN_EPSILON))

def adam_step(gradient, moment_one, moment_two, clip_scale):
    clipped = gradient * clip_scale
    new_one = BETA_ONE * moment_one + (1.0 - BETA_ONE) * clipped
    new_two = BETA_TWO * moment_two + (1.0 - BETA_TWO) * clipped * clipped
    return new_one / (1.0 - BETA_ONE ** ADAM_STEP) / (jnp.sqrt(new_two / (1.0 - BETA_TWO ** ADAM_STEP)) + ADAM_EPSILON)

def reference(offsets, targets, grid_fine, grid_coarse, weight_in, weight_mid, weight_out, fine_first, fine_second, coarse_first, coarse_second, in_first, in_second, mid_first, mid_second, out_first, out_second):
    tile_count = N_ROW * N_COL
    coarse_tile_rows = SR // RATIO
    coarse_tile_cols = SC // RATIO
    fine_padded = jnp.pad(grid_fine, ((0, 0), (0, 1), (0, 1)))
    coarse_padded = jnp.pad(grid_coarse, ((0, 0), (0, 1), (0, 1)))
    low_in = weight_in.astype(jnp.bfloat16)
    low_mid = weight_mid.astype(jnp.bfloat16)
    low_out = weight_out.astype(jnp.bfloat16)
    zero_index = jnp.zeros((), jnp.int32)

    def tile_starts(tile_index):
        row_tile = (tile_index // N_COL).astype(jnp.int32)
        col_tile = (tile_index % N_COL).astype(jnp.int32)
        return (row_tile, col_tile)

    def tile_forward(tile_index):
        row_tile, col_tile = tile_starts(tile_index)
        fine_ext = lax.dynamic_slice(fine_padded, (zero_index, row_tile * SR, col_tile * SC), (CH, SR + 1, SC + 1))
        coarse_ext = lax.dynamic_slice(coarse_padded, (zero_index, row_tile * coarse_tile_rows, col_tile * coarse_tile_cols), (CH, coarse_tile_rows + 1, coarse_tile_cols + 1))
        tables = level_tables(SR, SC, offsets[row_tile, col_tile, 0], offsets[row_tile, col_tile, 1])
        features = sample_features(fine_ext, coarse_ext, tables)
        predicted, pre_acts, activations = decoder_forward(features, low_in, low_mid, low_out)
        return (predicted, features, pre_acts, activations, tables)
    tile_range = jnp.arange(tile_count, dtype=jnp.int32)
    tile_preds = lax.map(lambda tile_index: tile_forward(tile_index)[0], tile_range)
    predicted = tile_preds.reshape(N_ROW, N_COL, OUT, SR, SC).transpose(2, 0, 3, 1, 4).reshape(OUT, ROWS, COLS)
    value_error = predicted - targets[0]
    row_error = jnp.pad(predicted[:, 1:, :] - predicted[:, :-1, :] - targets[1][:, :-1, :], ((0, 0), (0, 1), (0, 0)))
    col_error = jnp.pad(predicted[:, :, 1:] - predicted[:, :, :-1] - targets[2][:, :, :-1], ((0, 0), (0, 0), (0, 1)))
    row_prior = jnp.pad(row_error[:, :-1, :], ((0, 0), (1, 0), (0, 0)))
    col_prior = jnp.pad(col_error[:, :, :-1], ((0, 0), (0, 0), (1, 0)))
    cotangent = pixel_cotangent(value_error, row_error, row_prior, col_error, col_prior)
    tile_cots = cotangent.reshape(OUT, N_ROW, SR, N_COL, SC).transpose(1, 3, 0, 2, 4).reshape(tile_count, OUT, SR * SC)

    def tile_backward(running, inputs):
        tile_index, tile_cot = inputs
        unused_pred, features, pre_acts, activations, tables = tile_forward(tile_index)
        grad_in, grad_mid, grad_out, feature_grad = decoder_backward(features, pre_acts, activations, tile_cot, low_in, low_mid, low_out)
        fine_back, coarse_back = spread_features(feature_grad, tables)
        sum_in, sum_mid, sum_out, fine_acc, coarse_acc = running
        row_tile, col_tile = tile_starts(tile_index)
        fine_start = (zero_index, row_tile * SR, col_tile * SC)
        coarse_start = (zero_index, row_tile * coarse_tile_rows, col_tile * coarse_tile_cols)
        fine_acc = lax.dynamic_update_slice(fine_acc, lax.dynamic_slice(fine_acc, fine_start, fine_back.shape) + fine_back, fine_start)
        coarse_acc = lax.dynamic_update_slice(coarse_acc, lax.dynamic_slice(coarse_acc, coarse_start, coarse_back.shape) + coarse_back, coarse_start)
        return ((sum_in + grad_in, sum_mid + grad_mid, sum_out + grad_out, fine_acc, coarse_acc), None)
    initial = (jnp.zeros(weight_in.shape, jnp.float32), jnp.zeros(weight_mid.shape, jnp.float32), jnp.zeros(weight_out.shape, jnp.float32), jnp.zeros((CH, ROWS + 1, COLS + 1), jnp.float32), jnp.zeros((CH, CROWS + 1, CCOLS + 1), jnp.float32))
    finals, unused_stack = lax.scan(tile_backward, initial, (tile_range, tile_cots))
    grad_in, grad_mid, grad_out, fine_acc, coarse_acc = finals
    fine_grad = fine_acc[:, :ROWS, :COLS]
    coarse_grad = coarse_acc[:, :CROWS, :CCOLS]
    grid_total = jnp.sum(fine_grad * fine_grad) + jnp.sum(coarse_grad * coarse_grad)
    grid_scale = clip_factor(grid_total, CH * (ROWS * COLS + CROWS * CCOLS))
    decoder_total = jnp.sum(grad_in * grad_in) + jnp.sum(grad_mid * grad_mid) + jnp.sum(grad_out * grad_out)
    decoder_scale = clip_factor(decoder_total, weight_in.size + weight_mid.size + weight_out.size)
    fine_step = adam_step(fine_grad, fine_first, fine_second, grid_scale)
    coarse_step = adam_step(coarse_grad, coarse_first, coarse_second, grid_scale)
    input_step = adam_step(grad_in, in_first, in_second, decoder_scale)
    middle_step = adam_step(grad_mid, mid_first, mid_second, decoder_scale)
    output_step = adam_step(grad_out, out_first, out_second, decoder_scale)
    return (fine_step, coarse_step, input_step, middle_step, output_step)
```

```python
import jax
import jax.numpy as jnp
from jax import lax
from jax.experimental import pallas as pl
from jax.experimental.pallas import tpu as pltpu
from jax.sharding import Mesh
from jax.sharding import PartitionSpec as P

ROW = ("zl", "x")
COL = ("y", "zh", "c")

SUB = 4
RATIO = 4
ADAM_STEP = 10


BETA_ONE = 0.9
BETA_TWO = 0.99
ADAM_EPSILON = 1e-08
CLIP_RMS = 0.01
LOSS_VALUE = 0.25
MEAN_EPSILON = 1e-06


def axes_size(axes):
    total = 1
    for axis in axes:
        total *= lax.axis_size(axis)
    return total


def shifted(block, axis, distance):
    devices = range(axes_size(axis))
    route = [(i - distance, i) for i in devices if i - distance in devices]
    return lax.ppermute(block, axis, route)


def interp_table(samples, level_ratio, offset):
    positions = jnp.arange(samples, dtype=jnp.int32)
    base_index = positions // level_ratio
    fraction = (
        (positions % level_ratio).astype(jnp.float32) + offset.astype(jnp.float32) / SUB
    ) / level_ratio
    column = jnp.arange(samples // level_ratio + 1, dtype=jnp.int32)
    lower_hit = (column[None, :] == base_index[:, None]).astype(jnp.float32)
    upper_hit = (column[None, :] == base_index[:, None] + 1).astype(jnp.float32)
    return lower_hit * (1.0 - fraction)[:, None] + upper_hit * fraction[:, None]


def level_tables(row_count, col_count, shift_y, shift_x):
    return (
        interp_table(row_count, 1, shift_y),
        interp_table(col_count, 1, shift_x),
        interp_table(row_count, RATIO, shift_y),
        interp_table(col_count, RATIO, shift_x),
    )


def sample_level(extended, row_table, col_table):
    across = jnp.einsum("kjl,ml->kjm", extended, col_table, precision=lax.Precision.HIGHEST)
    return jnp.einsum("ij,kjm->kim", row_table, across, precision=lax.Precision.HIGHEST)


def spread_level(cotangent, row_table, col_table):
    backward = jnp.einsum("ij,kim->kjm", row_table, cotangent, precision=lax.Precision.HIGHEST)
    return jnp.einsum("kjm,ml->kjl", backward, col_table, precision=lax.Precision.HIGHEST)


def sample_features(fine_ext, coarse_ext, tables):
    fine_feat = sample_level(fine_ext, tables[0], tables[1])
    coarse_feat = sample_level(coarse_ext, tables[2], tables[3])
    channels, row_count, col_count = fine_feat.shape
    return jnp.concatenate(
        [
            fine_feat.reshape(channels, row_count * col_count),
            coarse_feat.reshape(channels, row_count * col_count),
        ],
        axis=0,
    ).astype(jnp.bfloat16)


def spread_features(feature_grad, tables):
    channels = feature_grad.shape[0] // 2
    row_count = tables[0].shape[0]
    col_count = tables[1].shape[0]
    fine_cot = feature_grad[:channels].reshape(channels, row_count, col_count)
    coarse_cot = feature_grad[channels:].reshape(channels, row_count, col_count)
    return (
        spread_level(fine_cot, tables[0], tables[1]),
        spread_level(coarse_cot, tables[2], tables[3]),
    )


def matmul(former, latter):
    return jnp.dot(former, latter, preferred_element_type=jnp.float32)


def contract_rows(former, latter):
    return lax.dot_general(
        former, latter, (((0,), (0,)), ((), ())), preferred_element_type=jnp.float32
    )


def contract_cols(former, latter):
    return lax.dot_general(
        former, latter, (((1,), (1,)), ((), ())), preferred_element_type=jnp.float32
    )


def silu_slope(pre_act):
    sigmoid = jax.nn.sigmoid(pre_act)
    return sigmoid * (1.0 + pre_act * (1.0 - sigmoid))


def decoder_forward(features, low_in, low_mid, low_out):
    pre_acts = [matmul(low_in, features)]
    activations = [jax.nn.silu(pre_acts[0]).astype(jnp.bfloat16)]
    pre_acts.append(matmul(low_mid[0], activations[-1]))
    activations.append(jax.nn.silu(pre_acts[-1]).astype(jnp.bfloat16))
    return (matmul(low_out, activations[-1]), pre_acts, activations)


def decoder_backward(features, pre_acts, activations, cotangent, low_in, low_mid, low_out):
    out_cotangent = cotangent.astype(jnp.bfloat16)
    grad_out = contract_cols(out_cotangent, activations[-1])
    upward = contract_rows(low_out, out_cotangent)
    grads_mid = []
    delta_low = (upward * silu_slope(pre_acts[1])).astype(jnp.bfloat16)
    grads_mid.insert(0, contract_cols(delta_low, activations[0]))
    upward = contract_rows(low_mid[0], delta_low)
    delta_low = (upward * silu_slope(pre_acts[0])).astype(jnp.bfloat16)
    grad_in = contract_cols(features, delta_low)
    feature_grad = contract_rows(low_in, delta_low)
    return (grad_in, grads_mid[0], grad_out, feature_grad)


def pixel_cotangent(value_error, row_error, row_prior, col_error, col_prior):
    return (
        2.0 * LOSS_VALUE * value_error
        + 2.0 * (row_prior - row_error)
        + 2.0 * (col_prior - col_error)
    )


def clip_factor(total, entries):
    return jnp.minimum(1.0, CLIP_RMS / jnp.sqrt(total / entries + MEAN_EPSILON))


def adam_step(gradient, moment_one, moment_two, clip_scale):
    clipped = gradient * clip_scale
    new_one = BETA_ONE * moment_one + (1.0 - BETA_ONE) * clipped
    new_two = BETA_TWO * moment_two + (1.0 - BETA_TWO) * clipped * clipped
    return (
        new_one
        / (1.0 - BETA_ONE**ADAM_STEP)
        / (jnp.sqrt(new_two / (1.0 - BETA_TWO**ADAM_STEP)) + ADAM_EPSILON)
    )


def swapped(block, axis, mask):
    size = lax.axis_size(axis)
    return lax.ppermute(block, axis, [(i, i ^ mask) for i in range(size)])


def pair_sum(values):
    values = list(values)
    while len(values) > 1:
        values = [values[i] + values[i + 1] for i in range(0, len(values), 2)]
    return values[0]


def exchange_sum(block, axis):
    return pair_sum([block] + [swapped(block, axis, d) for d in range(1, lax.axis_size(axis))])


def exchange_gather(block, axis):
    return [block] + [swapped(block, axis, d) for d in range(1, lax.axis_size(axis))]


def scatter_sum(blocks, axis):
    return pair_sum([blocks[0]] + [swapped(blocks[d], axis, d) for d in range(1, len(blocks))])


def vmem():
    return pl.BlockSpec(memory_space=pltpu.VMEM)


def smem():
    return pl.BlockSpec(memory_space=pltpu.SMEM)


def split_kernel(place_ref, mid_ref, in_ref, out_ref, keep_ref, send_ref):
    core = place_ref[0]
    tile = place_ref[1]
    for d in range(16):
        chunk = tile ^ d
        band = chunk >> 1
        side = chunk & 1
        for half, target in ((core, keep_ref), (1 - core, send_ref)):
            cols = pl.ds(pl.multiple_of((half * 2 + side) * 128, 128), 128)
            target[d, 0:64, :] = mid_ref[pl.ds(pl.multiple_of(band * 64, 64), 64), cols]
            target[d, 64:72, :] = in_ref[pl.ds(pl.multiple_of(band * 8, 8), 8), cols]
            target[d, 72:80, :] = jnp.where(band == 0, out_ref[:, cols], 0.0)


def split_grads(place, grad_mid, grad_in, grad_out):
    part = jax.ShapeDtypeStruct((16, 80, 128), jnp.float32)
    return pl.pallas_call(
        split_kernel,
        out_shape=(part, part),
        in_specs=[smem(), vmem(), vmem(), vmem()],
        out_specs=(vmem(), vmem()),
        name="split_grads",
    )(place, grad_mid, grad_in, grad_out)


def decoder_kernel(
    place_ref,
    own_ref,
    other_ref,
    mid_one_ref,
    mid_two_ref,
    in_one_ref,
    in_two_ref,
    out_one_ref,
    out_two_ref,
    mid_ref,
    in_ref,
    out_ref,
    scale_ref,
    in_grad,
    out_grad,
    *,
    decoder_entries,
    grid_entries,
):
    core = place_ref[0]
    tile = place_ref[1]
    own_sum = pair_sum([own_ref[d, 80:88, :] for d in range(16)])
    other_sum = pair_sum([other_ref[d, 80:88, :] for d in range(16)])
    totals = own_sum + other_sum
    grid_scale = clip_factor(totals[0:1, :], grid_entries)
    scale = clip_factor(totals[1:2, :], decoder_entries)
    scale_ref[...] = grid_scale
    for band in range(8):
        for block in range(4):
            half = block // 2
            chunk = band * 2 + block % 2
            d = tile ^ chunk
            data = jnp.where(half == core, own_ref[d, 0:80, :], other_ref[d, 0:80, :])
            cols = slice(block * 128, block * 128 + 128)
            rows = slice(band * 64, band * 64 + 64)
            mid_ref[rows, cols] = adam_step(
                data[0:64], mid_one_ref[rows, cols], mid_two_ref[rows, cols], scale
            )
            in_grad[band * 8 : band * 8 + 8, cols] = data[64:72]
            if band == 0:
                out_grad[:, cols] = data[72:80]
    for block in range(4):
        cols = slice(block * 128, block * 128 + 128)
        turned = in_grad[:, cols].T
        in_ref[cols, :] = adam_step(turned, in_one_ref[cols, :], in_two_ref[cols, :], scale[:, 0:64])
        out_ref[:, cols] = adam_step(
            out_grad[0:3, cols], out_one_ref[:, cols], out_two_ref[:, cols], scale
        )


def decoder_steps(place, own, other, moments, decoder_entries, grid_entries):
    shapes = (moments[0].shape, moments[2].shape, moments[4].shape, (1, 128))
    return pl.pallas_call(
        lambda *refs: decoder_kernel(
            *refs, decoder_entries=decoder_entries, grid_entries=grid_entries
        ),
        out_shape=tuple(jax.ShapeDtypeStruct(s, jnp.float32) for s in shapes),
        in_specs=[smem()] + [vmem()] * 8,
        out_specs=(vmem(),) * 4,
        scratch_shapes=[pltpu.VMEM((64, 512), jnp.float32), pltpu.VMEM((8, 512), jnp.float32)],
        name="decoder_steps",
    )(place, own, other, *moments)


def reduce_grads(place, grad_mid, grad_in, grad_out, grid_local):
    keep, send = split_grads(place, grad_mid, grad_in, grad_out)
    part = keep + swapped(send, "c", 1)
    part = scatter_sum([part[d * 4 : d * 4 + 4] for d in range(4)], "x")
    part = scatter_sum([part[d] for d in range(4)], "y")
    tail = jnp.broadcast_to(grid_local, (8, 128))
    part = exchange_sum(jnp.concatenate([part, tail]), "zl")
    part = exchange_sum(part, "zh")
    squares = jnp.sum(part[:80] * part[:80])
    tail = jnp.where(jnp.arange(8)[:, None] == 1, squares, part[80:])
    part = jnp.concatenate([part[:80], tail])
    own = jnp.stack(exchange_gather(part, "y"))
    own = jnp.concatenate(exchange_gather(own, "x"))
    return own, swapped(own, "c", 1)


def shards(
    offsets,
    targets,
    grid_fine,
    grid_coarse,
    weight_in,
    weight_mid,
    weight_out,
    fine_first,
    fine_second,
    coarse_first,
    coarse_second,
    in_first,
    in_second,
    mid_first,
    mid_second,
    out_first,
    out_second,
):
    channels, sample_rows, sample_cols = grid_fine.shape
    coarse_rows = grid_coarse.shape[1]
    coarse_cols = grid_coarse.shape[2]
    low_in = weight_in.astype(jnp.bfloat16)
    low_mid = weight_mid.astype(jnp.bfloat16)
    low_out = weight_out.astype(jnp.bfloat16)
    top_rows = jnp.concatenate([grid_fine[:, :1, :], grid_coarse[:, :1, :]], axis=2)
    top_rows = shifted(top_rows, ROW, -1)
    fine_tall = jnp.concatenate([grid_fine, top_rows[:, :, :sample_cols]], axis=1)
    coarse_tall = jnp.concatenate([grid_coarse, top_rows[:, :, sample_cols:]], axis=1)
    edge_cols = jnp.concatenate([fine_tall[:, :, :1], coarse_tall[:, :, :1]], axis=1)
    edge_cols = shifted(edge_cols, COL, -1)
    fine_ext = jnp.concatenate([fine_tall, edge_cols[:, : sample_rows + 1, :]], axis=2)
    coarse_ext = jnp.concatenate([coarse_tall, edge_cols[:, sample_rows + 1 :, :]], axis=2)
    tables = level_tables(sample_rows, sample_cols, offsets[0, 0, 0], offsets[0, 0, 1])
    features = sample_features(fine_ext, coarse_ext, tables)
    predicted, pre_acts, activations = decoder_forward(features, low_in, low_mid, low_out)
    outputs = predicted.shape[0]
    predicted = predicted.reshape(outputs, sample_rows, sample_cols)
    below = shifted(predicted[:, :1, :], ROW, -1)
    beside = shifted(predicted[:, :, :1], COL, -1)
    row_global = lax.axis_index(ROW) * sample_rows + jnp.arange(sample_rows, dtype=jnp.int32)
    col_global = lax.axis_index(COL) * sample_cols + jnp.arange(sample_cols, dtype=jnp.int32)
    row_valid = (row_global < axes_size(ROW) * sample_rows - 1)[None, :, None]
    col_valid = (col_global < axes_size(COL) * sample_cols - 1)[None, None, :]
    row_next = jnp.concatenate([predicted[:, 1:, :], below], axis=1)
    col_next = jnp.concatenate([predicted[:, :, 1:], beside], axis=2)
    value_error = predicted - targets[0]
    row_error = jnp.where(row_valid, row_next - predicted - targets[1], 0.0)
    col_error = jnp.where(col_valid, col_next - predicted - targets[2], 0.0)
    above = shifted(row_error[:, -1:, :], ROW, 1)
    before = shifted(col_error[:, :, -1:], COL, 1)
    row_prior = jnp.concatenate([above, row_error[:, :-1, :]], axis=1)
    col_prior = jnp.concatenate([before, col_error[:, :, :-1]], axis=2)
    cotangent = pixel_cotangent(value_error, row_error, row_prior, col_error, col_prior)
    grad_in, grad_mid, grad_out, feature_grad = decoder_backward(
        features,
        pre_acts,
        activations,
        cotangent.reshape(outputs, sample_rows * sample_cols),
        low_in,
        low_mid,
        low_out,
    )
    fine_back, coarse_back = spread_features(feature_grad, tables)
    side_cols = jnp.concatenate(
        [fine_back[:, :, sample_cols:], coarse_back[:, :, coarse_cols:]], axis=1
    )
    side_cols = shifted(side_cols, COL, 1)
    fine_tall_grad = jnp.concatenate(
        [fine_back[:, :, :1] + side_cols[:, : sample_rows + 1, :], fine_back[:, :, 1:sample_cols]],
        axis=2,
    )
    coarse_tall_grad = jnp.concatenate(
        [
            coarse_back[:, :, :1] + side_cols[:, sample_rows + 1 :, :],
            coarse_back[:, :, 1:coarse_cols],
        ],
        axis=2,
    )
    bottom_rows = jnp.concatenate(
        [fine_tall_grad[:, sample_rows:, :], coarse_tall_grad[:, coarse_rows:, :]], axis=2
    )
    bottom_rows = shifted(bottom_rows, ROW, 1)
    fine_grad = jnp.concatenate(
        [
            fine_tall_grad[:, :1, :] + bottom_rows[:, :, :sample_cols],
            fine_tall_grad[:, 1:sample_rows, :],
        ],
        axis=1,
    )
    coarse_grad = jnp.concatenate(
        [
            coarse_tall_grad[:, :1, :] + bottom_rows[:, :, sample_cols:],
            coarse_tall_grad[:, 1:coarse_rows, :],
        ],
        axis=1,
    )
    grid_local = jnp.sum(fine_grad * fine_grad) + jnp.sum(coarse_grad * coarse_grad)
    devices = axes_size(ROW) * axes_size(COL)
    grid_entries = (fine_grad.size + coarse_grad.size) * devices
    decoder_entries = weight_in.size + weight_mid.size + weight_out.size
    place = jnp.stack([lax.axis_index("c"), lax.axis_index("x") * 4 + lax.axis_index("y")])
    own, other = reduce_grads(
        place,
        grad_mid,
        grad_in,
        jnp.concatenate([grad_out, jnp.zeros((5, grad_out.shape[1]), jnp.float32)]),
        grid_local,
    )
    middle_step, input_step, output_step, scale = decoder_steps(
        place,
        own,
        other,
        (mid_first[0], mid_second[0], in_first, in_second, out_first, out_second),
        decoder_entries,
        grid_entries,
    )
    grid_scale = scale[0, 0]
    fine_step = adam_step(fine_grad, fine_first, fine_second, grid_scale)
    coarse_step = adam_step(coarse_grad, coarse_first, coarse_second, grid_scale)
    return (fine_step, coarse_step, input_step, middle_step[None], output_step)


def solution(mesh):
    sizes = {"zl": 4, "x": 4, "y": 4, "zh": 2, "c": 2}
    mesh = Mesh(mesh.devices.reshape(tuple(sizes.values())), tuple(sizes))
    placed = (
        P(ROW, COL, None),
        P(None, None, ROW, COL),
        P(None, ROW, COL),
        P(None, ROW, COL),
        P(),
        P(),
        P(),
        P(None, ROW, COL),
        P(None, ROW, COL),
        P(None, ROW, COL),
        P(None, ROW, COL),
        P(),
        P(),
        P(),
        P(),
        P(),
        P(),
    )
    return jax.shard_map(
        shards,
        mesh=mesh,
        in_specs=placed,
        out_specs=(P(None, ROW, COL), P(None, ROW, COL), P(), P(), P()),
        check_vma=False,
    )
```

```python
import jax
import jax.numpy as jnp
from jax import lax
from jax.experimental import pallas as pl
from jax.experimental.pallas import tpu as pltpu
from jax.sharding import Mesh
from jax.sharding import PartitionSpec as P

SUB = 4
RATIO = 4
ADAM_STEP = 10

BETA_ONE = 0.9
BETA_TWO = 0.99
ADAM_EPSILON = 1e-08
CLIP_RMS = 0.01
LOSS_VALUE = 0.25
MEAN_EPSILON = 1e-06

ROW = ("zl", "x")
COL = ("y", "zh", "c")
SR = 32
SC = 128
CH = 32
CR = 8
CC = 32
HID = 512
STEPS = 4
CHAINS = 2
BLOCK = SR * SC // STEPS
WIDTH = BLOCK // CHAINS
LINES = SR // STEPS
BANDS = CR // STEPS
F32 = jnp.float32
BF16 = jnp.bfloat16
MIB = 1 << 20


def axes_size(axes):
    total = 1
    for axis in axes:
        total *= lax.axis_size(axis)
    return total


def axes_index(axes):
    index = 0
    for axis in axes:
        index = index * lax.axis_size(axis) + lax.axis_index(axis)
    return index


def shifted(block, down, right):
    rows, cols = axes_size(ROW), axes_size(COL)
    if not right:
        return lax.ppermute(block, ROW, [(i, (i + down) % rows) for i in range(rows)])
    if not down:
        return lax.ppermute(block, COL, [(i, (i + right) % cols) for i in range(cols)])
    route = [
        (r * cols + c, (r + down) % rows * cols + (c + right) % cols)
        for r in range(rows)
        for c in range(cols)
    ]
    return lax.ppermute(block, ROW + COL, route)


def at_ends():
    row, col = axes_index(ROW), axes_index(COL)
    return row == 0, row == axes_size(ROW) - 1, col == 0, col == axes_size(COL) - 1


def swapped(block, axis, mask):
    size = lax.axis_size(axis)
    return lax.ppermute(block, axis, [(i, i ^ mask) for i in range(size)])


def pair_sum(values):
    values = list(values)
    while len(values) > 1:
        values = [values[i] + values[i + 1] for i in range(0, len(values), 2)]
    return values[0]


def exchange_sum(block, axis):
    return pair_sum([block] + [swapped(block, axis, d) for d in range(1, lax.axis_size(axis))])


def exchange_gather(block, axis):
    return [block] + [swapped(block, axis, d) for d in range(1, lax.axis_size(axis))]


def scatter_sum(blocks, axis):
    return pair_sum([blocks[0]] + [swapped(blocks[d], axis, d) for d in range(1, len(blocks))])


def vmem():
    return pl.BlockSpec(memory_space=pltpu.VMEM)


def smem():
    return pl.BlockSpec(memory_space=pltpu.SMEM)


def hbm():
    return pl.BlockSpec(memory_space=pltpu.HBM)


def in_hbm(array):
    return pltpu.with_memory_space_constraint(array, pltpu.HBM)


def whole(shape, memory_space=pltpu.VMEM):
    return pl.BlockSpec(shape, lambda b: (0,) * len(shape), memory_space=memory_space)


def lane_ids(rows):
    return lax.broadcasted_iota(jnp.int32, (rows, SC), 1)


def spread_lane(block, lane):
    return jnp.broadcast_to(block[:, lane : lane + 1], (block.shape[0], SC))


def dot(former, latter, former_dim=1, latter_dim=0, precision=None):
    return lax.dot_general(
        former,
        latter,
        (((former_dim,), (latter_dim,)), ((), ())),
        precision=precision,
        preferred_element_type=F32,
    )


def sigmoid(value):
    return 0.5 * jnp.tanh(0.5 * value) + 0.5


def coarse_table(shift_x):
    line = lax.broadcasted_iota(jnp.int32, (SC, SC), 0)
    sample = lax.broadcasted_iota(jnp.int32, (SC, SC), 1)
    base = sample >> 2
    fraction = ((sample & 3).astype(F32) + shift_x) * (1.0 / RATIO)
    return jnp.where(line == base, 1.0 - fraction, 0.0) + jnp.where(line == base + 1, fraction, 0.0)


def edges_kernel(fine_hbm, coarse_hbm, row_ref, col_ref, fine_ref, coarse_ref, fine, coarse, sems):
    copies = [
        pltpu.make_async_copy(fine_hbm, fine, sems.at[0]),
        pltpu.make_async_copy(coarse_hbm, coarse, sems.at[1]),
    ]
    for copy in copies:
        copy.start()
    for copy in copies:
        copy.wait()
    lane = lane_ids(CH)
    row_ref[:, 0:SC] = fine[:, 0, :]
    row_ref[:, SC:] = jnp.zeros((CH, SC), F32)
    row_ref[:, SC : SC + CC] = coarse[:, 0, :]
    coarse_ref[...] = jnp.zeros(coarse_ref.shape, F32)
    cols = jnp.zeros((CH, SC), F32)
    for i in range(SR):
        line = fine[:, i, :]
        fine_ref[i] = line
        cols = jnp.where(lane == i, spread_lane(line, 0), cols)
    for i in range(CR):
        line = coarse[:, i, :]
        coarse_ref[i, :, 0:CC] = line
        cols = jnp.where(lane == SR + i, spread_lane(line, 0), cols)
    col_ref[...] = cols


def edges(fine, coarse):
    shapes = ((CH, 2 * SC), (CH, SC), (SR, CH, SC), (CR, CH, SC))
    return pl.pallas_call(
        edges_kernel,
        out_shape=tuple(jax.ShapeDtypeStruct(d, F32) for d in shapes),
        in_specs=[hbm(), hbm()],
        out_specs=(vmem(),) * 4,
        scratch_shapes=[
            pltpu.VMEM(fine.shape, F32),
            pltpu.VMEM(coarse.shape, F32),
            pltpu.SemaphoreType.DMA((2,)),
        ],
        compiler_params=pltpu.CompilerParams(vmem_limit_bytes=8 * MIB),
        name="edges",
    )(in_hbm(fine), in_hbm(coarse))


def prepare_kernel(
    offset_ref,
    in_hbm,
    mid_hbm,
    out_hbm,
    target_hbm,
    shift_ref,
    in_ref,
    in_turned_ref,
    mid_ref,
    mid_turned_ref,
    out_ref,
    out_turned_ref,
    target_ref,
    ends_ref,
    w_in,
    w_mid,
    w_out,
    targets,
    sems,
):
    copies = [
        pltpu.make_async_copy(source, target, sems.at[i])
        for i, (source, target) in enumerate(
            ((in_hbm, w_in), (out_hbm, w_out), (target_hbm, targets), (mid_hbm, w_mid))
        )
    ]
    for copy in copies:
        copy.start()
    shift_ref[...] = jnp.zeros((8, SC), F32)
    for i in range(2):
        shift = offset_ref[0, 0, i].astype(F32) * (1.0 / SUB)
        shift_ref[i : i + 1, :] = jnp.full((1, SC), shift, F32)
    copies[0].wait()
    in_turned_ref[...] = w_in[...].astype(BF16)
    for block in range(4):
        cols = slice(block * 128, block * 128 + 128)
        in_ref[cols, :] = w_in[:, cols].T.astype(BF16)
    copies[1].wait()
    padded = jnp.concatenate([w_out[...], jnp.zeros((13, HID), F32)], axis=0)
    out_ref[...] = padded.astype(BF16)
    for block in range(4):
        cols = slice(block * 128, block * 128 + 128)
        out_turned_ref[cols, :] = padded[:, cols].T.astype(BF16)
    copies[2].wait()
    lane = lane_ids(3)
    ends = jnp.zeros((3, SC), F32)
    target_ref[...] = jnp.zeros(target_ref.shape, F32)
    for i in range(SR):
        for kind in range(3):
            line = targets[kind, :, i, :]
            target_ref[kind, 0:3, i * SC : i * SC + SC] = line
        ends = jnp.where(lane == i, spread_lane(line, SC - 1), ends)
    ends_ref[...] = jnp.zeros((8, SC), F32)
    ends_ref[0:3, :] = ends
    copies[3].wait()
    mid_ref[...] = w_mid[...].astype(BF16)
    for i in range(4):
        for j in range(4):
            rows = slice(i * 128, i * 128 + 128)
            cols = slice(j * 128, j * 128 + 128)
            mid_turned_ref[cols, rows] = w_mid[rows, cols].T.astype(BF16)


def prepare(offsets, w_in, w_mid, w_out, targets):
    outs = (
        jax.ShapeDtypeStruct((8, SC), F32),
        jax.ShapeDtypeStruct((HID, 2 * CH), BF16),
        jax.ShapeDtypeStruct((2 * CH, HID), BF16),
        jax.ShapeDtypeStruct((HID, HID), BF16),
        jax.ShapeDtypeStruct((HID, HID), BF16),
        jax.ShapeDtypeStruct((16, HID), BF16),
        jax.ShapeDtypeStruct((HID, 16), BF16),
        jax.ShapeDtypeStruct((3, 8, SR * SC), F32),
        jax.ShapeDtypeStruct((8, SC), F32),
    )
    return pl.pallas_call(
        prepare_kernel,
        out_shape=outs,
        in_specs=[smem(), hbm(), hbm(), hbm(), hbm()],
        out_specs=(vmem(),) * len(outs),
        scratch_shapes=[pltpu.VMEM(a.shape, F32) for a in (w_in, w_mid, w_out, targets)]
        + [pltpu.SemaphoreType.DMA((4,))],
        compiler_params=pltpu.CompilerParams(vmem_limit_bytes=8 * MIB),
        name="prepare",
    )(offsets, *(in_hbm(a) for a in (w_in, w_mid, w_out, targets)))


def forward_kernel(
    shift_ref,
    fine_ref,
    coarse_ref,
    row_ref,
    col_ref,
    corner_ref,
    target_ref,
    ends_ref,
    in_ref,
    mid_ref,
    out_ref,
    feat_ref,
    pre_ref,
    pred_ref,
    up_ref,
    left_ref,
    down_ref,
    right_ref,
    lines,
    bands,
):
    step = pl.program_id(0)
    shift_y = shift_ref[0:1, :]
    shift_x = shift_ref[1:2, :]

    @pl.when(step == 0)
    def _():
        lane = lane_ids(CH)
        unused_first_row, last_row, unused_first_col, last_col = at_ends()
        row_in = jnp.where(last_row, 0.0, row_ref[...])
        col_in = jnp.where(last_col, 0.0, col_ref[...])
        corner_in = jnp.where(jnp.logical_or(last_row, last_col), 0.0, corner_ref[...])

        def across(line, following):
            moved = jnp.where(lane == SC - 1, following, pltpu.roll(line, SC - 1, 1))
            return line * (1.0 - shift_x) + moved * shift_x

        stage = []
        for i in range(CR):
            stage.append(jnp.where(lane == CC, spread_lane(col_in, SR + i), coarse_ref[i]))
        stage.append(jnp.where(lane == CC, spread_lane(corner_in, SR), row_in[:, SC:]))
        bands[...] = dot(
            jnp.concatenate(stage, axis=0), coarse_table(shift_x), precision=lax.Precision.HIGHEST
        ).reshape(CR + 1, CH, SC)
        for i in range(SR):
            lines[i] = across(fine_ref[i], spread_lane(col_in, i))
        lines[SR] = across(row_in[:, 0:SC], spread_lane(corner_in, 0))
        left_ref[...] = jnp.zeros(left_ref.shape, F32)
        right_ref[...] = ends_ref[...]

    tiles = []
    for k in range(LINES):
        row = step * LINES + k
        band = step * BANDS + k // RATIO
        fine = lines[row] * (1.0 - shift_y) + lines[row + 1] * shift_y
        part = (k % RATIO + shift_y) * (1.0 / RATIO)
        coarse = bands[band] * (1.0 - part) + bands[band + 1] * part
        tiles.append(jnp.concatenate([fine, coarse], axis=0).astype(BF16))
    feat = jnp.concatenate(tiles, axis=1)
    feat_ref[...] = feat
    preds = []
    for chain in range(CHAINS):
        cols = slice(chain * WIDTH, chain * WIDTH + WIDTH)
        pre = dot(in_ref[...], feat[:, cols])
        act = (pre * sigmoid(pre)).astype(BF16)
        pre = dot(mid_ref[...], act)
        pre_ref[:, cols] = pre
        act = (pre * sigmoid(pre)).astype(BF16)
        preds.append(dot(out_ref[...], act)[0:8])
    pred = jnp.concatenate(preds, axis=1)
    pred_ref[...] = pred
    lane = lane_ids(8)
    left = left_ref[...]
    right = right_ref[...]
    for k in range(LINES):
        row = step * LINES + k
        tile = pred[:, k * SC : k * SC + SC]
        left = jnp.where(lane == row, spread_lane(tile, 0), left)
        right = right + jnp.where(lane == row, spread_lane(tile, SC - 1), 0.0)
    left_ref[...] = left
    right_ref[...] = right

    @pl.when(step == 0)
    def _():
        up_ref[...] = pred[:, 0:SC]

    @pl.when(step == STEPS - 1)
    def _():
        down_ref[...] = pred[:, BLOCK - SC :] + target_ref[1, :, SR * SC - SC :]


def forward(*args):
    edge = jax.ShapeDtypeStruct((8, SC), F32)
    return pl.pallas_call(
        forward_kernel,
        grid=(STEPS,),
        out_shape=(
            jax.ShapeDtypeStruct((2 * CH, SR * SC), BF16),
            jax.ShapeDtypeStruct((HID, SR * SC), F32),
            jax.ShapeDtypeStruct((8, SR * SC), F32),
            edge,
            edge,
            edge,
            edge,
        ),
        in_specs=[whole(a.shape) for a in args],
        out_specs=(
            pl.BlockSpec((2 * CH, BLOCK), lambda b: (0, b)),
            pl.BlockSpec((HID, BLOCK), lambda b: (0, b)),
            pl.BlockSpec((8, BLOCK), lambda b: (0, b)),
            whole((8, SC)),
            whole((8, SC)),
            whole((8, SC)),
            whole((8, SC)),
        ),
        scratch_shapes=[
            pltpu.VMEM((SR + 1, CH, SC), F32),
            pltpu.VMEM((CR + 1, CH, SC), F32),
        ],
        compiler_params=pltpu.CompilerParams(vmem_limit_bytes=24 * MIB),
        name="forward",
    )(*args)


def loss_cotangent(pred_ref, target_ref, below, beside, above, before, cot):
    first_row, last_row, first_col, last_col = at_ends()
    lane = lane_ids(3)
    cot[...] = jnp.zeros(cot.shape, F32)
    line = pred_ref[0:3, 0:SC]
    row_prior = jnp.where(first_row, 0.0, line - above[0:3, :])
    for i in range(SR):
        if i + 1 < SR:
            following = pred_ref[0:3, (i + 1) * SC : (i + 2) * SC]
        else:
            following = below[0:3, :]
        value_error = line - target_ref[0, 0:3, i * SC : i * SC + SC]
        row_error = following - line - target_ref[1, 0:3, i * SC : i * SC + SC]
        if i + 1 == SR:
            row_error = jnp.where(last_row, 0.0, row_error)
        beyond = jnp.where(lane == SC - 1, spread_lane(beside[0:3, :], i), pltpu.roll(line, SC - 1, 1))
        col_error = beyond - line - target_ref[2, 0:3, i * SC : i * SC + SC]
        col_error = jnp.where(jnp.logical_and(lane == SC - 1, last_col), 0.0, col_error)
        edge = jnp.where(first_col, 0.0, line - spread_lane(before[0:3, :], i))
        col_prior = jnp.where(lane == 0, edge, pltpu.roll(col_error, 1, 1))
        cot[0:3, i * SC : (i + 1) * SC] = (
            2.0 * LOSS_VALUE * value_error
            + 2.0 * (row_prior - row_error)
            + 2.0 * (col_prior - col_error)
        )
        line = following
        row_prior = row_error


def backward_kernel(
    shift_ref,
    feat_ref,
    pre_ref,
    pred_ref,
    below_ref,
    beside_ref,
    above_ref,
    before_ref,
    target_ref,
    in_ref,
    in_turned_ref,
    mid_turned_ref,
    out_turned_ref,
    keep_ref,
    send_ref,
    fine_ref,
    coarse_ref,
    row_ref,
    col_ref,
    corner_ref,
    cot,
    grad_mid,
    grad_in,
    grad_out,
    last_line,
    bands,
):
    step = pl.program_id(0)
    shift_y = shift_ref[0:1, :]
    shift_x = shift_ref[1:2, :]
    lane = lane_ids(CH)

    @pl.when(step == 0)
    def _():
        loss_cotangent(pred_ref, target_ref, below_ref, beside_ref, above_ref, before_ref, cot)
        grad_mid[...] = jnp.zeros(grad_mid.shape, F32)
        grad_in[...] = jnp.zeros(grad_in.shape, F32)
        grad_out[...] = jnp.zeros(grad_out.shape, F32)
        last_line[...] = jnp.zeros(last_line.shape, F32)
        bands[0] = jnp.zeros((CH, SC), F32)
        col_ref[...] = jnp.zeros((CH, SC), F32)

    feat_grads = []
    for chain in range(CHAINS):
        cols = slice(chain * WIDTH, chain * WIDTH + WIDTH)
        feat = feat_ref[:, cols]
        samples = pl.ds(pl.multiple_of(step * BLOCK + chain * WIDTH, WIDTH), WIDTH)
        out_cot = cot[:, samples].astype(BF16)
        pre = pre_ref[:, cols]
        gate = sigmoid(pre)
        act = (pre * gate).astype(BF16)
        grad_out[...] += dot(out_cot, act, 1, 1)
        upward = dot(out_turned_ref[...], out_cot)
        delta = (upward * (gate * (1.0 + pre * (1.0 - gate)))).astype(BF16)
        pre = dot(in_ref[...], feat)
        gate = sigmoid(pre)
        act = (pre * gate).astype(BF16)
        grad_mid[...] += dot(delta, act, 1, 1)
        upward = dot(mid_turned_ref[...], delta)
        delta = (upward * (gate * (1.0 + pre * (1.0 - gate)))).astype(BF16)
        grad_in[...] += dot(feat, delta, 1, 1)
        feat_grads.append(dot(in_turned_ref[...], delta))
    feat_grad = jnp.concatenate(feat_grads, axis=1)

    def along(line):
        moved = jnp.where(lane == 0, 0.0, pltpu.roll(line, 1, 1))
        return line * (1.0 - shift_x) + moved * shift_x

    prior = last_line[...]
    cols = col_ref[...]
    upper = bands[step * BANDS]
    lower = jnp.zeros((CH, SC), F32)
    for k in range(LINES):
        row = step * LINES + k
        fine = feat_grad[0:CH, k * SC : k * SC + SC]
        line = fine * (1.0 - shift_y) + prior * shift_y
        fine_ref[row] = along(line)
        cols = jnp.where(lane == row, spread_lane(line * shift_x, SC - 1), cols)
        prior = fine
        coarse = feat_grad[CH:, k * SC : k * SC + SC]
        part = (k % RATIO + shift_y) * (1.0 / RATIO)
        upper += coarse * (1.0 - part)
        lower += coarse * part
        if k % RATIO == RATIO - 1:
            bands[step * BANDS + k // RATIO] = upper
            upper = lower
            lower = jnp.zeros((CH, SC), F32)
    bands[step * BANDS + BANDS] = upper
    last_line[...] = prior
    col_ref[...] = cols

    @pl.when(step == STEPS - 1)
    def _():
        line = prior * shift_y
        row_ref[:, 0:SC] = along(line)
        corner = jnp.where(lane == 0, spread_lane(line * shift_x, SC - 1), 0.0)
        spread = dot(
            bands[...].reshape((CR + 1) * CH, SC),
            coarse_table(shift_x),
            1,
            1,
            precision=lax.Precision.HIGHEST,
        )
        ends = cols
        for i in range(CR):
            band = spread[i * CH : i * CH + CH]
            coarse_ref[i] = jnp.where(lane < CC, band, 0.0)
            ends = jnp.where(lane == SR + i, spread_lane(band, CC), ends)
        col_ref[...] = ends
        band = spread[CR * CH :]
        row_ref[:, SC:] = jnp.where(lane < CC, band, 0.0)
        corner_ref[...] = jnp.where(lane == SR, spread_lane(band, CC), corner)
        core = lax.axis_index("c")
        tile = axes_index(("x", "y"))
        for d in range(16):
            chunk = tile ^ d
            band = chunk >> 1
            side = chunk & 1
            for half, target in ((core, keep_ref), (1 - core, send_ref)):
                cols_at = pl.ds(pl.multiple_of((half * 2 + side) * 128, 128), 128)
                target[d, 0:64, :] = grad_mid[pl.ds(pl.multiple_of(band * 64, 64), 64), cols_at]
                target[d, 64:72, :] = grad_in[pl.ds(pl.multiple_of(band * 8, 8), 8), cols_at]
                target[d, 72:80, :] = jnp.where(band == 0, grad_out[0:8, cols_at], 0.0)


def backward(shifts, feat, pre, pred, *consts):
    part = jax.ShapeDtypeStruct((16, 80, 128), F32)
    consts = (pred, *consts)
    outs = (
        part,
        part,
        jax.ShapeDtypeStruct((SR, CH, SC), F32),
        jax.ShapeDtypeStruct((CR, CH, SC), F32),
        jax.ShapeDtypeStruct((CH, 2 * SC), F32),
        jax.ShapeDtypeStruct((CH, SC), F32),
        jax.ShapeDtypeStruct((CH, SC), F32),
    )
    return pl.pallas_call(
        backward_kernel,
        grid=(STEPS,),
        out_shape=outs,
        in_specs=[
            whole((8, SC)),
            pl.BlockSpec((2 * CH, BLOCK), lambda b: (0, b)),
            pl.BlockSpec((HID, BLOCK), lambda b: (0, b)),
        ]
        + [whole(a.shape) for a in consts],
        out_specs=tuple(whole(o.shape) for o in outs),
        scratch_shapes=[
            pltpu.VMEM((16, SR * SC), F32),
            pltpu.VMEM((HID, HID), F32),
            pltpu.VMEM((2 * CH, HID), F32),
            pltpu.VMEM((16, HID), F32),
            pltpu.VMEM((CH, SC), F32),
            pltpu.VMEM((CR + 1, CH, SC), F32),
        ],
        compiler_params=pltpu.CompilerParams(vmem_limit_bytes=32 * MIB),
        name="backward",
    )(shifts, feat, pre, *consts)


def join_kernel(fine_ref, coarse_ref, row_ref, col_ref, corner_ref, fine_out, coarse_out, total_ref):
    lane = lane_ids(CH)
    first_row, unused_last_row, first_col, unused_last_col = at_ends()
    rows = jnp.where(first_row, 0.0, row_ref[...])
    cols = jnp.where(first_col, 0.0, col_ref[...])
    corner = jnp.where(jnp.logical_or(first_row, first_col), 0.0, corner_ref[...])
    total = jnp.zeros((CH, SC), F32)
    for i in range(SR):
        line = fine_ref[i] + jnp.where(lane == 0, spread_lane(cols, i), 0.0)
        if i == 0:
            line += rows[:, 0:SC]
            line += jnp.where(lane == 0, spread_lane(corner, 0), 0.0)
        fine_out[:, i, :] = line
        total += line * line
    for i in range(CR):
        line = coarse_ref[i] + jnp.where(lane == 0, spread_lane(cols, SR + i), 0.0)
        if i == 0:
            line += rows[:, SC:]
            line += jnp.where(lane == 0, spread_lane(corner, SR), 0.0)
        coarse_out[:, i, :] = line[:, 0:CC]
        total += line * line
    total = jnp.sum(jnp.sum(total, axis=0, keepdims=True), axis=1, keepdims=True)
    total_ref[...] = jnp.broadcast_to(total, (8, SC))


def join(fine, coarse, row_in, col_in, corner_in):
    return pl.pallas_call(
        join_kernel,
        out_shape=(
            jax.ShapeDtypeStruct((CH, SR, SC), F32),
            jax.ShapeDtypeStruct((CH, CR, CC), F32),
            jax.ShapeDtypeStruct((8, SC), F32),
        ),
        in_specs=[vmem()] * 5,
        out_specs=(vmem(),) * 3,
        compiler_params=pltpu.CompilerParams(vmem_limit_bytes=8 * MIB),
        name="join",
    )(fine, coarse, row_in, col_in, corner_in)


def clip_factor(total, entries):
    return jnp.minimum(1.0, CLIP_RMS / jnp.sqrt(total / entries + MEAN_EPSILON))


def adam_step(gradient, moment_one, moment_two, clip_scale):
    clipped = gradient * clip_scale
    new_one = BETA_ONE * moment_one + (1.0 - BETA_ONE) * clipped
    new_two = BETA_TWO * moment_two + (1.0 - BETA_TWO) * clipped * clipped
    return (
        new_one
        * (1.0 / (1.0 - BETA_ONE**ADAM_STEP))
        / (jnp.sqrt(new_two * (1.0 / (1.0 - BETA_TWO**ADAM_STEP))) + ADAM_EPSILON)
    )


def steps_kernel(
    own_ref,
    other_ref,
    fine_ref,
    coarse_ref,
    mid_one_ref,
    mid_two_ref,
    in_one_ref,
    in_two_ref,
    out_one_ref,
    out_two_ref,
    fine_one_ref,
    fine_two_ref,
    coarse_one_ref,
    coarse_two_ref,
    mid_ref,
    in_ref,
    out_ref,
    fine_step_ref,
    coarse_step_ref,
    scales,
    *,
    decoder_entries,
    grid_entries,
):
    core = lax.axis_index("c")
    tile = axes_index(("x", "y"))
    band = pl.program_id(0)

    @pl.when(band == 0)
    def _():
        own_sum = pair_sum([own_ref[d, 80:88, :] for d in range(16)])
        other_sum = pair_sum([other_ref[d, 80:88, :] for d in range(16)])
        totals = own_sum + other_sum
        scales[0:1, :] = clip_factor(totals[0:1, :], grid_entries)
        scales[1:2, :] = clip_factor(totals[1:2, :], decoder_entries)

    grid_scale = scales[0:1, :]
    scale = scales[1:2, :]
    for block in range(4):
        half = block // 2
        d = tile ^ (band * 2 + block % 2)
        data = jnp.where(half == core, own_ref[d, 0:80, :], other_ref[d, 0:80, :])
        cols = slice(block * 128, block * 128 + 128)
        mid_ref[:, cols] = adam_step(data[0:64], mid_one_ref[:, cols], mid_two_ref[:, cols], scale)
        in_ref[:, cols] = adam_step(data[64:72], in_one_ref[:, cols], in_two_ref[:, cols], scale)

        @pl.when(band == 0)
        def _():
            out_ref[:, cols] = adam_step(
                data[72:75], out_one_ref[:, cols], out_two_ref[:, cols], scale
            )

    fine_step_ref[...] = adam_step(
        fine_ref[...], fine_one_ref[...], fine_two_ref[...], grid_scale[:, None, :]
    )
    coarse_step_ref[...] = adam_step(
        coarse_ref[...], coarse_one_ref[...], coarse_two_ref[...], grid_scale[:, None, 0:CC]
    )


def all_steps(own, other, fine, coarse, moments, decoder_entries, grid_entries):
    mid = pl.BlockSpec((64, 512), lambda b: (b, 0))
    inner = pl.BlockSpec((8, 512), lambda b: (b, 0))
    outer = whole((3, 512))
    fine_spec = pl.BlockSpec((CH // 8, SR, SC), lambda b: (b, 0, 0))
    coarse_spec = pl.BlockSpec((CH // 8, CR, CC), lambda b: (b, 0, 0))
    shapes = ((512, 512), (64, 512), (3, 512), fine.shape, coarse.shape)
    return pl.pallas_call(
        lambda *refs: steps_kernel(
            *refs, decoder_entries=decoder_entries, grid_entries=grid_entries
        ),
        grid=(8,),
        out_shape=tuple(jax.ShapeDtypeStruct(s, F32) for s in shapes),
        in_specs=[whole(own.shape), whole(other.shape), fine_spec, coarse_spec]
        + [mid, mid, inner, inner, outer, outer, fine_spec, fine_spec, coarse_spec, coarse_spec],
        out_specs=(mid, inner, outer, fine_spec, coarse_spec),
        scratch_shapes=[pltpu.VMEM((8, SC), F32)],
        compiler_params=pltpu.CompilerParams(vmem_limit_bytes=16 * MIB),
        name="steps",
    )(own, other, fine, coarse, *moments)


def reduce_grads(keep, send, grid_local):
    part = keep + swapped(send, "c", 1)
    part = scatter_sum([part[d * 4 : d * 4 + 4] for d in range(4)], "x")
    part = scatter_sum([part[d] for d in range(4)], "y")
    part = exchange_sum(jnp.concatenate([part, grid_local]), "zl")
    part = exchange_sum(part, "zh")
    squares = jnp.sum(part[:80] * part[:80])
    tail = jnp.where(jnp.arange(8)[:, None] == 1, squares, part[80:])
    part = jnp.concatenate([part[:80], tail])
    own = jnp.stack(exchange_gather(part, "y"))
    own = jnp.concatenate(exchange_gather(own, "x"))
    return own, swapped(own, "c", 1)


def local_grads(offsets, targets, grid_fine, grid_coarse, weight_in, weight_mid, weight_out):
    row_out, col_out, fine_lines, coarse_lines = edges(grid_fine, grid_coarse)
    row_in = shifted(row_out, -1, 0)
    col_in = shifted(col_out, 0, -1)
    corner_in = shifted(col_out, -1, -1)
    shifts, low_in, in_turned, low_mid, mid_turned, low_out, out_turned, lines, ends = prepare(
        offsets, weight_in.T, weight_mid[0], weight_out, targets
    )
    feat, pre, pred, up, left, down, right = forward(
        shifts, fine_lines, coarse_lines, row_in, col_in, corner_in, lines, ends, low_in, low_mid, low_out
    )
    halos = (shifted(up, -1, 0), shifted(left, 0, -1), shifted(down, 1, 0), shifted(right, 0, 1))
    keep, send, fine, coarse, row_out, col_out, corner_out = backward(
        shifts, feat, pre, pred, *halos, lines, low_in, in_turned, mid_turned, out_turned
    )
    row_in = shifted(row_out, 1, 0)
    col_in = shifted(col_out, 0, 1)
    corner_in = shifted(corner_out, 1, 1)
    return (keep, send, *join(fine, coarse, row_in, col_in, corner_in))


def shards(
    offsets,
    targets,
    grid_fine,
    grid_coarse,
    weight_in,
    weight_mid,
    weight_out,
    fine_first,
    fine_second,
    coarse_first,
    coarse_second,
    in_first,
    in_second,
    mid_first,
    mid_second,
    out_first,
    out_second,
):
    keep, send, fine_grad, coarse_grad, grid_local = local_grads(
        offsets, targets, grid_fine, grid_coarse, weight_in, weight_mid, weight_out
    )
    devices = axes_size(ROW) * axes_size(COL)
    grid_entries = (fine_grad.size + coarse_grad.size) * devices
    decoder_entries = weight_in.size + weight_mid.size + weight_out.size
    own, other = reduce_grads(keep, send, grid_local)
    middle_step, input_step, output_step, fine_step, coarse_step = all_steps(
        own,
        other,
        fine_grad,
        coarse_grad,
        (
            mid_first[0],
            mid_second[0],
            in_first.T,
            in_second.T,
            out_first,
            out_second,
            fine_first,
            fine_second,
            coarse_first,
            coarse_second,
        ),
        decoder_entries,
        grid_entries,
    )
    return (fine_step, coarse_step, input_step.T, middle_step[None], output_step)


def solution(mesh):
    sizes = {"zl": 4, "x": 4, "y": 4, "zh": 2, "c": 2}
    mesh = Mesh(mesh.devices.reshape(tuple(sizes.values())), tuple(sizes))
    placed = (
        P(ROW, COL, None),
        P(None, None, ROW, COL),
        P(None, ROW, COL),
        P(None, ROW, COL),
        P(),
        P(),
        P(),
        P(None, ROW, COL),
        P(None, ROW, COL),
        P(None, ROW, COL),
        P(None, ROW, COL),
        P(),
        P(),
        P(),
        P(),
        P(),
        P(),
    )
    return jax.shard_map(
        shards,
        mesh=mesh,
        in_specs=placed,
        out_specs=(P(None, ROW, COL), P(None, ROW, COL), P(), P(), P()),
        check_vma=False,
    )
```

```python
import jax
import jax.numpy as jnp
from jax import lax
from jax.experimental import pallas as pl
from jax.experimental.pallas import tpu as pltpu
from jax.sharding import Mesh
from jax.sharding import PartitionSpec as P

SUB = 4
RATIO = 4
ADAM_STEP = 10

BETA_ONE = 0.9
BETA_TWO = 0.99
ADAM_EPSILON = 1e-08
CLIP_RMS = 0.01
LOSS_VALUE = 0.25
MEAN_EPSILON = 1e-06

ROW = ("zl", "x")
COL = ("y", "zh", "c")
SR = 32
SC = 128
CH = 32
CR = 8
CC = 32
HID = 512
CHAINS = 4
WIDTH = SR * SC // CHAINS
LINES = SR // CHAINS
PARTS = 2
F32 = jnp.float32
BF16 = jnp.bfloat16
MIB = 1 << 20


def axes_size(axes):
    total = 1
    for axis in axes:
        total *= lax.axis_size(axis)
    return total


def axes_index(axes):
    index = 0
    for axis in axes:
        index = index * lax.axis_size(axis) + lax.axis_index(axis)
    return index


def shifted(block, down, right):
    rows, cols = axes_size(ROW), axes_size(COL)
    if not right:
        return lax.ppermute(block, ROW, [(i, (i + down) % rows) for i in range(rows)])
    if not down:
        return lax.ppermute(block, COL, [(i, (i + right) % cols) for i in range(cols)])
    route = [
        (r * cols + c, (r + down) % rows * cols + (c + right) % cols)
        for r in range(rows)
        for c in range(cols)
    ]
    return lax.ppermute(block, ROW + COL, route)


def meetings(block_one, block_two, axes):
    size = axes_size(axes)
    one = [(i, i ^ 1) for i in range(size)]
    two = [(i, (i + 1 if i % 2 else i - 1) % size) for i in range(size)]
    return lax.ppermute(block_one, axes, one), lax.ppermute(block_two, axes, two)


def at_ends():
    row, col = axes_index(ROW), axes_index(COL)
    return row == 0, row == axes_size(ROW) - 1, col == 0, col == axes_size(COL) - 1


def swapped(block, axis, mask):
    size = lax.axis_size(axis)
    return lax.ppermute(block, axis, [(i, i ^ mask) for i in range(size)])


def pair_sum(values):
    values = list(values)
    while len(values) > 1:
        values = [values[i] + values[i + 1] for i in range(0, len(values), 2)]
    return values[0]


def exchange_sum(block, axis):
    return pair_sum([block] + [swapped(block, axis, d) for d in range(1, lax.axis_size(axis))])


def exchange_gather(block, axis):
    return [block] + [swapped(block, axis, d) for d in range(1, lax.axis_size(axis))]


def scatter_sum(blocks, axis):
    return pair_sum([blocks[0]] + [swapped(blocks[d], axis, d) for d in range(1, len(blocks))])


def vmem():
    return pl.BlockSpec(memory_space=pltpu.VMEM)


def smem():
    return pl.BlockSpec(memory_space=pltpu.SMEM)


def hbm():
    return pl.BlockSpec(memory_space=pltpu.HBM)


def in_hbm(array):
    return pltpu.with_memory_space_constraint(array, pltpu.HBM)


def whole(shape, memory_space=pltpu.VMEM):
    return pl.BlockSpec(shape, lambda b: (0,) * len(shape), memory_space=memory_space)


def lane_ids(rows):
    return lax.broadcasted_iota(jnp.int32, (rows, SC), 1)


def spread_lane(block, lane):
    return jnp.broadcast_to(block[:, lane : lane + 1], (block.shape[0], SC))


def dot(former, latter, former_dim=1, latter_dim=0, precision=None):
    return lax.dot_general(
        former,
        latter,
        (((former_dim,), (latter_dim,)), ((), ())),
        precision=precision,
        preferred_element_type=F32,
    )


def sigmoid(value):
    return 0.5 * jnp.tanh(0.5 * value) + 0.5


def coarse_table(shift_x):
    line = lax.broadcasted_iota(jnp.int32, (SC, SC), 0)
    sample = lax.broadcasted_iota(jnp.int32, (SC, SC), 1)
    base = sample >> 2
    fraction = ((sample & 3).astype(F32) + shift_x) * (1.0 / RATIO)
    return jnp.where(line == base, 1.0 - fraction, 0.0) + jnp.where(line == base + 1, fraction, 0.0)


def edges_kernel(fine_hbm, coarse_hbm, row_ref, col_ref, fine_ref, coarse_ref, fine, coarse, sems):
    copies = [
        pltpu.make_async_copy(fine_hbm, fine, sems.at[0]),
        pltpu.make_async_copy(coarse_hbm, coarse, sems.at[1]),
    ]
    for copy in copies:
        copy.start()
    for copy in copies:
        copy.wait()
    lane = lane_ids(CH)
    row_ref[:, 0:SC] = fine[:, 0, :]
    row_ref[:, SC:] = jnp.zeros((CH, SC), F32)
    row_ref[:, SC : SC + CC] = coarse[:, 0, :]
    coarse_ref[...] = jnp.zeros(coarse_ref.shape, F32)
    cols = jnp.zeros((CH, SC), F32)
    for i in range(SR):
        line = fine[:, i, :]
        fine_ref[i] = line
        cols = jnp.where(lane == i, spread_lane(line, 0), cols)
    for i in range(CR):
        line = coarse[:, i, :]
        coarse_ref[i, :, 0:CC] = line
        cols = jnp.where(lane == SR + i, spread_lane(line, 0), cols)
    col_ref[...] = cols


def edges(fine, coarse):
    shapes = ((CH, 2 * SC), (CH, SC), (SR, CH, SC), (CR, CH, SC))
    return pl.pallas_call(
        edges_kernel,
        out_shape=tuple(jax.ShapeDtypeStruct(d, F32) for d in shapes),
        in_specs=[hbm(), hbm()],
        out_specs=(vmem(),) * 4,
        scratch_shapes=[
            pltpu.VMEM(fine.shape, F32),
            pltpu.VMEM(coarse.shape, F32),
            pltpu.SemaphoreType.DMA((2,)),
        ],
        compiler_params=pltpu.CompilerParams(vmem_limit_bytes=8 * MIB),
        name="edges",
    )(in_hbm(fine), in_hbm(coarse))


def prepare_kernel(
    offset_ref,
    in_hbm,
    mid_hbm,
    out_hbm,
    target_hbm,
    shift_ref,
    in_ref,
    in_turned_ref,
    mid_ref,
    mid_turned_ref,
    out_ref,
    out_turned_ref,
    target_ref,
    ends_ref,
    w_in,
    w_mid,
    w_out,
    targets,
    sems,
):
    copies = [
        pltpu.make_async_copy(source, target, sems.at[i])
        for i, (source, target) in enumerate(
            ((in_hbm, w_in), (out_hbm, w_out), (target_hbm, targets), (mid_hbm, w_mid))
        )
    ]
    for copy in copies:
        copy.start()
    shift_ref[...] = jnp.zeros((8, SC), F32)
    for i in range(2):
        shift = offset_ref[0, 0, i].astype(F32) * (1.0 / SUB)
        shift_ref[i : i + 1, :] = jnp.full((1, SC), shift, F32)
    copies[0].wait()
    in_turned_ref[...] = w_in[...].astype(BF16)
    for block in range(4):
        cols = slice(block * 128, block * 128 + 128)
        in_ref[cols, :] = w_in[:, cols].T.astype(BF16)
    copies[1].wait()
    padded = jnp.concatenate([w_out[...], jnp.zeros((13, HID), F32)], axis=0)
    out_ref[...] = padded.astype(BF16)
    for block in range(4):
        cols = slice(block * 128, block * 128 + 128)
        out_turned_ref[cols, :] = padded[:, cols].T.astype(BF16)
    copies[2].wait()
    lane = lane_ids(3)
    ends = jnp.zeros((3, SC), F32)
    target_ref[...] = jnp.zeros(target_ref.shape, F32)
    for i in range(SR):
        for kind in range(3):
            line = targets[kind, :, i, :]
            target_ref[kind, 0:3, i * SC : i * SC + SC] = line
        ends = jnp.where(lane == i, spread_lane(line, SC - 1), ends)
    ends_ref[...] = jnp.zeros((8, SC), F32)
    ends_ref[0:3, :] = ends
    copies[3].wait()
    mid_ref[...] = w_mid[...].astype(BF16)
    for i in range(4):
        for j in range(4):
            rows = slice(i * 128, i * 128 + 128)
            cols = slice(j * 128, j * 128 + 128)
            mid_turned_ref[cols, rows] = w_mid[rows, cols].T.astype(BF16)


def prepare(offsets, w_in, w_mid, w_out, targets):
    outs = (
        jax.ShapeDtypeStruct((8, SC), F32),
        jax.ShapeDtypeStruct((HID, 2 * CH), BF16),
        jax.ShapeDtypeStruct((2 * CH, HID), BF16),
        jax.ShapeDtypeStruct((HID, HID), BF16),
        jax.ShapeDtypeStruct((HID, HID), BF16),
        jax.ShapeDtypeStruct((16, HID), BF16),
        jax.ShapeDtypeStruct((HID, 16), BF16),
        jax.ShapeDtypeStruct((3, 8, SR * SC), F32),
        jax.ShapeDtypeStruct((8, SC), F32),
    )
    return pl.pallas_call(
        prepare_kernel,
        out_shape=outs,
        in_specs=[smem(), hbm(), hbm(), hbm(), hbm()],
        out_specs=(vmem(),) * len(outs),
        scratch_shapes=[pltpu.VMEM(a.shape, F32) for a in (w_in, w_mid, w_out, targets)]
        + [pltpu.SemaphoreType.DMA((4,))],
        compiler_params=pltpu.CompilerParams(vmem_limit_bytes=8 * MIB),
        name="prepare",
    )(offsets, *(in_hbm(a) for a in (w_in, w_mid, w_out, targets)))


def forward_kernel(
    shift_ref,
    fine_ref,
    coarse_ref,
    row_ref,
    col_ref,
    corner_ref,
    target_ref,
    ends_ref,
    in_ref,
    mid_ref,
    out_ref,
    feat_ref,
    pre_ref,
    pred_ref,
    row_one_ref,
    row_two_ref,
    col_one_ref,
    col_two_ref,
):
    shift_y = shift_ref[0:1, :]
    shift_x = shift_ref[1:2, :]
    lane = lane_ids(CH)
    unused_first_row, last_row, unused_first_col, last_col = at_ends()
    row_in = jnp.where(last_row, 0.0, row_ref[...])
    col_in = jnp.where(last_col, 0.0, col_ref[...])
    corner_in = jnp.where(jnp.logical_or(last_row, last_col), 0.0, corner_ref[...])

    def across(line, following):
        moved = jnp.where(lane == SC - 1, following, pltpu.roll(line, SC - 1, 1))
        return line * (1.0 - shift_x) + moved * shift_x

    stage = []
    for i in range(CR):
        stage.append(jnp.where(lane == CC, spread_lane(col_in, SR + i), coarse_ref[i]))
    stage.append(jnp.where(lane == CC, spread_lane(corner_in, SR), row_in[:, SC:]))
    bands = dot(
        jnp.concatenate(stage, axis=0), coarse_table(shift_x), precision=lax.Precision.HIGHEST
    )
    bands = [bands[i * CH : i * CH + CH] for i in range(CR + 1)]
    lane8 = lane_ids(8)
    left = jnp.zeros((8, SC), F32)
    right = ends_ref[...]
    line = across(fine_ref[0], spread_lane(col_in, 0))
    for chain in range(CHAINS):
        tiles = []
        for k in range(LINES):
            row = chain * LINES + k
            if row + 1 < SR:
                following = across(fine_ref[row + 1], spread_lane(col_in, row + 1))
            else:
                following = across(row_in[:, 0:SC], spread_lane(corner_in, 0))
            fine = line * (1.0 - shift_y) + following * shift_y
            line = following
            band = row // RATIO
            part = (row % RATIO + shift_y) * (1.0 / RATIO)
            coarse = bands[band] * (1.0 - part) + bands[band + 1] * part
            tiles.append(jnp.concatenate([fine, coarse], axis=0).astype(BF16))
        feat = jnp.concatenate(tiles, axis=1)
        cols = slice(chain * WIDTH, chain * WIDTH + WIDTH)
        feat_ref[:, cols] = feat
        pre = dot(in_ref[...], feat)
        act = (pre * sigmoid(pre)).astype(BF16)
        pre = dot(mid_ref[...], act)
        pre_ref[:, cols] = pre
        act = (pre * sigmoid(pre)).astype(BF16)
        pred = dot(out_ref[...], act)[0:8]
        pred_ref[:, cols] = pred
        for k in range(LINES):
            row = chain * LINES + k
            tile = pred[:, k * SC : k * SC + SC]
            left = jnp.where(lane8 == row, spread_lane(tile, 0), left)
            right = right + jnp.where(lane8 == row, spread_lane(tile, SC - 1), 0.0)
        if chain == 0:
            up = pred[:, 0:SC]
    down = pred[:, WIDTH - SC :] + target_ref[1, :, SR * SC - SC :]
    odd_row = axes_index(ROW) % 2 == 1
    odd_col = axes_index(COL) % 2 == 1
    row_one_ref[...] = jnp.where(odd_row, up, down)
    row_two_ref[...] = jnp.where(odd_row, down, up)
    col_one_ref[...] = jnp.where(odd_col, left, right)
    col_two_ref[...] = jnp.where(odd_col, right, left)


def forward(*args):
    edge = jax.ShapeDtypeStruct((8, SC), F32)
    outs = (
        jax.ShapeDtypeStruct((2 * CH, SR * SC), BF16),
        jax.ShapeDtypeStruct((HID, SR * SC), F32),
        jax.ShapeDtypeStruct((8, SR * SC), F32),
        edge,
        edge,
        edge,
        edge,
    )
    return pl.pallas_call(
        forward_kernel,
        out_shape=outs,
        in_specs=[vmem()] * len(args),
        out_specs=(vmem(),) * len(outs),
        compiler_params=pltpu.CompilerParams(vmem_limit_bytes=24 * MIB),
        name="forward",
    )(*args)


def loss_cotangent(pred_ref, target_ref, below, beside, above, before, cot):
    first_row, last_row, first_col, last_col = at_ends()
    lane = lane_ids(3)
    cot[...] = jnp.zeros(cot.shape, F32)
    line = pred_ref[0:3, 0:SC]
    row_prior = jnp.where(first_row, 0.0, line - above)
    for i in range(SR):
        if i + 1 < SR:
            following = pred_ref[0:3, (i + 1) * SC : (i + 2) * SC]
        else:
            following = below
        value_error = line - target_ref[0, 0:3, i * SC : i * SC + SC]
        row_error = following - line - target_ref[1, 0:3, i * SC : i * SC + SC]
        if i + 1 == SR:
            row_error = jnp.where(last_row, 0.0, row_error)
        beyond = jnp.where(lane == SC - 1, spread_lane(beside, i), pltpu.roll(line, SC - 1, 1))
        col_error = beyond - line - target_ref[2, 0:3, i * SC : i * SC + SC]
        col_error = jnp.where(jnp.logical_and(lane == SC - 1, last_col), 0.0, col_error)
        edge = jnp.where(first_col, 0.0, line - spread_lane(before, i))
        col_prior = jnp.where(lane == 0, edge, pltpu.roll(col_error, 1, 1))
        cot[0:3, i * SC : (i + 1) * SC] = (
            2.0 * LOSS_VALUE * value_error
            + 2.0 * (row_prior - row_error)
            + 2.0 * (col_prior - col_error)
        )
        line = following
        row_prior = row_error


def backward_kernel(
    shift_ref,
    feat_ref,
    pre_ref,
    pred_ref,
    row_one_ref,
    row_two_ref,
    col_one_ref,
    col_two_ref,
    target_ref,
    in_ref,
    in_turned_ref,
    mid_turned_ref,
    out_turned_ref,
    keep_ref,
    send_ref,
    fine_ref,
    coarse_ref,
    row_ref,
    col_ref,
    corner_ref,
    cot,
    grad_mid,
    grad_in,
    grad_out,
):
    shift_y = shift_ref[0:1, :]
    shift_x = shift_ref[1:2, :]
    lane = lane_ids(CH)
    odd_row = axes_index(ROW) % 2 == 1
    odd_col = axes_index(COL) % 2 == 1
    row_one, row_two = row_one_ref[0:3, :], row_two_ref[0:3, :]
    col_one, col_two = col_one_ref[0:3, :], col_two_ref[0:3, :]
    loss_cotangent(
        pred_ref,
        target_ref,
        jnp.where(odd_row, row_two, row_one),
        jnp.where(odd_col, col_two, col_one),
        jnp.where(odd_row, row_one, row_two),
        jnp.where(odd_col, col_one, col_two),
        cot,
    )

    def along(line):
        moved = jnp.where(lane == 0, 0.0, pltpu.roll(line, 1, 1))
        return line * (1.0 - shift_x) + moved * shift_x

    prior = jnp.zeros((CH, SC), F32)
    ends = jnp.zeros((CH, SC), F32)
    upper = jnp.zeros((CH, SC), F32)
    lower = jnp.zeros((CH, SC), F32)
    bands = []
    for chain in range(CHAINS):
        cols = slice(chain * WIDTH, chain * WIDTH + WIDTH)
        feat = feat_ref[:, cols]
        out_cot = cot[:, cols].astype(BF16)
        pre = pre_ref[:, cols]
        gate = sigmoid(pre)
        act = (pre * gate).astype(BF16)
        part = dot(out_cot, act, 1, 1)
        grad_out[...] = part if chain == 0 else grad_out[...] + part
        upward = dot(out_turned_ref[...], out_cot)
        delta = (upward * (gate * (1.0 + pre * (1.0 - gate)))).astype(BF16)
        pre = dot(in_ref[...], feat)
        gate = sigmoid(pre)
        act = (pre * gate).astype(BF16)
        part = dot(delta, act, 1, 1)
        grad_mid[...] = part if chain == 0 else grad_mid[...] + part
        upward = dot(mid_turned_ref[...], delta)
        delta = (upward * (gate * (1.0 + pre * (1.0 - gate)))).astype(BF16)
        part = dot(feat, delta, 1, 1)
        grad_in[...] = part if chain == 0 else grad_in[...] + part
        feat_grad = dot(in_turned_ref[...], delta)
        for k in range(LINES):
            row = chain * LINES + k
            fine = feat_grad[0:CH, k * SC : k * SC + SC]
            line = fine * (1.0 - shift_y) + prior * shift_y
            fine_ref[row] = along(line)
            ends = jnp.where(lane == row, spread_lane(line * shift_x, SC - 1), ends)
            prior = fine
            coarse = feat_grad[CH:, k * SC : k * SC + SC]
            weight = (row % RATIO + shift_y) * (1.0 / RATIO)
            upper += coarse * (1.0 - weight)
            lower += coarse * weight
            if row % RATIO == RATIO - 1:
                bands.append(upper)
                upper = lower
                lower = jnp.zeros((CH, SC), F32)
    bands.append(upper)
    line = prior * shift_y
    row_ref[:, 0:SC] = along(line)
    corner = jnp.where(lane == 0, spread_lane(line * shift_x, SC - 1), 0.0)
    spread = dot(
        jnp.concatenate(bands, axis=0),
        coarse_table(shift_x),
        1,
        1,
        precision=lax.Precision.HIGHEST,
    )
    for i in range(CR):
        band = spread[i * CH : i * CH + CH]
        coarse_ref[i] = jnp.where(lane < CC, band, 0.0)
        ends = jnp.where(lane == SR + i, spread_lane(band, CC), ends)
    col_ref[...] = ends
    band = spread[CR * CH :]
    row_ref[:, SC:] = jnp.where(lane < CC, band, 0.0)
    corner_ref[...] = jnp.where(lane == SR, spread_lane(band, CC), corner)
    core = lax.axis_index("c")
    tile = axes_index(("x", "y"))
    for d in range(16):
        chunk = tile ^ d
        band = chunk >> 1
        side = chunk & 1
        for half, target in ((core, keep_ref), (1 - core, send_ref)):
            cols = pl.ds(pl.multiple_of((half * 2 + side) * 128, 128), 128)
            target[d, 0:64, :] = grad_mid[pl.ds(pl.multiple_of(band * 64, 64), 64), cols]
            target[d, 64:72, :] = grad_in[pl.ds(pl.multiple_of(band * 8, 8), 8), cols]
            target[d, 72:80, :] = jnp.where(band == 0, grad_out[0:8, cols], 0.0)


def backward(*args):
    part = jax.ShapeDtypeStruct((16, 80, 128), F32)
    outs = (
        part,
        part,
        jax.ShapeDtypeStruct((SR, CH, SC), F32),
        jax.ShapeDtypeStruct((CR, CH, SC), F32),
        jax.ShapeDtypeStruct((CH, 2 * SC), F32),
        jax.ShapeDtypeStruct((CH, SC), F32),
        jax.ShapeDtypeStruct((CH, SC), F32),
    )
    return pl.pallas_call(
        backward_kernel,
        out_shape=outs,
        in_specs=[vmem()] * len(args),
        out_specs=(vmem(),) * len(outs),
        scratch_shapes=[
            pltpu.VMEM((16, SR * SC), F32),
            pltpu.VMEM((HID, HID), F32),
            pltpu.VMEM((2 * CH, HID), F32),
            pltpu.VMEM((16, HID), F32),
        ],
        compiler_params=pltpu.CompilerParams(vmem_limit_bytes=32 * MIB),
        name="backward",
    )(*args)


def join_kernel(fine_ref, coarse_ref, row_ref, col_ref, corner_ref, fine_out, coarse_out, total_ref):
    lane = lane_ids(CH)
    first_row, unused_last_row, first_col, unused_last_col = at_ends()
    rows = jnp.where(first_row, 0.0, row_ref[...])
    cols = jnp.where(first_col, 0.0, col_ref[...])
    corner = jnp.where(jnp.logical_or(first_row, first_col), 0.0, corner_ref[...])
    total = jnp.zeros((CH, SC), F32)
    for i in range(SR):
        line = fine_ref[i] + jnp.where(lane == 0, spread_lane(cols, i), 0.0)
        if i == 0:
            line += rows[:, 0:SC]
            line += jnp.where(lane == 0, spread_lane(corner, 0), 0.0)
        fine_out[:, i, :] = line
        total += line * line
    for i in range(CR):
        line = coarse_ref[i] + jnp.where(lane == 0, spread_lane(cols, SR + i), 0.0)
        if i == 0:
            line += rows[:, SC:]
            line += jnp.where(lane == 0, spread_lane(corner, SR), 0.0)
        coarse_out[:, i, :] = line[:, 0:CC]
        total += line * line
    total = jnp.sum(jnp.sum(total, axis=0, keepdims=True), axis=1, keepdims=True)
    total_ref[...] = jnp.broadcast_to(total, (8, SC))


def join(fine, coarse, row_in, col_in, corner_in):
    return pl.pallas_call(
        join_kernel,
        out_shape=(
            jax.ShapeDtypeStruct((CH, SR, SC), F32),
            jax.ShapeDtypeStruct((CH, CR, CC), F32),
            jax.ShapeDtypeStruct((8, SC), F32),
        ),
        in_specs=[vmem()] * 5,
        out_specs=(vmem(),) * 3,
        compiler_params=pltpu.CompilerParams(vmem_limit_bytes=8 * MIB),
        name="join",
    )(fine, coarse, row_in, col_in, corner_in)


def clip_factor(total, entries):
    return jnp.minimum(1.0, CLIP_RMS / jnp.sqrt(total / entries + MEAN_EPSILON))


def adam_step(gradient, moment_one, moment_two, clip_scale):
    clipped = gradient * clip_scale
    new_one = BETA_ONE * moment_one + (1.0 - BETA_ONE) * clipped
    new_two = BETA_TWO * moment_two + (1.0 - BETA_TWO) * clipped * clipped
    return (
        new_one
        * (1.0 / (1.0 - BETA_ONE**ADAM_STEP))
        / (jnp.sqrt(new_two * (1.0 / (1.0 - BETA_TWO**ADAM_STEP))) + ADAM_EPSILON)
    )


def steps_kernel(
    own_ref,
    other_ref,
    fine_ref,
    coarse_ref,
    mid_one_ref,
    mid_two_ref,
    in_one_ref,
    in_two_ref,
    out_one_ref,
    out_two_ref,
    fine_one_ref,
    fine_two_ref,
    coarse_one_ref,
    coarse_two_ref,
    mid_ref,
    in_ref,
    out_ref,
    fine_step_ref,
    coarse_step_ref,
    scales,
    *,
    decoder_entries,
    grid_entries,
):
    core = lax.axis_index("c")
    tile = axes_index(("x", "y"))
    step = pl.program_id(0)

    @pl.when(step == 0)
    def _():
        own_sum = pair_sum([own_ref[d, 80:88, :] for d in range(16)])
        other_sum = pair_sum([other_ref[d, 80:88, :] for d in range(16)])
        totals = own_sum + other_sum
        scales[0:1, :] = clip_factor(totals[0:1, :], grid_entries)
        scales[1:2, :] = clip_factor(totals[1:2, :], decoder_entries)
        for block in range(4):
            d = tile ^ (block % 2)
            data = jnp.where(block // 2 == core, own_ref[d, 72:80, :], other_ref[d, 72:80, :])
            cols = slice(block * 128, block * 128 + 128)
            out_ref[:, cols] = adam_step(
                data[0:3], out_one_ref[:, cols], out_two_ref[:, cols], scales[1:2, :]
            )

    grid_scale = scales[0:1, :]
    scale = scales[1:2, :]
    for k in range(8 // PARTS):
        for block in range(4):
            d = tile ^ ((step * (8 // PARTS) + k) * 2 + block % 2)
            data = jnp.where(block // 2 == core, own_ref[d, 0:72, :], other_ref[d, 0:72, :])
            at = (slice(k * 64, k * 64 + 64), slice(block * 128, block * 128 + 128))
            mid_ref[at] = adam_step(data[0:64], mid_one_ref[at], mid_two_ref[at], scale)
            at = (slice(k * 8, k * 8 + 8), slice(block * 128, block * 128 + 128))
            in_ref[at] = adam_step(data[64:72], in_one_ref[at], in_two_ref[at], scale)
    fine_step_ref[...] = adam_step(
        fine_ref[...], fine_one_ref[...], fine_two_ref[...], grid_scale[:, None, :]
    )
    coarse_step_ref[...] = adam_step(
        coarse_ref[...], coarse_one_ref[...], coarse_two_ref[...], grid_scale[:, None, 0:CC]
    )


def all_steps(own, other, fine, coarse, moments, decoder_entries, grid_entries):
    mid = pl.BlockSpec((512 // PARTS, 512), lambda b: (b, 0))
    inner = pl.BlockSpec((64 // PARTS, 512), lambda b: (b, 0))
    outer = whole((3, 512))
    fine_spec = pl.BlockSpec((CH // PARTS, SR, SC), lambda b: (b, 0, 0))
    coarse_spec = pl.BlockSpec((CH // PARTS, CR, CC), lambda b: (b, 0, 0))
    shapes = ((512, 512), (64, 512), (3, 512), fine.shape, coarse.shape)
    return pl.pallas_call(
        lambda *refs: steps_kernel(
            *refs, decoder_entries=decoder_entries, grid_entries=grid_entries
        ),
        grid=(PARTS,),
        out_shape=tuple(jax.ShapeDtypeStruct(s, F32) for s in shapes),
        in_specs=[whole(own.shape), whole(other.shape), fine_spec, coarse_spec]
        + [mid, mid, inner, inner, outer, outer, fine_spec, fine_spec, coarse_spec, coarse_spec],
        out_specs=(mid, inner, outer, fine_spec, coarse_spec),
        scratch_shapes=[pltpu.VMEM((8, SC), F32)],
        compiler_params=pltpu.CompilerParams(vmem_limit_bytes=16 * MIB),
        name="steps",
    )(own, other, fine, coarse, *moments)


def tally_kernel(one_ref, two_ref, out_ref):
    total = one_ref[...] + two_ref[...]
    grads = total[0:80]
    squares = jnp.sum(grads * grads, axis=0, keepdims=True)
    squares = jnp.broadcast_to(jnp.sum(squares, axis=1, keepdims=True), (1, SC))
    out_ref[...] = total
    out_ref[81:82, :] = squares


def tally(one, two):
    return pl.pallas_call(
        tally_kernel,
        out_shape=jax.ShapeDtypeStruct(one.shape, F32),
        in_specs=[vmem(), vmem()],
        out_specs=vmem(),
        compiler_params=pltpu.CompilerParams(vmem_limit_bytes=4 * MIB),
        name="tally",
    )(one, two)


def reduce_grads(keep, send, fine, coarse, halos):
    part = keep + swapped(send, "c", 1)
    part = scatter_sum([part[d * 4 : d * 4 + 4] for d in range(4)], "x")
    part, *halos = lax.optimization_barrier((part, *halos))
    fine, coarse, grid_local = join(fine, coarse, *halos)
    part = scatter_sum([part[d] for d in range(4)], "y")
    part = exchange_sum(jnp.concatenate([part, grid_local]), "zl")
    part = tally(part, swapped(part, "zh", 1))
    own = jnp.stack(exchange_gather(part, "y"))
    own = jnp.concatenate(exchange_gather(own, "x"))
    return own, swapped(own, "c", 1), fine, coarse


def local_grads(offsets, targets, grid_fine, grid_coarse, weight_in, weight_mid, weight_out):
    row_out, col_out, fine_lines, coarse_lines = edges(grid_fine, grid_coarse)
    row_in = shifted(row_out, -1, 0)
    col_in = shifted(col_out, 0, -1)
    corner_in = shifted(col_out, -1, -1)
    shifts, low_in, in_turned, low_mid, mid_turned, low_out, out_turned, lines, ends = prepare(
        offsets, weight_in.T, weight_mid[0], weight_out, targets
    )
    feat, pre, pred, row_one, row_two, col_one, col_two = forward(
        shifts, fine_lines, coarse_lines, row_in, col_in, corner_in, lines, ends, low_in, low_mid, low_out
    )
    halos = (*meetings(row_one, row_two, ROW), *meetings(col_one, col_two, COL))
    keep, send, fine, coarse, row_out, col_out, corner_out = backward(
        shifts, feat, pre, pred, *halos, lines, low_in, in_turned, mid_turned, out_turned
    )
    halos = (shifted(row_out, 1, 0), shifted(col_out, 0, 1), shifted(corner_out, 1, 1))
    return keep, send, fine, coarse, halos


def shards(
    offsets,
    targets,
    grid_fine,
    grid_coarse,
    weight_in,
    weight_mid,
    weight_out,
    fine_first,
    fine_second,
    coarse_first,
    coarse_second,
    in_first,
    in_second,
    mid_first,
    mid_second,
    out_first,
    out_second,
):
    keep, send, fine, coarse, halos = local_grads(
        offsets, targets, grid_fine, grid_coarse, weight_in, weight_mid, weight_out
    )
    own, other, fine_grad, coarse_grad = reduce_grads(keep, send, fine, coarse, halos)
    devices = axes_size(ROW) * axes_size(COL)
    grid_entries = (fine_grad.size + coarse_grad.size) * devices
    decoder_entries = weight_in.size + weight_mid.size + weight_out.size
    middle_step, input_step, output_step, fine_step, coarse_step = all_steps(
        own,
        other,
        fine_grad,
        coarse_grad,
        (
            mid_first[0],
            mid_second[0],
            in_first.T,
            in_second.T,
            out_first,
            out_second,
            fine_first,
            fine_second,
            coarse_first,
            coarse_second,
        ),
        decoder_entries,
        grid_entries,
    )
    return (fine_step, coarse_step, input_step.T, middle_step[None], output_step)


def solution(mesh):
    sizes = {"zl": 4, "x": 4, "y": 4, "zh": 2, "c": 2}
    mesh = Mesh(mesh.devices.reshape(tuple(sizes.values())), tuple(sizes))
    placed = (
        P(ROW, COL, None),
        P(None, None, ROW, COL),
        P(None, ROW, COL),
        P(None, ROW, COL),
        P(),
        P(),
        P(),
        P(None, ROW, COL),
        P(None, ROW, COL),
        P(None, ROW, COL),
        P(None, ROW, COL),
        P(),
        P(),
        P(),
        P(),
        P(),
        P(),
    )
    return jax.shard_map(
        shards,
        mesh=mesh,
        in_specs=placed,
        out_specs=(P(None, ROW, COL), P(None, ROW, COL), P(), P(), P()),
        check_vma=False,
    )
```

```python
import jax
import jax.numpy as jnp
from jax import lax
from jax.experimental import pallas as pl
from jax.experimental.pallas import tpu as pltpu
from jax.sharding import Mesh
from jax.sharding import PartitionSpec as P

SUB = 4
RATIO = 4
ADAM_STEP = 10

BETA_ONE = 0.9
BETA_TWO = 0.99
ADAM_EPSILON = 1e-08
CLIP_RMS = 0.01
LOSS_VALUE = 0.25
MEAN_EPSILON = 1e-06

ROW = ("zl", "x")
COL = ("y", "zh", "c")
SR = 32
SC = 128
CH = 32
CR = 8
CC = 32
HID = 512
CHAINS = 4
WIDTH = SR * SC // CHAINS
LINES = SR // CHAINS
PARTS = 2
FINE_CORNER = 64
COARSE_CORNER = 65
F32 = jnp.float32
BF16 = jnp.bfloat16
MIB = 1 << 20


def axes_size(axes):
    total = 1
    for axis in axes:
        total *= lax.axis_size(axis)
    return total


def axes_index(axes):
    index = 0
    for axis in axes:
        index = index * lax.axis_size(axis) + lax.axis_index(axis)
    return index


def shifted(block, down, right):
    rows, cols = axes_size(ROW), axes_size(COL)
    if not right:
        return lax.ppermute(block, ROW, [(i, (i + down) % rows) for i in range(rows)])
    if not down:
        return lax.ppermute(block, COL, [(i, (i + right) % cols) for i in range(cols)])
    route = [
        (r * cols + c, (r + down) % rows * cols + (c + right) % cols)
        for r in range(rows)
        for c in range(cols)
    ]
    return lax.ppermute(block, ROW + COL, route)


def meetings(block_one, block_two, axes):
    size = axes_size(axes)
    one = [(i, i ^ 1) for i in range(size)]
    two = [(i, (i + 1 if i % 2 else i - 1) % size) for i in range(size)]
    block_two = lax.ppermute(block_two, axes, two)
    return lax.ppermute(block_one, axes, one), block_two


def at_ends():
    row, col = axes_index(ROW), axes_index(COL)
    return row == 0, row == axes_size(ROW) - 1, col == 0, col == axes_size(COL) - 1


def swapped(block, axis, mask):
    size = lax.axis_size(axis)
    return lax.ppermute(block, axis, [(i, i ^ mask) for i in range(size)])


def pair_sum(values):
    values = list(values)
    while len(values) > 1:
        values = [values[i] + values[i + 1] for i in range(0, len(values), 2)]
    return values[0]


def exchange_sum(block, axis):
    return pair_sum([block] + [swapped(block, axis, d) for d in range(1, lax.axis_size(axis))])


def all_to_all(blocks):
    return lax.all_to_all(blocks, ("x", "y"), 0, 0, tiled=True)


def scatter_sum(blocks, axis):
    return pair_sum([blocks[0]] + [swapped(blocks[d], axis, d) for d in range(1, len(blocks))])


def vmem():
    return pl.BlockSpec(memory_space=pltpu.VMEM)


def smem():
    return pl.BlockSpec(memory_space=pltpu.SMEM)


def hbm():
    return pl.BlockSpec(memory_space=pltpu.HBM)


def in_hbm(array):
    return pltpu.with_memory_space_constraint(array, pltpu.HBM)


def whole(shape, memory_space=pltpu.VMEM):
    return pl.BlockSpec(shape, lambda b: (0,) * len(shape), memory_space=memory_space)


def lane_ids(rows):
    return lax.broadcasted_iota(jnp.int32, (rows, SC), 1)


def spread_lane(block, lane):
    return jnp.broadcast_to(block[:, lane : lane + 1], (block.shape[0], SC))


def dot(former, latter, former_dim=1, latter_dim=0, precision=None):
    return lax.dot_general(
        former,
        latter,
        (((former_dim,), (latter_dim,)), ((), ())),
        precision=precision,
        preferred_element_type=F32,
    )


def sigmoid(value):
    return 0.5 * jnp.tanh(0.5 * value) + 0.5


def coarse_table(shift_x):
    line = lax.broadcasted_iota(jnp.int32, (SC, SC), 0)
    sample = lax.broadcasted_iota(jnp.int32, (SC, SC), 1)
    base = sample >> 2
    fraction = ((sample & 3).astype(F32) + shift_x) * (1.0 / RATIO)
    return jnp.where(line == base, 1.0 - fraction, 0.0) + jnp.where(line == base + 1, fraction, 0.0)


def edges_kernel(fine_hbm, coarse_hbm, row_ref, col_ref, fine_ref, coarse_ref, fine, coarse, sems):
    copies = [
        pltpu.make_async_copy(fine_hbm, fine, sems.at[0]),
        pltpu.make_async_copy(coarse_hbm, coarse, sems.at[1]),
    ]
    for copy in copies:
        copy.start()
    for copy in copies:
        copy.wait()
    lane = lane_ids(CH)
    row_ref[:, 0:SC] = fine[:, 0, :]
    row_ref[:, SC:] = jnp.zeros((CH, SC), F32)
    row_ref[:, SC : SC + CC] = coarse[:, 0, :]
    coarse_ref[...] = jnp.zeros(coarse_ref.shape, F32)
    cols = jnp.zeros((CH, SC), F32)
    for i in range(SR):
        line = fine[:, i, :]
        fine_ref[i] = line
        cols = jnp.where(lane == i, spread_lane(line, 0), cols)
    for i in range(CR):
        line = coarse[:, i, :]
        coarse_ref[i, :, 0:CC] = line
        cols = jnp.where(lane == SR + i, spread_lane(line, 0), cols)
    col_ref[...] = cols


def edges(fine, coarse):
    shapes = ((CH, 2 * SC), (CH, SC), (SR, CH, SC), (CR, CH, SC))
    return pl.pallas_call(
        edges_kernel,
        out_shape=tuple(jax.ShapeDtypeStruct(d, F32) for d in shapes),
        in_specs=[hbm(), hbm()],
        out_specs=(vmem(),) * 4,
        scratch_shapes=[
            pltpu.VMEM(fine.shape, F32),
            pltpu.VMEM(coarse.shape, F32),
            pltpu.SemaphoreType.DMA((2,)),
        ],
        compiler_params=pltpu.CompilerParams(vmem_limit_bytes=8 * MIB),
        name="edges",
    )(in_hbm(fine), in_hbm(coarse))


def prepare_kernel(
    offset_ref,
    in_hbm,
    mid_hbm,
    out_hbm,
    target_hbm,
    shift_ref,
    in_ref,
    in_turned_ref,
    mid_ref,
    mid_turned_ref,
    out_ref,
    out_turned_ref,
    target_ref,
    ends_ref,
    w_in,
    w_mid,
    w_out,
    targets,
    sems,
):
    copies = [
        pltpu.make_async_copy(source, target, sems.at[i])
        for i, (source, target) in enumerate(
            ((in_hbm, w_in), (out_hbm, w_out), (target_hbm, targets), (mid_hbm, w_mid))
        )
    ]
    for copy in copies:
        copy.start()
    shift_ref[...] = jnp.zeros((8, SC), F32)
    for i in range(2):
        shift = offset_ref[0, 0, i].astype(F32) * (1.0 / SUB)
        shift_ref[i : i + 1, :] = jnp.full((1, SC), shift, F32)
    copies[0].wait()
    in_turned_ref[...] = w_in[...].astype(BF16)
    for block in range(4):
        cols = slice(block * 128, block * 128 + 128)
        in_ref[cols, :] = w_in[:, cols].T.astype(BF16)
    copies[1].wait()
    padded = jnp.concatenate([w_out[...], jnp.zeros((13, HID), F32)], axis=0)
    out_ref[...] = padded.astype(BF16)
    for block in range(4):
        cols = slice(block * 128, block * 128 + 128)
        out_turned_ref[cols, :] = padded[:, cols].T.astype(BF16)
    copies[2].wait()
    lane = lane_ids(3)
    ends = jnp.zeros((3, SC), F32)
    target_ref[...] = jnp.zeros(target_ref.shape, F32)
    for i in range(SR):
        for kind in range(3):
            line = targets[kind, :, i, :]
            target_ref[kind, 0:3, i * SC : i * SC + SC] = line
        ends = jnp.where(lane == i, spread_lane(line, SC - 1), ends)
    ends_ref[...] = jnp.zeros((8, SC), F32)
    ends_ref[0:3, :] = ends
    copies[3].wait()
    mid_ref[...] = w_mid[...].astype(BF16)
    for i in range(4):
        for j in range(4):
            rows = slice(i * 128, i * 128 + 128)
            cols = slice(j * 128, j * 128 + 128)
            mid_turned_ref[cols, rows] = w_mid[rows, cols].T.astype(BF16)


def prepare(offsets, w_in, w_mid, w_out, targets):
    outs = (
        jax.ShapeDtypeStruct((8, SC), F32),
        jax.ShapeDtypeStruct((HID, 2 * CH), BF16),
        jax.ShapeDtypeStruct((2 * CH, HID), BF16),
        jax.ShapeDtypeStruct((HID, HID), BF16),
        jax.ShapeDtypeStruct((HID, HID), BF16),
        jax.ShapeDtypeStruct((16, HID), BF16),
        jax.ShapeDtypeStruct((HID, 16), BF16),
        jax.ShapeDtypeStruct((3, 8, SR * SC), F32),
        jax.ShapeDtypeStruct((8, SC), F32),
    )
    return pl.pallas_call(
        prepare_kernel,
        out_shape=outs,
        in_specs=[smem(), hbm(), hbm(), hbm(), hbm()],
        out_specs=(vmem(),) * len(outs),
        scratch_shapes=[pltpu.VMEM(a.shape, F32) for a in (w_in, w_mid, w_out, targets)]
        + [pltpu.SemaphoreType.DMA((4,))],
        compiler_params=pltpu.CompilerParams(vmem_limit_bytes=8 * MIB),
        name="prepare",
    )(offsets, *(in_hbm(a) for a in (w_in, w_mid, w_out, targets)))


def forward_kernel(
    shift_ref,
    fine_ref,
    coarse_ref,
    row_ref,
    col_ref,
    corner_ref,
    target_ref,
    ends_ref,
    in_ref,
    mid_ref,
    out_ref,
    feat_ref,
    pre_ref,
    pred_ref,
    row_one_ref,
    row_two_ref,
    col_one_ref,
    col_two_ref,
):
    shift_y = shift_ref[0:1, :]
    shift_x = shift_ref[1:2, :]
    lane = lane_ids(CH)
    unused_first_row, last_row, unused_first_col, last_col = at_ends()
    row_in = jnp.where(last_row, 0.0, row_ref[...])
    col_in = jnp.where(last_col, 0.0, col_ref[...])
    corner_in = jnp.where(jnp.logical_or(last_row, last_col), 0.0, corner_ref[...])

    def across(line, following):
        moved = jnp.where(lane == SC - 1, following, pltpu.roll(line, SC - 1, 1))
        return line * (1.0 - shift_x) + moved * shift_x

    stage = []
    for i in range(CR):
        stage.append(jnp.where(lane == CC, spread_lane(col_in, SR + i), coarse_ref[i]))
    stage.append(jnp.where(lane == CC, spread_lane(corner_in, SR), row_in[:, SC:]))
    bands = dot(
        jnp.concatenate(stage, axis=0), coarse_table(shift_x), precision=lax.Precision.HIGHEST
    )
    bands = [bands[i * CH : i * CH + CH] for i in range(CR + 1)]
    lane8 = lane_ids(8)
    left = jnp.zeros((8, SC), F32)
    right = ends_ref[...]
    line = across(fine_ref[0], spread_lane(col_in, 0))
    for chain in range(CHAINS):
        tiles = []
        for k in range(LINES):
            row = chain * LINES + k
            if row + 1 < SR:
                following = across(fine_ref[row + 1], spread_lane(col_in, row + 1))
            else:
                following = across(row_in[:, 0:SC], spread_lane(corner_in, 0))
            fine = line * (1.0 - shift_y) + following * shift_y
            line = following
            band = row // RATIO
            part = (row % RATIO + shift_y) * (1.0 / RATIO)
            coarse = bands[band] * (1.0 - part) + bands[band + 1] * part
            tiles.append(jnp.concatenate([fine, coarse], axis=0).astype(BF16))
        feat = jnp.concatenate(tiles, axis=1)
        cols = slice(chain * WIDTH, chain * WIDTH + WIDTH)
        feat_ref[:, cols] = feat
        pre = dot(in_ref[...], feat)
        act = (pre * sigmoid(pre)).astype(BF16)
        pre = dot(mid_ref[...], act)
        pre_ref[:, cols] = pre
        act = (pre * sigmoid(pre)).astype(BF16)
        pred = dot(out_ref[...], act)[0:8]
        pred_ref[:, cols] = pred
        for k in range(LINES):
            row = chain * LINES + k
            tile = pred[:, k * SC : k * SC + SC]
            left = jnp.where(lane8 == row, spread_lane(tile, 0), left)
            right = right + jnp.where(lane8 == row, spread_lane(tile, SC - 1), 0.0)
        if chain == 0:
            up = pred[:, 0:SC]
    down = pred[:, WIDTH - SC :] + target_ref[1, :, SR * SC - SC :]
    odd_row = axes_index(ROW) % 2 == 1
    odd_col = axes_index(COL) % 2 == 1
    row_one_ref[...] = jnp.where(odd_row, up, down)
    row_two_ref[...] = jnp.where(odd_row, down, up)
    col_one_ref[...] = jnp.where(odd_col, left, right)
    col_two_ref[...] = jnp.where(odd_col, right, left)


def forward(*args):
    edge = jax.ShapeDtypeStruct((8, SC), F32)
    outs = (
        jax.ShapeDtypeStruct((2 * CH, SR * SC), BF16),
        jax.ShapeDtypeStruct((HID, SR * SC), F32),
        jax.ShapeDtypeStruct((8, SR * SC), F32),
        edge,
        edge,
        edge,
        edge,
    )
    return pl.pallas_call(
        forward_kernel,
        out_shape=outs,
        in_specs=[vmem()] * len(args),
        out_specs=(vmem(),) * len(outs),
        compiler_params=pltpu.CompilerParams(vmem_limit_bytes=24 * MIB),
        name="forward",
    )(*args)


def loss_cotangent(pred_ref, target_ref, below, beside, above, before, cot):
    first_row, last_row, first_col, last_col = at_ends()
    lane = lane_ids(3)
    cot[...] = jnp.zeros(cot.shape, F32)
    line = pred_ref[0:3, 0:SC]
    row_prior = jnp.where(first_row, 0.0, line - above)
    for i in range(SR):
        if i + 1 < SR:
            following = pred_ref[0:3, (i + 1) * SC : (i + 2) * SC]
        else:
            following = below
        value_error = line - target_ref[0, 0:3, i * SC : i * SC + SC]
        row_error = following - line - target_ref[1, 0:3, i * SC : i * SC + SC]
        if i + 1 == SR:
            row_error = jnp.where(last_row, 0.0, row_error)
        beyond = jnp.where(lane == SC - 1, spread_lane(beside, i), pltpu.roll(line, SC - 1, 1))
        col_error = beyond - line - target_ref[2, 0:3, i * SC : i * SC + SC]
        col_error = jnp.where(jnp.logical_and(lane == SC - 1, last_col), 0.0, col_error)
        edge = jnp.where(first_col, 0.0, line - spread_lane(before, i))
        col_prior = jnp.where(lane == 0, edge, pltpu.roll(col_error, 1, 1))
        cot[0:3, i * SC : (i + 1) * SC] = (
            2.0 * LOSS_VALUE * value_error
            + 2.0 * (row_prior - row_error)
            + 2.0 * (col_prior - col_error)
        )
        line = following
        row_prior = row_error


def backward_kernel(
    shift_ref,
    feat_ref,
    pre_ref,
    pred_ref,
    row_one_ref,
    row_two_ref,
    col_one_ref,
    col_two_ref,
    target_ref,
    in_ref,
    in_turned_ref,
    mid_turned_ref,
    out_turned_ref,
    keep_ref,
    send_ref,
    fine_ref,
    coarse_ref,
    row_ref,
    col_ref,
    cot,
    grad_mid,
    grad_in,
    grad_out,
):
    shift_y = shift_ref[0:1, :]
    shift_x = shift_ref[1:2, :]
    lane = lane_ids(CH)
    odd_row = axes_index(ROW) % 2 == 1
    odd_col = axes_index(COL) % 2 == 1
    row_one, row_two = row_one_ref[0:3, :], row_two_ref[0:3, :]
    col_one, col_two = col_one_ref[0:3, :], col_two_ref[0:3, :]
    loss_cotangent(
        pred_ref,
        target_ref,
        jnp.where(odd_row, row_two, row_one),
        jnp.where(odd_col, col_two, col_one),
        jnp.where(odd_row, row_one, row_two),
        jnp.where(odd_col, col_one, col_two),
        cot,
    )

    def along(line):
        moved = jnp.where(lane == 0, 0.0, pltpu.roll(line, 1, 1))
        return line * (1.0 - shift_x) + moved * shift_x

    prior = jnp.zeros((CH, SC), F32)
    ends = jnp.zeros((CH, SC), F32)
    upper = jnp.zeros((CH, SC), F32)
    lower = jnp.zeros((CH, SC), F32)
    bands = []
    for chain in range(CHAINS):
        cols = slice(chain * WIDTH, chain * WIDTH + WIDTH)
        feat = feat_ref[:, cols]
        out_cot = cot[:, cols].astype(BF16)
        pre = pre_ref[:, cols]
        gate = sigmoid(pre)
        act = (pre * gate).astype(BF16)
        part = dot(out_cot, act, 1, 1)
        grad_out[...] = part if chain == 0 else grad_out[...] + part
        upward = dot(out_turned_ref[...], out_cot)
        delta = (upward * (gate * (1.0 + pre * (1.0 - gate)))).astype(BF16)
        pre = dot(in_ref[...], feat)
        gate = sigmoid(pre)
        act = (pre * gate).astype(BF16)
        part = dot(delta, act, 1, 1)
        grad_mid[...] = part if chain == 0 else grad_mid[...] + part
        upward = dot(mid_turned_ref[...], delta)
        delta = (upward * (gate * (1.0 + pre * (1.0 - gate)))).astype(BF16)
        part = dot(feat, delta, 1, 1)
        grad_in[...] = part if chain == 0 else grad_in[...] + part
        feat_grad = dot(in_turned_ref[...], delta)
        for k in range(LINES):
            row = chain * LINES + k
            fine = feat_grad[0:CH, k * SC : k * SC + SC]
            line = fine * (1.0 - shift_y) + prior * shift_y
            fine_ref[row] = along(line)
            ends = jnp.where(lane == row, spread_lane(line * shift_x, SC - 1), ends)
            prior = fine
            coarse = feat_grad[CH:, k * SC : k * SC + SC]
            weight = (row % RATIO + shift_y) * (1.0 / RATIO)
            upper += coarse * (1.0 - weight)
            lower += coarse * weight
            if row % RATIO == RATIO - 1:
                bands.append(upper)
                upper = lower
                lower = jnp.zeros((CH, SC), F32)
    bands.append(upper)
    line = prior * shift_y
    row_ref[:, 0:SC] = along(line)
    ends = jnp.where(lane == FINE_CORNER, spread_lane(line * shift_x, SC - 1), ends)
    spread = dot(
        jnp.concatenate(bands, axis=0),
        coarse_table(shift_x),
        1,
        1,
        precision=lax.Precision.HIGHEST,
    )
    for i in range(CR):
        band = spread[i * CH : i * CH + CH]
        coarse_ref[i] = jnp.where(lane < CC, band, 0.0)
        ends = jnp.where(lane == SR + i, spread_lane(band, CC), ends)
    band = spread[CR * CH :]
    row_ref[:, SC:] = jnp.where(lane < CC, band, 0.0)
    col_ref[...] = jnp.where(lane == COARSE_CORNER, spread_lane(band, CC), ends)
    core = lax.axis_index("c")
    tile = axes_index(("x", "y"))
    for d in range(16):
        chunk = tile ^ d
        band = chunk >> 1
        side = chunk & 1
        for half, target in ((core, keep_ref), (1 - core, send_ref)):
            cols = pl.ds(pl.multiple_of((half * 2 + side) * 128, 128), 128)
            target[d, 0:64, :] = grad_mid[pl.ds(pl.multiple_of(band * 64, 64), 64), cols]
            target[d, 64:72, :] = grad_in[pl.ds(pl.multiple_of(band * 8, 8), 8), cols]
            target[d, 72:80, :] = jnp.where(band == 0, grad_out[0:8, cols], 0.0)


def backward(*args):
    part = jax.ShapeDtypeStruct((16, 80, 128), F32)
    outs = (
        part,
        part,
        jax.ShapeDtypeStruct((SR, CH, SC), F32),
        jax.ShapeDtypeStruct((CR, CH, SC), F32),
        jax.ShapeDtypeStruct((CH, 2 * SC), F32),
        jax.ShapeDtypeStruct((CH, SC), F32),
    )
    return pl.pallas_call(
        backward_kernel,
        out_shape=outs,
        in_specs=[vmem()] * len(args),
        out_specs=(vmem(),) * len(outs),
        scratch_shapes=[
            pltpu.VMEM((16, SR * SC), F32),
            pltpu.VMEM((HID, HID), F32),
            pltpu.VMEM((2 * CH, HID), F32),
            pltpu.VMEM((16, HID), F32),
        ],
        compiler_params=pltpu.CompilerParams(vmem_limit_bytes=32 * MIB),
        name="backward",
    )(*args)


def turn_kernel(row_ref, col_ref, out_ref):
    lane = lane_ids(CH)
    unused_first_row, unused_last_row, first_col, unused_last_col = at_ends()
    cols = jnp.where(first_col, 0.0, col_ref[...])
    fine = jnp.where(lane == 0, spread_lane(cols, FINE_CORNER), 0.0)
    coarse = jnp.where(lane == 0, spread_lane(cols, COARSE_CORNER), 0.0)
    out_ref[:, 0:SC] = row_ref[:, 0:SC] + fine
    out_ref[:, SC:] = row_ref[:, SC:] + coarse


def turn(row_out, col_in):
    return pl.pallas_call(
        turn_kernel,
        out_shape=jax.ShapeDtypeStruct(row_out.shape, F32),
        in_specs=[vmem(), vmem()],
        out_specs=vmem(),
        compiler_params=pltpu.CompilerParams(vmem_limit_bytes=4 * MIB),
        name="turn",
    )(row_out, col_in)


def join_kernel(fine_ref, coarse_ref, row_ref, col_ref, fine_out, coarse_out, total_ref):
    lane = lane_ids(CH)
    first_row, unused_last_row, first_col, unused_last_col = at_ends()
    rows = jnp.where(first_row, 0.0, row_ref[...])
    cols = jnp.where(first_col, 0.0, col_ref[...])
    total = jnp.zeros((CH, SC), F32)
    for i in range(SR):
        line = fine_ref[i] + jnp.where(lane == 0, spread_lane(cols, i), 0.0)
        if i == 0:
            line += rows[:, 0:SC]
        fine_out[:, i, :] = line
        total += line * line
    for i in range(CR):
        line = coarse_ref[i] + jnp.where(lane == 0, spread_lane(cols, SR + i), 0.0)
        if i == 0:
            line += rows[:, SC:]
        coarse_out[:, i, :] = line[:, 0:CC]
        total += line * line
    total = jnp.sum(jnp.sum(total, axis=0, keepdims=True), axis=1, keepdims=True)
    total_ref[...] = jnp.broadcast_to(total, (8, SC))


def join(fine, coarse, row_in, col_in):
    return pl.pallas_call(
        join_kernel,
        out_shape=(
            jax.ShapeDtypeStruct((CH, SR, SC), F32),
            jax.ShapeDtypeStruct((CH, CR, CC), F32),
            jax.ShapeDtypeStruct((8, SC), F32),
        ),
        in_specs=[vmem()] * 4,
        out_specs=(vmem(),) * 3,
        compiler_params=pltpu.CompilerParams(vmem_limit_bytes=8 * MIB),
        name="join",
    )(fine, coarse, row_in, col_in)


def clip_factor(total, entries):
    return jnp.minimum(1.0, CLIP_RMS / jnp.sqrt(total / entries + MEAN_EPSILON))


def adam_step(gradient, moment_one, moment_two, clip_scale):
    clipped = gradient * clip_scale
    new_one = BETA_ONE * moment_one + (1.0 - BETA_ONE) * clipped
    new_two = BETA_TWO * moment_two + (1.0 - BETA_TWO) * clipped * clipped
    return (
        new_one
        * (1.0 / (1.0 - BETA_ONE**ADAM_STEP))
        / (jnp.sqrt(new_two * (1.0 / (1.0 - BETA_TWO**ADAM_STEP))) + ADAM_EPSILON)
    )


def steps_kernel(
    own_ref,
    other_ref,
    fine_ref,
    coarse_ref,
    mid_one_ref,
    mid_two_ref,
    in_one_ref,
    in_two_ref,
    out_one_ref,
    out_two_ref,
    fine_one_ref,
    fine_two_ref,
    coarse_one_ref,
    coarse_two_ref,
    mid_ref,
    in_ref,
    out_ref,
    fine_step_ref,
    coarse_step_ref,
    scales,
    *,
    decoder_entries,
    grid_entries,
):
    core = lax.axis_index("c")
    step = pl.program_id(0)

    @pl.when(step == 0)
    def _():
        own_sum = pair_sum([own_ref[d, 80:88, :] for d in range(16)])
        other_sum = pair_sum([other_ref[d, 80:88, :] for d in range(16)])
        totals = own_sum + other_sum
        scales[0:1, :] = clip_factor(totals[0:1, :], grid_entries)
        scales[1:2, :] = clip_factor(totals[1:2, :], decoder_entries)
        for block in range(4):
            d = block % 2
            data = jnp.where(block // 2 == core, own_ref[d, 72:80, :], other_ref[d, 72:80, :])
            cols = slice(block * 128, block * 128 + 128)
            out_ref[:, cols] = adam_step(
                data[0:3], out_one_ref[:, cols], out_two_ref[:, cols], scales[1:2, :]
            )

    grid_scale = scales[0:1, :]
    scale = scales[1:2, :]
    for k in range(8 // PARTS):
        for block in range(4):
            d = (step * (8 // PARTS) + k) * 2 + block % 2
            data = jnp.where(block // 2 == core, own_ref[d, 0:72, :], other_ref[d, 0:72, :])
            at = (slice(k * 64, k * 64 + 64), slice(block * 128, block * 128 + 128))
            mid_ref[at] = adam_step(data[0:64], mid_one_ref[at], mid_two_ref[at], scale)
            at = (slice(k * 8, k * 8 + 8), slice(block * 128, block * 128 + 128))
            in_ref[at] = adam_step(data[64:72], in_one_ref[at], in_two_ref[at], scale)
    fine_step_ref[...] = adam_step(
        fine_ref[...], fine_one_ref[...], fine_two_ref[...], grid_scale[:, None, :]
    )
    coarse_step_ref[...] = adam_step(
        coarse_ref[...], coarse_one_ref[...], coarse_two_ref[...], grid_scale[:, None, 0:CC]
    )


def all_steps(own, other, fine, coarse, moments, decoder_entries, grid_entries):
    mid = pl.BlockSpec((512 // PARTS, 512), lambda b: (b, 0))
    inner = pl.BlockSpec((64 // PARTS, 512), lambda b: (b, 0))
    outer = whole((3, 512))
    fine_spec = pl.BlockSpec((CH // PARTS, SR, SC), lambda b: (b, 0, 0))
    coarse_spec = pl.BlockSpec((CH // PARTS, CR, CC), lambda b: (b, 0, 0))
    shapes = ((512, 512), (64, 512), (3, 512), fine.shape, coarse.shape)
    return pl.pallas_call(
        lambda *refs: steps_kernel(
            *refs, decoder_entries=decoder_entries, grid_entries=grid_entries
        ),
        grid=(PARTS,),
        out_shape=tuple(jax.ShapeDtypeStruct(s, F32) for s in shapes),
        in_specs=[whole(own.shape), whole(other.shape), fine_spec, coarse_spec]
        + [mid, mid, inner, inner, outer, outer, fine_spec, fine_spec, coarse_spec, coarse_spec],
        out_specs=(mid, inner, outer, fine_spec, coarse_spec),
        scratch_shapes=[pltpu.VMEM((8, SC), F32)],
        compiler_params=pltpu.CompilerParams(vmem_limit_bytes=16 * MIB),
        name="steps",
    )(own, other, fine, coarse, *moments)


def tally_kernel(one_ref, two_ref, out_ref):
    total = one_ref[...] + two_ref[...]
    grads = total[0:80]
    squares = jnp.sum(grads * grads, axis=0, keepdims=True)
    squares = jnp.broadcast_to(jnp.sum(squares, axis=1, keepdims=True), (1, SC))
    out_ref[...] = total
    out_ref[81:82, :] = squares


def tally(one, two):
    return pl.pallas_call(
        tally_kernel,
        out_shape=jax.ShapeDtypeStruct(one.shape, F32),
        in_specs=[vmem(), vmem()],
        out_specs=vmem(),
        compiler_params=pltpu.CompilerParams(vmem_limit_bytes=4 * MIB),
        name="tally",
    )(one, two)


def reduce_grads(keep, send, fine, coarse, row_out, col_in):
    part = keep + swapped(send, "c", 1)
    part = scatter_sum([part[d * 4 : d * 4 + 4] for d in range(4)], "x")
    part, col_in = lax.optimization_barrier((part, col_in))
    row_in = shifted(turn(row_out, col_in), 1, 0)
    part = scatter_sum([part[d] for d in range(4)], "y")
    fine, coarse, grid_local = join(fine, coarse, row_in, col_in)
    part = exchange_sum(jnp.concatenate([part, grid_local]), "zl")
    across = [(i, i ^ 5) for i in range(axes_size(("zl", "zh")))]
    part = tally(part, lax.ppermute(part, ("zl", "zh"), across))
    own = all_to_all(jnp.broadcast_to(part, (16, *part.shape)))
    return own, swapped(own, "c", 1), fine, coarse


def local_grads(offsets, targets, grid_fine, grid_coarse, weight_in, weight_mid, weight_out):
    row_out, col_out, fine_lines, coarse_lines = edges(grid_fine, grid_coarse)
    corner_in = shifted(col_out, -1, -1)
    col_in = shifted(col_out, 0, -1)
    row_in = shifted(row_out, -1, 0)
    shifts, low_in, in_turned, low_mid, mid_turned, low_out, out_turned, lines, ends = prepare(
        offsets, weight_in.T, weight_mid[0], weight_out, targets
    )
    feat, pre, pred, row_one, row_two, col_one, col_two = forward(
        shifts, fine_lines, coarse_lines, row_in, col_in, corner_in, lines, ends, low_in, low_mid, low_out
    )
    cols = meetings(col_one, col_two, COL)
    halos = (*meetings(row_one, row_two, ROW), *cols)
    keep, send, fine, coarse, row_out, col_out = backward(
        shifts, feat, pre, pred, *halos, lines, low_in, in_turned, mid_turned, out_turned
    )
    return keep, send, fine, coarse, row_out, shifted(col_out, 0, 1)


def shards(
    offsets,
    targets,
    grid_fine,
    grid_coarse,
    weight_in,
    weight_mid,
    weight_out,
    fine_first,
    fine_second,
    coarse_first,
    coarse_second,
    in_first,
    in_second,
    mid_first,
    mid_second,
    out_first,
    out_second,
):
    keep, send, fine, coarse, row_out, col_in = local_grads(
        offsets, targets, grid_fine, grid_coarse, weight_in, weight_mid, weight_out
    )
    own, other, fine_grad, coarse_grad = reduce_grads(keep, send, fine, coarse, row_out, col_in)
    devices = axes_size(ROW) * axes_size(COL)
    grid_entries = (fine_grad.size + coarse_grad.size) * devices
    decoder_entries = weight_in.size + weight_mid.size + weight_out.size
    middle_step, input_step, output_step, fine_step, coarse_step = all_steps(
        own,
        other,
        fine_grad,
        coarse_grad,
        (
            mid_first[0],
            mid_second[0],
            in_first.T,
            in_second.T,
            out_first,
            out_second,
            fine_first,
            fine_second,
            coarse_first,
            coarse_second,
        ),
        decoder_entries,
        grid_entries,
    )
    return (fine_step, coarse_step, input_step.T, middle_step[None], output_step)


def solution(mesh):
    sizes = {"zl": 4, "x": 4, "y": 4, "zh": 2, "c": 2}
    mesh = Mesh(mesh.devices.reshape(tuple(sizes.values())), tuple(sizes))
    placed = (
        P(ROW, COL, None),
        P(None, None, ROW, COL),
        P(None, ROW, COL),
        P(None, ROW, COL),
        P(),
        P(),
        P(),
        P(None, ROW, COL),
        P(None, ROW, COL),
        P(None, ROW, COL),
        P(None, ROW, COL),
        P(),
        P(),
        P(),
        P(),
        P(),
        P(),
    )
    return jax.shard_map(
        shards,
        mesh=mesh,
        in_specs=placed,
        out_specs=(P(None, ROW, COL), P(None, ROW, COL), P(), P(), P()),
        check_vma=False,
    )
```

```python
import jax
import jax.numpy as jnp
from jax import lax
from jax.experimental import pallas as pl
from jax.experimental.pallas import tpu as pltpu
from jax.sharding import Mesh
from jax.sharding import PartitionSpec as P

SUB = 4
RATIO = 4
ADAM_STEP = 10

BETA_ONE = 0.9
BETA_TWO = 0.99
ADAM_EPSILON = 1e-08
CLIP_RMS = 0.01
LOSS_VALUE = 0.25
MEAN_EPSILON = 1e-06

ROW = ("zl", "x")
COL = ("y", "zh", "c")
SR = 32
SC = 128
CH = 32
CR = 8
CC = 32
HID = 512
CHAINS = 4
WIDTH = SR * SC // CHAINS
LINES = SR // CHAINS
PARTS = 2
FINE_CORNER = 64
COARSE_CORNER = 65
F32 = jnp.float32
BF16 = jnp.bfloat16
MIB = 1 << 20


def axes_size(axes):
    total = 1
    for axis in axes:
        total *= lax.axis_size(axis)
    return total


def axes_index(axes):
    index = 0
    for axis in axes:
        index = index * lax.axis_size(axis) + lax.axis_index(axis)
    return index


def shifted(block, down, right):
    rows, cols = axes_size(ROW), axes_size(COL)
    if not right:
        return lax.ppermute(block, ROW, [(i, (i + down) % rows) for i in range(rows)])
    if not down:
        return lax.ppermute(block, COL, [(i, (i + right) % cols) for i in range(cols)])
    route = [
        (r * cols + c, (r + down) % rows * cols + (c + right) % cols)
        for r in range(rows)
        for c in range(cols)
    ]
    return lax.ppermute(block, ROW + COL, route)


def meetings(block_one, block_two, axes):
    size = axes_size(axes)
    one = [(i, i ^ 1) for i in range(size)]
    two = [(i, (i + 1 if i % 2 else i - 1) % size) for i in range(size)]
    block_two = lax.ppermute(block_two, axes, two)
    return lax.ppermute(block_one, axes, one), block_two


def at_ends():
    row, col = axes_index(ROW), axes_index(COL)
    return row == 0, row == axes_size(ROW) - 1, col == 0, col == axes_size(COL) - 1


def swapped(block, axis, mask):
    size = lax.axis_size(axis)
    return lax.ppermute(block, axis, [(i, i ^ mask) for i in range(size)])


def pair_sum(values):
    values = list(values)
    while len(values) > 1:
        values = [values[i] + values[i + 1] for i in range(0, len(values), 2)]
    return values[0]


def exchange_sum(block, axis):
    return pair_sum([block] + [swapped(block, axis, d) for d in range(1, lax.axis_size(axis))])


def all_to_all(blocks):
    return lax.all_to_all(blocks, ("x", "y"), 0, 0, tiled=True)


def scatter_sum(blocks, axis):
    return pair_sum([blocks[0]] + [swapped(blocks[d], axis, d) for d in range(1, len(blocks))])


def vmem():
    return pl.BlockSpec(memory_space=pltpu.VMEM)


def smem():
    return pl.BlockSpec(memory_space=pltpu.SMEM)


def hbm():
    return pl.BlockSpec(memory_space=pltpu.HBM)


def in_hbm(array):
    return pltpu.with_memory_space_constraint(array, pltpu.HBM)


def whole(shape, memory_space=pltpu.VMEM):
    return pl.BlockSpec(shape, lambda b: (0,) * len(shape), memory_space=memory_space)


def lane_ids(rows):
    return lax.broadcasted_iota(jnp.int32, (rows, SC), 1)


def spread_lane(block, lane):
    return jnp.broadcast_to(block[:, lane : lane + 1], (block.shape[0], SC))


def dot(former, latter, former_dim=1, latter_dim=0, precision=None):
    return lax.dot_general(
        former,
        latter,
        (((former_dim,), (latter_dim,)), ((), ())),
        precision=precision,
        preferred_element_type=F32,
    )


def sigmoid(value):
    return 0.5 * jnp.tanh(0.5 * value) + 0.5


def coarse_table(shift_x):
    line = lax.broadcasted_iota(jnp.int32, (SC, SC), 0)
    sample = lax.broadcasted_iota(jnp.int32, (SC, SC), 1)
    base = sample >> 2
    fraction = ((sample & 3).astype(F32) + shift_x) * (1.0 / RATIO)
    return jnp.where(line == base, 1.0 - fraction, 0.0) + jnp.where(line == base + 1, fraction, 0.0)


def edges_kernel(fine_hbm, coarse_hbm, row_ref, col_ref, fine_ref, coarse_ref, fine, coarse, sems):
    copies = [
        pltpu.make_async_copy(fine_hbm, fine, sems.at[0]),
        pltpu.make_async_copy(coarse_hbm, coarse, sems.at[1]),
    ]
    for copy in copies:
        copy.start()
    for copy in copies:
        copy.wait()
    lane = lane_ids(CH)
    row_ref[:, 0:SC] = fine[:, 0, :]
    row_ref[:, SC:] = jnp.zeros((CH, SC), F32)
    row_ref[:, SC : SC + CC] = coarse[:, 0, :]
    coarse_ref[...] = jnp.zeros(coarse_ref.shape, F32)
    cols = jnp.zeros((CH, SC), F32)
    for i in range(SR):
        line = fine[:, i, :]
        fine_ref[i] = line
        cols = jnp.where(lane == i, spread_lane(line, 0), cols)
    for i in range(CR):
        line = coarse[:, i, :]
        coarse_ref[i, :, 0:CC] = line
        cols = jnp.where(lane == SR + i, spread_lane(line, 0), cols)
    col_ref[...] = cols


def edges(fine, coarse):
    shapes = ((CH, 2 * SC), (CH, SC), (SR, CH, SC), (CR, CH, SC))
    return pl.pallas_call(
        edges_kernel,
        out_shape=tuple(jax.ShapeDtypeStruct(d, F32) for d in shapes),
        in_specs=[hbm(), hbm()],
        out_specs=(vmem(),) * 4,
        scratch_shapes=[
            pltpu.VMEM(fine.shape, F32),
            pltpu.VMEM(coarse.shape, F32),
            pltpu.SemaphoreType.DMA((2,)),
        ],
        compiler_params=pltpu.CompilerParams(vmem_limit_bytes=8 * MIB),
        name="edges",
    )(in_hbm(fine), in_hbm(coarse))


def prepare_kernel(
    offset_hbm,
    in_hbm,
    mid_hbm,
    out_hbm,
    target_hbm,
    shift_ref,
    in_ref,
    mid_ref,
    out_ref,
    floor_ref,
    ends_ref,
    w_in,
    w_mid,
    w_out,
    targets,
    offsets,
    sems,
):
    sources = (target_hbm, in_hbm, out_hbm, offset_hbm, mid_hbm)
    copies = [
        pltpu.make_async_copy(source, target, sems.at[i])
        for i, (source, target) in enumerate(zip(sources, (targets, w_in, w_out, offsets, w_mid)))
    ]
    for copy in copies:
        copy.start()
    copies[0].wait()
    lane = lane_ids(3)
    ends = jnp.zeros((3, SC), F32)
    for i in range(SR):
        ends = jnp.where(lane == i, spread_lane(targets[2, :, i, :], SC - 1), ends)
    ends_ref[...] = jnp.zeros((8, SC), F32)
    ends_ref[0:3, :] = ends
    floor_ref[...] = jnp.zeros((8, SC), F32)
    floor_ref[0:3, :] = targets[1, :, SR - 1, :]
    copies[1].wait()
    for block in range(4):
        cols = slice(block * 128, block * 128 + 128)
        in_ref[cols, :] = w_in[:, cols].T.astype(BF16)
    copies[2].wait()
    padded = jnp.concatenate([w_out[...], jnp.zeros((13, HID), F32)], axis=0)
    out_ref[...] = padded.astype(BF16)
    copies[3].wait()
    shift_ref[...] = jnp.zeros((8, SC), F32)
    for i in range(2):
        shift = offsets[0, 0, i].astype(F32) * (1.0 / SUB)
        shift_ref[i : i + 1, :] = jnp.full((1, SC), shift, F32)
    copies[4].wait()
    mid_ref[...] = w_mid[...].astype(BF16)


def prepare(offsets, w_in, w_mid, w_out, targets):
    outs = (
        jax.ShapeDtypeStruct((8, SC), F32),
        jax.ShapeDtypeStruct((HID, 2 * CH), BF16),
        jax.ShapeDtypeStruct((HID, HID), BF16),
        jax.ShapeDtypeStruct((16, HID), BF16),
        jax.ShapeDtypeStruct((8, SC), F32),
        jax.ShapeDtypeStruct((8, SC), F32),
    )
    return pl.pallas_call(
        prepare_kernel,
        out_shape=outs,
        in_specs=[hbm()] * 5,
        out_specs=(vmem(),) * len(outs),
        scratch_shapes=[pltpu.VMEM(a.shape, F32) for a in (w_in, w_mid, w_out, targets)]
        + [pltpu.SMEM(offsets.shape, jnp.int32), pltpu.SemaphoreType.DMA((5,))],
        compiler_params=pltpu.CompilerParams(vmem_limit_bytes=8 * MIB),
        name="prepare",
    )(*(in_hbm(a) for a in (offsets, w_in, w_mid, w_out, targets)))


def turned_kernel(
    in_hbm,
    mid_hbm,
    out_hbm,
    target_hbm,
    unused_pred_ref,
    in_turned_ref,
    mid_turned_ref,
    out_turned_ref,
    target_ref,
    w_in,
    w_mid,
    w_out,
    targets,
    sems,
):
    sources = (target_hbm, in_hbm, out_hbm, mid_hbm)
    copies = [
        pltpu.make_async_copy(source, target, sems.at[i])
        for i, (source, target) in enumerate(zip(sources, (targets, w_in, w_out, w_mid)))
    ]
    for copy in copies:
        copy.start()
    target_ref[...] = jnp.zeros(target_ref.shape, F32)
    copies[0].wait()
    for i in range(SR):
        for kind in range(3):
            target_ref[kind, 0:3, i * SC : i * SC + SC] = targets[kind, :, i, :]
    copies[1].wait()
    in_turned_ref[...] = w_in[...].astype(BF16)
    copies[2].wait()
    padded = jnp.concatenate([w_out[...], jnp.zeros((13, HID), F32)], axis=0)
    for block in range(4):
        cols = slice(block * 128, block * 128 + 128)
        out_turned_ref[cols, :] = padded[:, cols].T.astype(BF16)
    copies[3].wait()
    for i in range(4):
        for j in range(4):
            rows = slice(i * 128, i * 128 + 128)
            cols = slice(j * 128, j * 128 + 128)
            mid_turned_ref[cols, rows] = w_mid[rows, cols].T.astype(BF16)


def turned(w_in, w_mid, w_out, targets, pred):
    outs = (
        jax.ShapeDtypeStruct((2 * CH, HID), BF16),
        jax.ShapeDtypeStruct((HID, HID), BF16),
        jax.ShapeDtypeStruct((HID, 16), BF16),
        jax.ShapeDtypeStruct((3, 8, SR * SC), F32),
    )
    return pl.pallas_call(
        turned_kernel,
        out_shape=outs,
        in_specs=[hbm()] * 4 + [vmem()],
        out_specs=(vmem(),) * len(outs),
        scratch_shapes=[pltpu.VMEM(a.shape, F32) for a in (w_in, w_mid, w_out, targets)]
        + [pltpu.SemaphoreType.DMA((4,))],
        compiler_params=pltpu.CompilerParams(vmem_limit_bytes=8 * MIB),
        name="turned",
    )(*(in_hbm(a) for a in (w_in, w_mid, w_out, targets)), pred)


def forward_kernel(
    shift_ref,
    fine_ref,
    coarse_ref,
    row_ref,
    col_ref,
    corner_ref,
    floor_ref,
    ends_ref,
    in_ref,
    mid_ref,
    out_ref,
    feat_ref,
    pre_ref,
    pred_ref,
    row_one_ref,
    row_two_ref,
    col_two_ref,
    col_one_ref,
):
    shift_y = shift_ref[0:1, :]
    shift_x = shift_ref[1:2, :]
    lane = lane_ids(CH)
    unused_first_row, last_row, unused_first_col, last_col = at_ends()
    row_in = jnp.where(last_row, 0.0, row_ref[...])
    col_in = jnp.where(last_col, 0.0, col_ref[...])
    corner_in = jnp.where(jnp.logical_or(last_row, last_col), 0.0, corner_ref[...])

    def across(line, following):
        moved = jnp.where(lane == SC - 1, following, pltpu.roll(line, SC - 1, 1))
        return line * (1.0 - shift_x) + moved * shift_x

    stage = []
    for i in range(CR):
        stage.append(jnp.where(lane == CC, spread_lane(col_in, SR + i), coarse_ref[i]))
    stage.append(jnp.where(lane == CC, spread_lane(corner_in, SR), row_in[:, SC:]))
    bands = dot(
        jnp.concatenate(stage, axis=0), coarse_table(shift_x), precision=lax.Precision.HIGHEST
    )
    bands = [bands[i * CH : i * CH + CH] for i in range(CR + 1)]
    lane8 = lane_ids(8)
    left = jnp.zeros((8, SC), F32)
    right = ends_ref[...]
    line = across(fine_ref[0], spread_lane(col_in, 0))
    for chain in range(CHAINS):
        tiles = []
        for k in range(LINES):
            row = chain * LINES + k
            if row + 1 < SR:
                following = across(fine_ref[row + 1], spread_lane(col_in, row + 1))
            else:
                following = across(row_in[:, 0:SC], spread_lane(corner_in, 0))
            fine = line * (1.0 - shift_y) + following * shift_y
            line = following
            band = row // RATIO
            part = (row % RATIO + shift_y) * (1.0 / RATIO)
            coarse = bands[band] * (1.0 - part) + bands[band + 1] * part
            tiles.append(jnp.concatenate([fine, coarse], axis=0).astype(BF16))
        feat = jnp.concatenate(tiles, axis=1)
        cols = slice(chain * WIDTH, chain * WIDTH + WIDTH)
        feat_ref[:, cols] = feat
        pre = dot(in_ref[...], feat)
        act = (pre * sigmoid(pre)).astype(BF16)
        pre = dot(mid_ref[...], act)
        pre_ref[:, cols] = pre
        act = (pre * sigmoid(pre)).astype(BF16)
        pred = dot(out_ref[...], act)[0:8]
        pred_ref[:, cols] = pred
        for k in range(LINES):
            row = chain * LINES + k
            tile = pred[:, k * SC : k * SC + SC]
            left = jnp.where(lane8 == row, spread_lane(tile, 0), left)
            right = right + jnp.where(lane8 == row, spread_lane(tile, SC - 1), 0.0)
        if chain == 0:
            up = pred[:, 0:SC]
    down = pred[:, WIDTH - SC :] + floor_ref[...]
    odd_row = axes_index(ROW) % 2 == 1
    odd_col = axes_index(COL) % 2 == 1
    row_one_ref[...] = jnp.where(odd_row, up, down)
    row_two_ref[...] = jnp.where(odd_row, down, up)
    col_one_ref[...] = jnp.where(odd_col, left, right)
    col_two_ref[...] = jnp.where(odd_col, right, left)


def forward(*args):
    edge = jax.ShapeDtypeStruct((8, SC), F32)
    outs = (
        jax.ShapeDtypeStruct((2 * CH, SR * SC), BF16),
        jax.ShapeDtypeStruct((HID, SR * SC), F32),
        jax.ShapeDtypeStruct((8, SR * SC), F32),
        edge,
        edge,
        edge,
        edge,
    )
    return pl.pallas_call(
        forward_kernel,
        out_shape=outs,
        in_specs=[vmem()] * len(args),
        out_specs=(vmem(),) * len(outs),
        compiler_params=pltpu.CompilerParams(vmem_limit_bytes=24 * MIB),
        name="forward",
    )(*args)


def loss_cotangent(pred_ref, target_ref, below, beside, above, before, cot):
    first_row, last_row, first_col, last_col = at_ends()
    lane = lane_ids(3)
    cot[...] = jnp.zeros(cot.shape, F32)
    line = pred_ref[0:3, 0:SC]
    row_prior = jnp.where(first_row, 0.0, line - above)
    for i in range(SR):
        if i + 1 < SR:
            following = pred_ref[0:3, (i + 1) * SC : (i + 2) * SC]
        else:
            following = below
        value_error = line - target_ref[0, 0:3, i * SC : i * SC + SC]
        row_error = following - line - target_ref[1, 0:3, i * SC : i * SC + SC]
        if i + 1 == SR:
            row_error = jnp.where(last_row, 0.0, row_error)
        beyond = jnp.where(lane == SC - 1, spread_lane(beside, i), pltpu.roll(line, SC - 1, 1))
        col_error = beyond - line - target_ref[2, 0:3, i * SC : i * SC + SC]
        col_error = jnp.where(jnp.logical_and(lane == SC - 1, last_col), 0.0, col_error)
        edge = jnp.where(first_col, 0.0, line - spread_lane(before, i))
        col_prior = jnp.where(lane == 0, edge, pltpu.roll(col_error, 1, 1))
        cot[0:3, i * SC : (i + 1) * SC] = (
            2.0 * LOSS_VALUE * value_error
            + 2.0 * (row_prior - row_error)
            + 2.0 * (col_prior - col_error)
        )
        line = following
        row_prior = row_error


def backward_kernel(
    shift_ref,
    feat_ref,
    pre_ref,
    pred_ref,
    row_one_ref,
    row_two_ref,
    col_two_ref,
    col_one_ref,
    target_ref,
    in_ref,
    in_turned_ref,
    mid_turned_ref,
    out_turned_ref,
    keep_ref,
    send_ref,
    fine_ref,
    coarse_ref,
    row_ref,
    col_ref,
    cot,
    grad_mid,
    grad_in,
    grad_out,
):
    shift_y = shift_ref[0:1, :]
    shift_x = shift_ref[1:2, :]
    lane = lane_ids(CH)
    odd_row = axes_index(ROW) % 2 == 1
    odd_col = axes_index(COL) % 2 == 1
    row_one, row_two = row_one_ref[0:3, :], row_two_ref[0:3, :]
    col_one, col_two = col_one_ref[0:3, :], col_two_ref[0:3, :]
    loss_cotangent(
        pred_ref,
        target_ref,
        jnp.where(odd_row, row_two, row_one),
        jnp.where(odd_col, col_two, col_one),
        jnp.where(odd_row, row_one, row_two),
        jnp.where(odd_col, col_one, col_two),
        cot,
    )

    def along(line):
        moved = jnp.where(lane == 0, 0.0, pltpu.roll(line, 1, 1))
        return line * (1.0 - shift_x) + moved * shift_x

    prior = jnp.zeros((CH, SC), F32)
    ends = jnp.zeros((CH, SC), F32)
    upper = jnp.zeros((CH, SC), F32)
    lower = jnp.zeros((CH, SC), F32)
    bands = []
    for chain in range(CHAINS):
        cols = slice(chain * WIDTH, chain * WIDTH + WIDTH)
        feat = feat_ref[:, cols]
        out_cot = cot[:, cols].astype(BF16)
        pre = pre_ref[:, cols]
        gate = sigmoid(pre)
        act = (pre * gate).astype(BF16)
        part = dot(out_cot, act, 1, 1)
        grad_out[...] = part if chain == 0 else grad_out[...] + part
        upward = dot(out_turned_ref[...], out_cot)
        delta = (upward * (gate * (1.0 + pre * (1.0 - gate)))).astype(BF16)
        pre = dot(in_ref[...], feat)
        gate = sigmoid(pre)
        act = (pre * gate).astype(BF16)
        part = dot(delta, act, 1, 1)
        grad_mid[...] = part if chain == 0 else grad_mid[...] + part
        upward = dot(mid_turned_ref[...], delta)
        delta = (upward * (gate * (1.0 + pre * (1.0 - gate)))).astype(BF16)
        part = dot(feat, delta, 1, 1)
        grad_in[...] = part if chain == 0 else grad_in[...] + part
        feat_grad = dot(in_turned_ref[...], delta)
        for k in range(LINES):
            row = chain * LINES + k
            fine = feat_grad[0:CH, k * SC : k * SC + SC]
            line = fine * (1.0 - shift_y) + prior * shift_y
            fine_ref[row] = along(line)
            ends = jnp.where(lane == row, spread_lane(line * shift_x, SC - 1), ends)
            prior = fine
            coarse = feat_grad[CH:, k * SC : k * SC + SC]
            weight = (row % RATIO + shift_y) * (1.0 / RATIO)
            upper += coarse * (1.0 - weight)
            lower += coarse * weight
            if row % RATIO == RATIO - 1:
                bands.append(upper)
                upper = lower
                lower = jnp.zeros((CH, SC), F32)
    bands.append(upper)
    line = prior * shift_y
    row_ref[:, 0:SC] = along(line)
    ends = jnp.where(lane == FINE_CORNER, spread_lane(line * shift_x, SC - 1), ends)
    spread = dot(
        jnp.concatenate(bands, axis=0),
        coarse_table(shift_x),
        1,
        1,
        precision=lax.Precision.HIGHEST,
    )
    for i in range(CR):
        band = spread[i * CH : i * CH + CH]
        coarse_ref[i] = jnp.where(lane < CC, band, 0.0)
        ends = jnp.where(lane == SR + i, spread_lane(band, CC), ends)
    band = spread[CR * CH :]
    row_ref[:, SC:] = jnp.where(lane < CC, band, 0.0)
    col_ref[...] = jnp.where(lane == COARSE_CORNER, spread_lane(band, CC), ends)
    core = lax.axis_index("c")
    tile = axes_index(("x", "y"))
    for d in range(16):
        chunk = tile ^ d
        band = chunk >> 1
        side = chunk & 1
        for half, target in ((core, keep_ref), (1 - core, send_ref)):
            cols = pl.ds(pl.multiple_of((half * 2 + side) * 128, 128), 128)
            target[d, 0:64, :] = grad_mid[pl.ds(pl.multiple_of(band * 64, 64), 64), cols]
            target[d, 64:72, :] = grad_in[pl.ds(pl.multiple_of(band * 8, 8), 8), cols]
            target[d, 72:80, :] = jnp.where(band == 0, grad_out[0:8, cols], 0.0)


def backward(*args):
    part = jax.ShapeDtypeStruct((16, 80, 128), F32)
    outs = (
        part,
        part,
        jax.ShapeDtypeStruct((SR, CH, SC), F32),
        jax.ShapeDtypeStruct((CR, CH, SC), F32),
        jax.ShapeDtypeStruct((CH, 2 * SC), F32),
        jax.ShapeDtypeStruct((CH, SC), F32),
    )
    return pl.pallas_call(
        backward_kernel,
        out_shape=outs,
        in_specs=[vmem()] * len(args),
        out_specs=(vmem(),) * len(outs),
        scratch_shapes=[
            pltpu.VMEM((16, SR * SC), F32),
            pltpu.VMEM((HID, HID), F32),
            pltpu.VMEM((2 * CH, HID), F32),
            pltpu.VMEM((16, HID), F32),
        ],
        compiler_params=pltpu.CompilerParams(vmem_limit_bytes=32 * MIB),
        name="backward",
    )(*args)


def turn_kernel(row_ref, col_ref, out_ref):
    lane = lane_ids(CH)
    unused_first_row, unused_last_row, first_col, unused_last_col = at_ends()
    cols = jnp.where(first_col, 0.0, col_ref[...])
    fine = jnp.where(lane == 0, spread_lane(cols, FINE_CORNER), 0.0)
    coarse = jnp.where(lane == 0, spread_lane(cols, COARSE_CORNER), 0.0)
    out_ref[:, 0:SC] = row_ref[:, 0:SC] + fine
    out_ref[:, SC:] = row_ref[:, SC:] + coarse


def turn(row_out, col_in):
    return pl.pallas_call(
        turn_kernel,
        out_shape=jax.ShapeDtypeStruct(row_out.shape, F32),
        in_specs=[vmem(), vmem()],
        out_specs=vmem(),
        compiler_params=pltpu.CompilerParams(vmem_limit_bytes=4 * MIB),
        name="turn",
    )(row_out, col_in)


def join_kernel(fine_ref, coarse_ref, row_ref, col_ref, fine_out, coarse_out, total_ref):
    lane = lane_ids(CH)
    first_row, unused_last_row, first_col, unused_last_col = at_ends()
    rows = jnp.where(first_row, 0.0, row_ref[...])
    cols = jnp.where(first_col, 0.0, col_ref[...])
    total = jnp.zeros((CH, SC), F32)
    for i in range(SR):
        line = fine_ref[i] + jnp.where(lane == 0, spread_lane(cols, i), 0.0)
        if i == 0:
            line += rows[:, 0:SC]
        fine_out[:, i, :] = line
        total += line * line
    for i in range(CR):
        line = coarse_ref[i] + jnp.where(lane == 0, spread_lane(cols, SR + i), 0.0)
        if i == 0:
            line += rows[:, SC:]
        coarse_out[:, i, :] = line[:, 0:CC]
        total += line * line
    total = jnp.sum(jnp.sum(total, axis=0, keepdims=True), axis=1, keepdims=True)
    total_ref[...] = jnp.broadcast_to(total, (8, SC))


def join(fine, coarse, row_in, col_in):
    return pl.pallas_call(
        join_kernel,
        out_shape=(
            jax.ShapeDtypeStruct((CH, SR, SC), F32),
            jax.ShapeDtypeStruct((CH, CR, CC), F32),
            jax.ShapeDtypeStruct((8, SC), F32),
        ),
        in_specs=[vmem()] * 4,
        out_specs=(vmem(),) * 3,
        compiler_params=pltpu.CompilerParams(vmem_limit_bytes=8 * MIB),
        name="join",
    )(fine, coarse, row_in, col_in)


def clip_factor(total, entries):
    return jnp.minimum(1.0, CLIP_RMS / jnp.sqrt(total / entries + MEAN_EPSILON))


def adam_step(gradient, moment_one, moment_two, clip_scale):
    clipped = gradient * clip_scale
    new_one = BETA_ONE * moment_one + (1.0 - BETA_ONE) * clipped
    new_two = BETA_TWO * moment_two + (1.0 - BETA_TWO) * clipped * clipped
    return (
        new_one
        * (1.0 / (1.0 - BETA_ONE**ADAM_STEP))
        / (jnp.sqrt(new_two * (1.0 / (1.0 - BETA_TWO**ADAM_STEP))) + ADAM_EPSILON)
    )


def steps_kernel(
    own_ref,
    other_ref,
    fine_ref,
    coarse_ref,
    mid_one_ref,
    mid_two_ref,
    in_one_ref,
    in_two_ref,
    out_one_ref,
    out_two_ref,
    fine_one_ref,
    fine_two_ref,
    coarse_one_ref,
    coarse_two_ref,
    mid_ref,
    in_ref,
    out_ref,
    fine_step_ref,
    coarse_step_ref,
    scales,
    *,
    decoder_entries,
    grid_entries,
):
    core = lax.axis_index("c")
    step = pl.program_id(0)

    @pl.when(step == 0)
    def _():
        own_sum = pair_sum([own_ref[d, 80:88, :] for d in range(16)])
        other_sum = pair_sum([other_ref[d, 80:88, :] for d in range(16)])
        totals = own_sum + other_sum
        scales[0:1, :] = clip_factor(totals[0:1, :], grid_entries)
        scales[1:2, :] = clip_factor(totals[1:2, :], decoder_entries)
        for block in range(4):
            d = block % 2
            data = jnp.where(block // 2 == core, own_ref[d, 72:80, :], other_ref[d, 72:80, :])
            cols = slice(block * 128, block * 128 + 128)
            out_ref[:, cols] = adam_step(
                data[0:3], out_one_ref[:, cols], out_two_ref[:, cols], scales[1:2, :]
            )

    grid_scale = scales[0:1, :]
    scale = scales[1:2, :]
    for k in range(8 // PARTS):
        for block in range(4):
            d = (step * (8 // PARTS) + k) * 2 + block % 2
            data = jnp.where(block // 2 == core, own_ref[d, 0:72, :], other_ref[d, 0:72, :])
            at = (slice(k * 64, k * 64 + 64), slice(block * 128, block * 128 + 128))
            mid_ref[at] = adam_step(data[0:64], mid_one_ref[at], mid_two_ref[at], scale)
            at = (slice(k * 8, k * 8 + 8), slice(block * 128, block * 128 + 128))
            in_ref[at] = adam_step(data[64:72], in_one_ref[at], in_two_ref[at], scale)
    fine_step_ref[...] = adam_step(
        fine_ref[...], fine_one_ref[...], fine_two_ref[...], grid_scale[:, None, :]
    )
    coarse_step_ref[...] = adam_step(
        coarse_ref[...], coarse_one_ref[...], coarse_two_ref[...], grid_scale[:, None, 0:CC]
    )


def all_steps(own, other, fine, coarse, moments, decoder_entries, grid_entries):
    mid = pl.BlockSpec((512 // PARTS, 512), lambda b: (b, 0))
    inner = pl.BlockSpec((64 // PARTS, 512), lambda b: (b, 0))
    outer = whole((3, 512))
    fine_spec = pl.BlockSpec((CH // PARTS, SR, SC), lambda b: (b, 0, 0))
    coarse_spec = pl.BlockSpec((CH // PARTS, CR, CC), lambda b: (b, 0, 0))
    shapes = ((512, 512), (64, 512), (3, 512), fine.shape, coarse.shape)
    return pl.pallas_call(
        lambda *refs: steps_kernel(
            *refs, decoder_entries=decoder_entries, grid_entries=grid_entries
        ),
        grid=(PARTS,),
        out_shape=tuple(jax.ShapeDtypeStruct(s, F32) for s in shapes),
        in_specs=[whole(own.shape), whole(other.shape), fine_spec, coarse_spec]
        + [mid, mid, inner, inner, outer, outer, fine_spec, fine_spec, coarse_spec, coarse_spec],
        out_specs=(mid, inner, outer, fine_spec, coarse_spec),
        scratch_shapes=[pltpu.VMEM((8, SC), F32)],
        compiler_params=pltpu.CompilerParams(vmem_limit_bytes=16 * MIB),
        name="steps",
    )(own, other, fine, coarse, *moments)


def tally_kernel(one_ref, two_ref, out_ref):
    total = one_ref[...] + two_ref[...]
    grads = total[0:80]
    squares = jnp.sum(grads * grads, axis=0, keepdims=True)
    squares = jnp.broadcast_to(jnp.sum(squares, axis=1, keepdims=True), (1, SC))
    out_ref[...] = total
    out_ref[81:82, :] = squares


def tally(one, two):
    return pl.pallas_call(
        tally_kernel,
        out_shape=jax.ShapeDtypeStruct(one.shape, F32),
        in_specs=[vmem(), vmem()],
        out_specs=vmem(),
        compiler_params=pltpu.CompilerParams(vmem_limit_bytes=4 * MIB),
        name="tally",
    )(one, two)


def reduce_grads(keep, send, fine, coarse, row_out, col_in):
    part = keep + swapped(send, "c", 1)
    part = scatter_sum([part[d * 4 : d * 4 + 4] for d in range(4)], "x")
    part, col_in = lax.optimization_barrier((part, col_in))
    row_in = shifted(turn(row_out, col_in), 1, 0)
    part = scatter_sum([part[d] for d in range(4)], "y")
    fine, coarse, grid_local = join(fine, coarse, row_in, col_in)
    part = exchange_sum(jnp.concatenate([part, grid_local]), "zl")
    across = [(i, i ^ 5) for i in range(axes_size(("zl", "zh")))]
    part = tally(part, lax.ppermute(part, ("zl", "zh"), across))
    own = all_to_all(jnp.broadcast_to(part, (16, *part.shape)))
    return own, swapped(own, "c", 1), fine, coarse


def local_grads(offsets, targets, grid_fine, grid_coarse, weight_in, weight_mid, weight_out):
    row_out, col_out, fine_lines, coarse_lines = edges(grid_fine, grid_coarse)
    corner_in = shifted(col_out, -1, -1)
    col_in = shifted(col_out, 0, -1)
    row_in = shifted(row_out, -1, 0)
    shifts, low_in, low_mid, low_out, floor, ends = prepare(
        offsets, weight_in.T, weight_mid[0], weight_out, targets
    )
    feat, pre, pred, row_one, row_two, col_two, col_one = forward(
        shifts, fine_lines, coarse_lines, row_in, col_in, corner_in, floor, ends, low_in, low_mid, low_out
    )
    late = turned(weight_in.T, weight_mid[0], weight_out, targets, pred)
    in_turned, mid_turned, out_turned, lines = late
    col_one, col_two = meetings(col_one, col_two, COL)
    halos = (*meetings(row_one, row_two, ROW), col_two, col_one)
    keep, send, fine, coarse, row_out, col_out = backward(
        shifts, feat, pre, pred, *halos, lines, low_in, in_turned, mid_turned, out_turned
    )
    return keep, send, fine, coarse, row_out, shifted(col_out, 0, 1)


def shards(
    offsets,
    targets,
    grid_fine,
    grid_coarse,
    weight_in,
    weight_mid,
    weight_out,
    fine_first,
    fine_second,
    coarse_first,
    coarse_second,
    in_first,
    in_second,
    mid_first,
    mid_second,
    out_first,
    out_second,
):
    keep, send, fine, coarse, row_out, col_in = local_grads(
        offsets, targets, grid_fine, grid_coarse, weight_in, weight_mid, weight_out
    )
    own, other, fine_grad, coarse_grad = reduce_grads(keep, send, fine, coarse, row_out, col_in)
    devices = axes_size(ROW) * axes_size(COL)
    grid_entries = (fine_grad.size + coarse_grad.size) * devices
    decoder_entries = weight_in.size + weight_mid.size + weight_out.size
    middle_step, input_step, output_step, fine_step, coarse_step = all_steps(
        own,
        other,
        fine_grad,
        coarse_grad,
        (
            mid_first[0],
            mid_second[0],
            in_first.T,
            in_second.T,
            out_first,
            out_second,
            fine_first,
            fine_second,
            coarse_first,
            coarse_second,
        ),
        decoder_entries,
        grid_entries,
    )
    return (fine_step, coarse_step, input_step.T, middle_step[None], output_step)


def solution(mesh):
    sizes = {"zl": 4, "x": 4, "y": 4, "zh": 2, "c": 2}
    mesh = Mesh(mesh.devices.reshape(tuple(sizes.values())), tuple(sizes))
    placed = (
        P(ROW, COL, None),
        P(None, None, ROW, COL),
        P(None, ROW, COL),
        P(None, ROW, COL),
        P(),
        P(),
        P(),
        P(None, ROW, COL),
        P(None, ROW, COL),
        P(None, ROW, COL),
        P(None, ROW, COL),
        P(),
        P(),
        P(),
        P(),
        P(),
        P(),
    )
    return jax.shard_map(
        shards,
        mesh=mesh,
        in_specs=placed,
        out_specs=(P(None, ROW, COL), P(None, ROW, COL), P(), P(), P()),
        check_vma=False,
    )
```

```python
import jax
import jax.numpy as jnp
from jax import lax
from jax.experimental import pallas as pl
from jax.experimental.pallas import tpu as pltpu
from jax.sharding import Mesh
from jax.sharding import PartitionSpec as P

SUB = 4
RATIO = 4
ADAM_STEP = 10

BETA_ONE = 0.9
BETA_TWO = 0.99
ADAM_EPSILON = 1e-08
CLIP_RMS = 0.01
LOSS_VALUE = 0.25
MEAN_EPSILON = 1e-06

ROW = ("zl", "x")
COL = ("y", "zh", "c")
SR = 32
SC = 128
CH = 32
CR = 8
CC = 32
HID = 512
CHAINS = 4
WIDTH = SR * SC // CHAINS
LINES = SR // CHAINS
PARTS = 1
FINE_CORNER = 64
COARSE_CORNER = 65
F32 = jnp.float32
BF16 = jnp.bfloat16
MIB = 1 << 20


def axes_size(axes):
    total = 1
    for axis in axes:
        total *= lax.axis_size(axis)
    return total


def axes_index(axes):
    index = 0
    for axis in axes:
        index = index * lax.axis_size(axis) + lax.axis_index(axis)
    return index


def shifted(block, down, right):
    rows, cols = axes_size(ROW), axes_size(COL)
    if not right:
        return lax.ppermute(block, ROW, [(i, (i + down) % rows) for i in range(rows)])
    if not down:
        return lax.ppermute(block, COL, [(i, (i + right) % cols) for i in range(cols)])
    route = [
        (r * cols + c, (r + down) % rows * cols + (c + right) % cols)
        for r in range(rows)
        for c in range(cols)
    ]
    return lax.ppermute(block, ROW + COL, route)


def meetings(block_one, block_two, axes):
    size = axes_size(axes)
    one = [(i, i ^ 1) for i in range(size)]
    two = [(i, (i + 1 if i % 2 else i - 1) % size) for i in range(size)]
    block_two = lax.ppermute(block_two, axes, two)
    return lax.ppermute(block_one, axes, one), block_two


def at_ends():
    row, col = axes_index(ROW), axes_index(COL)
    return row == 0, row == axes_size(ROW) - 1, col == 0, col == axes_size(COL) - 1


def swapped(block, axis, mask):
    size = lax.axis_size(axis)
    return lax.ppermute(block, axis, [(i, i ^ mask) for i in range(size)])


def pair_sum(values):
    values = list(values)
    while len(values) > 1:
        values = [values[i] + values[i + 1] for i in range(0, len(values), 2)]
    return values[0]


def exchange_sum(block, axis):
    return pair_sum([block] + [swapped(block, axis, d) for d in range(1, lax.axis_size(axis))])


def all_to_all(blocks):
    return lax.all_to_all(blocks, ("x", "y"), 0, 0, tiled=True)


def scatter_sum(blocks, axis):
    return pair_sum([blocks[0]] + [swapped(blocks[d], axis, d) for d in range(1, len(blocks))])


def vmem():
    return pl.BlockSpec(memory_space=pltpu.VMEM)


def smem():
    return pl.BlockSpec(memory_space=pltpu.SMEM)


def hbm():
    return pl.BlockSpec(memory_space=pltpu.HBM)


def in_hbm(array):
    return pltpu.with_memory_space_constraint(array, pltpu.HBM)


def whole(shape, memory_space=pltpu.VMEM):
    return pl.BlockSpec(shape, lambda b: (0,) * len(shape), memory_space=memory_space)


def lane_ids(rows):
    return lax.broadcasted_iota(jnp.int32, (rows, SC), 1)


def spread_lane(block, lane):
    return jnp.broadcast_to(block[:, lane : lane + 1], (block.shape[0], SC))


def dot(former, latter, former_dim=1, latter_dim=0, precision=None):
    return lax.dot_general(
        former,
        latter,
        (((former_dim,), (latter_dim,)), ((), ())),
        precision=precision,
        preferred_element_type=F32,
    )


def sigmoid(value):
    return 0.5 * jnp.tanh(0.5 * value) + 0.5


def coarse_table(shift_x):
    line = lax.broadcasted_iota(jnp.int32, (SC, SC), 0)
    sample = lax.broadcasted_iota(jnp.int32, (SC, SC), 1)
    base = sample >> 2
    fraction = ((sample & 3).astype(F32) + shift_x) * (1.0 / RATIO)
    return jnp.where(line == base, 1.0 - fraction, 0.0) + jnp.where(line == base + 1, fraction, 0.0)


def edges_kernel(fine_hbm, coarse_hbm, row_ref, col_ref, fine_ref, coarse_ref, fine, coarse, sems):
    copies = [
        pltpu.make_async_copy(fine_hbm, fine, sems.at[0]),
        pltpu.make_async_copy(coarse_hbm, coarse, sems.at[1]),
    ]
    for copy in copies:
        copy.start()
    for copy in copies:
        copy.wait()
    lane = lane_ids(CH)
    row_ref[:, 0:SC] = fine[:, 0, :]
    row_ref[:, SC:] = jnp.zeros((CH, SC), F32)
    row_ref[:, SC : SC + CC] = coarse[:, 0, :]
    coarse_ref[...] = jnp.zeros(coarse_ref.shape, F32)
    cols = jnp.zeros((CH, SC), F32)
    for i in range(SR):
        line = fine[:, i, :]
        fine_ref[i] = line
        cols = jnp.where(lane == i, spread_lane(line, 0), cols)
    for i in range(CR):
        line = coarse[:, i, :]
        coarse_ref[i, :, 0:CC] = line
        cols = jnp.where(lane == SR + i, spread_lane(line, 0), cols)
    col_ref[...] = cols


def edges(fine, coarse):
    shapes = ((CH, 2 * SC), (CH, SC), (SR, CH, SC), (CR, CH, SC))
    return pl.pallas_call(
        edges_kernel,
        out_shape=tuple(jax.ShapeDtypeStruct(d, F32) for d in shapes),
        in_specs=[hbm(), hbm()],
        out_specs=(vmem(),) * 4,
        scratch_shapes=[
            pltpu.VMEM(fine.shape, F32),
            pltpu.VMEM(coarse.shape, F32),
            pltpu.SemaphoreType.DMA((2,)),
        ],
        compiler_params=pltpu.CompilerParams(vmem_limit_bytes=8 * MIB),
        name="edges",
    )(in_hbm(fine), in_hbm(coarse))


def prepare_kernel(
    offset_hbm,
    in_hbm,
    mid_hbm,
    out_hbm,
    target_hbm,
    shift_ref,
    in_ref,
    mid_ref,
    out_ref,
    floor_ref,
    ends_ref,
    w_in,
    w_mid,
    w_out,
    targets,
    offsets,
    sems,
):
    sources = (target_hbm, in_hbm, out_hbm, offset_hbm, mid_hbm)
    copies = [
        pltpu.make_async_copy(source, target, sems.at[i])
        for i, (source, target) in enumerate(zip(sources, (targets, w_in, w_out, offsets, w_mid)))
    ]
    for copy in copies:
        copy.start()
    copies[0].wait()
    lane = lane_ids(3)
    ends = jnp.zeros((3, SC), F32)
    for i in range(SR):
        ends = jnp.where(lane == i, spread_lane(targets[2, :, i, :], SC - 1), ends)
    ends_ref[...] = jnp.zeros((8, SC), F32)
    ends_ref[0:3, :] = ends
    floor_ref[...] = jnp.zeros((8, SC), F32)
    floor_ref[0:3, :] = targets[1, :, SR - 1, :]
    copies[1].wait()
    for block in range(4):
        cols = slice(block * 128, block * 128 + 128)
        in_ref[cols, :] = w_in[:, cols].T.astype(BF16)
    copies[2].wait()
    padded = jnp.concatenate([w_out[...], jnp.zeros((13, HID), F32)], axis=0)
    out_ref[...] = padded.astype(BF16)
    copies[3].wait()
    shift_ref[...] = jnp.zeros((8, SC), F32)
    for i in range(2):
        shift = offsets[0, 0, i].astype(F32) * (1.0 / SUB)
        shift_ref[i : i + 1, :] = jnp.full((1, SC), shift, F32)
    copies[4].wait()
    mid_ref[...] = w_mid[...].astype(BF16)


def prepare(offsets, w_in, w_mid, w_out, targets):
    outs = (
        jax.ShapeDtypeStruct((8, SC), F32),
        jax.ShapeDtypeStruct((HID, 2 * CH), BF16),
        jax.ShapeDtypeStruct((HID, HID), BF16),
        jax.ShapeDtypeStruct((16, HID), BF16),
        jax.ShapeDtypeStruct((8, SC), F32),
        jax.ShapeDtypeStruct((8, SC), F32),
    )
    return pl.pallas_call(
        prepare_kernel,
        out_shape=outs,
        in_specs=[hbm()] * 5,
        out_specs=(vmem(),) * len(outs),
        scratch_shapes=[pltpu.VMEM(a.shape, F32) for a in (w_in, w_mid, w_out, targets)]
        + [pltpu.SMEM(offsets.shape, jnp.int32), pltpu.SemaphoreType.DMA((5,))],
        compiler_params=pltpu.CompilerParams(vmem_limit_bytes=8 * MIB),
        name="prepare",
    )(*(in_hbm(a) for a in (offsets, w_in, w_mid, w_out, targets)))


def turned_kernel(
    in_hbm,
    mid_hbm,
    out_hbm,
    target_hbm,
    unused_pred_ref,
    in_turned_ref,
    mid_turned_ref,
    out_turned_ref,
    target_ref,
    w_in,
    w_mid,
    w_out,
    targets,
    sems,
):
    sources = (target_hbm, in_hbm, out_hbm, mid_hbm)
    copies = [
        pltpu.make_async_copy(source, target, sems.at[i])
        for i, (source, target) in enumerate(zip(sources, (targets, w_in, w_out, w_mid)))
    ]
    for copy in copies:
        copy.start()
    target_ref[...] = jnp.zeros(target_ref.shape, F32)
    copies[0].wait()
    for i in range(SR):
        for kind in range(3):
            target_ref[kind, 0:3, i * SC : i * SC + SC] = targets[kind, :, i, :]
    copies[1].wait()
    in_turned_ref[...] = w_in[...].astype(BF16)
    copies[2].wait()
    padded = jnp.concatenate([w_out[...], jnp.zeros((13, HID), F32)], axis=0)
    for block in range(4):
        cols = slice(block * 128, block * 128 + 128)
        out_turned_ref[cols, :] = padded[:, cols].T.astype(BF16)
    copies[3].wait()
    for i in range(4):
        for j in range(4):
            rows = slice(i * 128, i * 128 + 128)
            cols = slice(j * 128, j * 128 + 128)
            mid_turned_ref[cols, rows] = w_mid[rows, cols].T.astype(BF16)


def turned(w_in, w_mid, w_out, targets, pred):
    outs = (
        jax.ShapeDtypeStruct((2 * CH, HID), BF16),
        jax.ShapeDtypeStruct((HID, HID), BF16),
        jax.ShapeDtypeStruct((HID, 16), BF16),
        jax.ShapeDtypeStruct((3, 8, SR * SC), F32),
    )
    return pl.pallas_call(
        turned_kernel,
        out_shape=outs,
        in_specs=[hbm()] * 4 + [vmem()],
        out_specs=(vmem(),) * len(outs),
        scratch_shapes=[pltpu.VMEM(a.shape, F32) for a in (w_in, w_mid, w_out, targets)]
        + [pltpu.SemaphoreType.DMA((4,))],
        compiler_params=pltpu.CompilerParams(vmem_limit_bytes=8 * MIB),
        name="turned",
    )(*(in_hbm(a) for a in (w_in, w_mid, w_out, targets)), pred)


def forward_kernel(
    shift_ref,
    fine_ref,
    coarse_ref,
    row_ref,
    col_ref,
    corner_ref,
    floor_ref,
    ends_ref,
    in_ref,
    mid_ref,
    out_ref,
    feat_ref,
    pre_ref,
    pred_ref,
    row_one_ref,
    row_two_ref,
    col_two_ref,
    col_one_ref,
):
    shift_y = shift_ref[0:1, :]
    shift_x = shift_ref[1:2, :]
    lane = lane_ids(CH)
    unused_first_row, last_row, unused_first_col, last_col = at_ends()
    row_in = jnp.where(last_row, 0.0, row_ref[...])
    col_in = jnp.where(last_col, 0.0, col_ref[...])
    corner_in = jnp.where(jnp.logical_or(last_row, last_col), 0.0, corner_ref[...])

    def across(line, following):
        moved = jnp.where(lane == SC - 1, following, pltpu.roll(line, SC - 1, 1))
        return line * (1.0 - shift_x) + moved * shift_x

    stage = []
    for i in range(CR):
        stage.append(jnp.where(lane == CC, spread_lane(col_in, SR + i), coarse_ref[i]))
    stage.append(jnp.where(lane == CC, spread_lane(corner_in, SR), row_in[:, SC:]))
    bands = dot(
        jnp.concatenate(stage, axis=0), coarse_table(shift_x), precision=lax.Precision.HIGHEST
    )
    bands = [bands[i * CH : i * CH + CH] for i in range(CR + 1)]
    lane8 = lane_ids(8)
    left = jnp.zeros((8, SC), F32)
    right = ends_ref[...]
    line = across(fine_ref[0], spread_lane(col_in, 0))
    for chain in range(CHAINS):
        tiles = []
        for k in range(LINES):
            row = chain * LINES + k
            if row + 1 < SR:
                following = across(fine_ref[row + 1], spread_lane(col_in, row + 1))
            else:
                following = across(row_in[:, 0:SC], spread_lane(corner_in, 0))
            fine = line * (1.0 - shift_y) + following * shift_y
            line = following
            band = row // RATIO
            part = (row % RATIO + shift_y) * (1.0 / RATIO)
            coarse = bands[band] * (1.0 - part) + bands[band + 1] * part
            tiles.append(jnp.concatenate([fine, coarse], axis=0).astype(BF16))
        feat = jnp.concatenate(tiles, axis=1)
        cols = slice(chain * WIDTH, chain * WIDTH + WIDTH)
        feat_ref[:, cols] = feat
        pre = dot(in_ref[...], feat)
        act = (pre * sigmoid(pre)).astype(BF16)
        pre = dot(mid_ref[...], act)
        pre_ref[:, cols] = pre
        act = (pre * sigmoid(pre)).astype(BF16)
        pred = dot(out_ref[...], act)[0:8]
        pred_ref[:, cols] = pred
        for k in range(LINES):
            row = chain * LINES + k
            tile = pred[:, k * SC : k * SC + SC]
            left = jnp.where(lane8 == row, spread_lane(tile, 0), left)
            right = right + jnp.where(lane8 == row, spread_lane(tile, SC - 1), 0.0)
        if chain == 0:
            up = pred[:, 0:SC]
    down = pred[:, WIDTH - SC :] + floor_ref[...]
    odd_row = axes_index(ROW) % 2 == 1
    odd_col = axes_index(COL) % 2 == 1
    row_one_ref[...] = jnp.where(odd_row, up, down)
    row_two_ref[...] = jnp.where(odd_row, down, up)
    col_one_ref[...] = jnp.where(odd_col, left, right)
    col_two_ref[...] = jnp.where(odd_col, right, left)


def forward(*args):
    edge = jax.ShapeDtypeStruct((8, SC), F32)
    outs = (
        jax.ShapeDtypeStruct((2 * CH, SR * SC), BF16),
        jax.ShapeDtypeStruct((HID, SR * SC), F32),
        jax.ShapeDtypeStruct((8, SR * SC), F32),
        edge,
        edge,
        edge,
        edge,
    )
    return pl.pallas_call(
        forward_kernel,
        out_shape=outs,
        in_specs=[vmem()] * len(args),
        out_specs=(vmem(),) * len(outs),
        compiler_params=pltpu.CompilerParams(vmem_limit_bytes=24 * MIB),
        name="forward",
    )(*args)


def loss_cotangent(pred_ref, target_ref, below, beside, above, before, cot):
    first_row, last_row, first_col, last_col = at_ends()
    lane = lane_ids(3)
    cot[...] = jnp.zeros(cot.shape, F32)
    line = pred_ref[0:3, 0:SC]
    row_prior = jnp.where(first_row, 0.0, line - above)
    for i in range(SR):
        if i + 1 < SR:
            following = pred_ref[0:3, (i + 1) * SC : (i + 2) * SC]
        else:
            following = below
        value_error = line - target_ref[0, 0:3, i * SC : i * SC + SC]
        row_error = following - line - target_ref[1, 0:3, i * SC : i * SC + SC]
        if i + 1 == SR:
            row_error = jnp.where(last_row, 0.0, row_error)
        beyond = jnp.where(lane == SC - 1, spread_lane(beside, i), pltpu.roll(line, SC - 1, 1))
        col_error = beyond - line - target_ref[2, 0:3, i * SC : i * SC + SC]
        col_error = jnp.where(jnp.logical_and(lane == SC - 1, last_col), 0.0, col_error)
        edge = jnp.where(first_col, 0.0, line - spread_lane(before, i))
        col_prior = jnp.where(lane == 0, edge, pltpu.roll(col_error, 1, 1))
        cot[0:3, i * SC : (i + 1) * SC] = (
            2.0 * LOSS_VALUE * value_error
            + 2.0 * (row_prior - row_error)
            + 2.0 * (col_prior - col_error)
        )
        line = following
        row_prior = row_error


def backward_kernel(
    shift_ref,
    feat_ref,
    pre_ref,
    pred_ref,
    row_one_ref,
    row_two_ref,
    col_two_ref,
    col_one_ref,
    target_ref,
    in_ref,
    in_turned_ref,
    mid_turned_ref,
    out_turned_ref,
    keep_ref,
    send_ref,
    fine_ref,
    coarse_ref,
    row_ref,
    col_ref,
    cot,
    grad_mid,
    grad_in,
    grad_out,
):
    shift_y = shift_ref[0:1, :]
    shift_x = shift_ref[1:2, :]
    lane = lane_ids(CH)
    odd_row = axes_index(ROW) % 2 == 1
    odd_col = axes_index(COL) % 2 == 1
    row_one, row_two = row_one_ref[0:3, :], row_two_ref[0:3, :]
    col_one, col_two = col_one_ref[0:3, :], col_two_ref[0:3, :]
    loss_cotangent(
        pred_ref,
        target_ref,
        jnp.where(odd_row, row_two, row_one),
        jnp.where(odd_col, col_two, col_one),
        jnp.where(odd_row, row_one, row_two),
        jnp.where(odd_col, col_one, col_two),
        cot,
    )

    def along(line):
        moved = jnp.where(lane == 0, 0.0, pltpu.roll(line, 1, 1))
        return line * (1.0 - shift_x) + moved * shift_x

    prior = jnp.zeros((CH, SC), F32)
    ends = jnp.zeros((CH, SC), F32)
    upper = jnp.zeros((CH, SC), F32)
    lower = jnp.zeros((CH, SC), F32)
    bands = []
    for chain in range(CHAINS):
        cols = slice(chain * WIDTH, chain * WIDTH + WIDTH)
        feat = feat_ref[:, cols]
        out_cot = cot[:, cols].astype(BF16)
        pre = pre_ref[:, cols]
        gate = sigmoid(pre)
        act = (pre * gate).astype(BF16)
        part = dot(out_cot, act, 1, 1)
        grad_out[...] = part if chain == 0 else grad_out[...] + part
        upward = dot(out_turned_ref[...], out_cot)
        delta = (upward * (gate * (1.0 + pre * (1.0 - gate)))).astype(BF16)
        pre = dot(in_ref[...], feat)
        gate = sigmoid(pre)
        act = (pre * gate).astype(BF16)
        part = dot(delta, act, 1, 1)
        grad_mid[...] = part if chain == 0 else grad_mid[...] + part
        upward = dot(mid_turned_ref[...], delta)
        delta = (upward * (gate * (1.0 + pre * (1.0 - gate)))).astype(BF16)
        part = dot(feat, delta, 1, 1)
        grad_in[...] = part if chain == 0 else grad_in[...] + part
        feat_grad = dot(in_turned_ref[...], delta)
        for k in range(LINES):
            row = chain * LINES + k
            fine = feat_grad[0:CH, k * SC : k * SC + SC]
            line = fine * (1.0 - shift_y) + prior * shift_y
            fine_ref[row] = along(line)
            ends = jnp.where(lane == row, spread_lane(line * shift_x, SC - 1), ends)
            prior = fine
            coarse = feat_grad[CH:, k * SC : k * SC + SC]
            weight = (row % RATIO + shift_y) * (1.0 / RATIO)
            upper += coarse * (1.0 - weight)
            lower += coarse * weight
            if row % RATIO == RATIO - 1:
                bands.append(upper)
                upper = lower
                lower = jnp.zeros((CH, SC), F32)
    bands.append(upper)
    line = prior * shift_y
    row_ref[:, 0:SC] = along(line)
    ends = jnp.where(lane == FINE_CORNER, spread_lane(line * shift_x, SC - 1), ends)
    spread = dot(
        jnp.concatenate(bands, axis=0),
        coarse_table(shift_x),
        1,
        1,
        precision=lax.Precision.HIGHEST,
    )
    for i in range(CR):
        band = spread[i * CH : i * CH + CH]
        coarse_ref[i] = jnp.where(lane < CC, band, 0.0)
        ends = jnp.where(lane == SR + i, spread_lane(band, CC), ends)
    band = spread[CR * CH :]
    row_ref[:, SC:] = jnp.where(lane < CC, band, 0.0)
    col_ref[...] = jnp.where(lane == COARSE_CORNER, spread_lane(band, CC), ends)
    core = lax.axis_index("c")
    tile = axes_index(("x", "y"))
    for d in range(16):
        chunk = tile ^ d
        band = chunk >> 1
        side = chunk & 1
        for half, target in ((core, keep_ref), (1 - core, send_ref)):
            cols = pl.ds(pl.multiple_of((half * 2 + side) * 128, 128), 128)
            target[d, 0:64, :] = grad_mid[pl.ds(pl.multiple_of(band * 64, 64), 64), cols]
            target[d, 64:72, :] = grad_in[pl.ds(pl.multiple_of(band * 8, 8), 8), cols]
            target[d, 72:80, :] = jnp.where(band == 0, grad_out[0:8, cols], 0.0)


def backward(*args):
    part = jax.ShapeDtypeStruct((16, 80, 128), F32)
    outs = (
        part,
        part,
        jax.ShapeDtypeStruct((SR, CH, SC), F32),
        jax.ShapeDtypeStruct((CR, CH, SC), F32),
        jax.ShapeDtypeStruct((CH, 2 * SC), F32),
        jax.ShapeDtypeStruct((CH, SC), F32),
    )
    return pl.pallas_call(
        backward_kernel,
        out_shape=outs,
        in_specs=[vmem()] * len(args),
        out_specs=(vmem(),) * len(outs),
        scratch_shapes=[
            pltpu.VMEM((16, SR * SC), F32),
            pltpu.VMEM((HID, HID), F32),
            pltpu.VMEM((2 * CH, HID), F32),
            pltpu.VMEM((16, HID), F32),
        ],
        compiler_params=pltpu.CompilerParams(vmem_limit_bytes=32 * MIB),
        name="backward",
    )(*args)


def turn_kernel(row_ref, col_ref, out_ref):
    lane = lane_ids(CH)
    unused_first_row, unused_last_row, first_col, unused_last_col = at_ends()
    cols = jnp.where(first_col, 0.0, col_ref[...])
    fine = jnp.where(lane == 0, spread_lane(cols, FINE_CORNER), 0.0)
    coarse = jnp.where(lane == 0, spread_lane(cols, COARSE_CORNER), 0.0)
    out_ref[:, 0:SC] = row_ref[:, 0:SC] + fine
    out_ref[:, SC:] = row_ref[:, SC:] + coarse


def turn(row_out, col_in):
    return pl.pallas_call(
        turn_kernel,
        out_shape=jax.ShapeDtypeStruct(row_out.shape, F32),
        in_specs=[vmem(), vmem()],
        out_specs=vmem(),
        compiler_params=pltpu.CompilerParams(vmem_limit_bytes=4 * MIB),
        name="turn",
    )(row_out, col_in)


def join_kernel(fine_ref, coarse_ref, row_ref, col_ref, fine_out, coarse_out, total_ref):
    lane = lane_ids(CH)
    first_row, unused_last_row, first_col, unused_last_col = at_ends()
    rows = jnp.where(first_row, 0.0, row_ref[...])
    cols = jnp.where(first_col, 0.0, col_ref[...])
    total = jnp.zeros((CH, SC), F32)
    for i in range(SR):
        line = fine_ref[i] + jnp.where(lane == 0, spread_lane(cols, i), 0.0)
        if i == 0:
            line += rows[:, 0:SC]
        fine_out[:, i, :] = line
        total += line * line
    for i in range(CR):
        line = coarse_ref[i] + jnp.where(lane == 0, spread_lane(cols, SR + i), 0.0)
        if i == 0:
            line += rows[:, SC:]
        coarse_out[:, i, :] = line[:, 0:CC]
        total += line * line
    total = jnp.sum(jnp.sum(total, axis=0, keepdims=True), axis=1, keepdims=True)
    total_ref[...] = jnp.broadcast_to(total, (8, SC))


def join(fine, coarse, row_in, col_in):
    return pl.pallas_call(
        join_kernel,
        out_shape=(
            jax.ShapeDtypeStruct((CH, SR, SC), F32),
            jax.ShapeDtypeStruct((CH, CR, CC), F32),
            jax.ShapeDtypeStruct((8, SC), F32),
        ),
        in_specs=[vmem()] * 4,
        out_specs=(vmem(),) * 3,
        compiler_params=pltpu.CompilerParams(vmem_limit_bytes=8 * MIB),
        name="join",
    )(fine, coarse, row_in, col_in)


def clip_factor(total, entries):
    return jnp.minimum(1.0, CLIP_RMS / jnp.sqrt(total / entries + MEAN_EPSILON))


def adam_step(gradient, moment_one, moment_two, clip_scale):
    clipped = gradient * clip_scale
    new_one = BETA_ONE * moment_one + (1.0 - BETA_ONE) * clipped
    new_two = BETA_TWO * moment_two + (1.0 - BETA_TWO) * clipped * clipped
    return (
        new_one
        * (1.0 / (1.0 - BETA_ONE**ADAM_STEP))
        / (jnp.sqrt(new_two * (1.0 / (1.0 - BETA_TWO**ADAM_STEP))) + ADAM_EPSILON)
    )


def steps_kernel(
    own_ref,
    other_ref,
    fine_ref,
    coarse_ref,
    mid_one_ref,
    mid_two_ref,
    in_one_ref,
    in_two_ref,
    out_one_ref,
    out_two_ref,
    fine_one_ref,
    fine_two_ref,
    coarse_one_ref,
    coarse_two_ref,
    mid_ref,
    in_ref,
    out_ref,
    fine_step_ref,
    coarse_step_ref,
    scales,
    *,
    decoder_entries,
    grid_entries,
):
    core = lax.axis_index("c")
    step = pl.program_id(0)

    @pl.when(step == 0)
    def _():
        own_sum = pair_sum([own_ref[d, 80:88, :] for d in range(16)])
        other_sum = pair_sum([other_ref[d, 80:88, :] for d in range(16)])
        totals = own_sum + other_sum
        scales[0:1, :] = clip_factor(totals[0:1, :], grid_entries)
        scales[1:2, :] = clip_factor(totals[1:2, :], decoder_entries)
        for block in range(4):
            d = block % 2
            data = jnp.where(block // 2 == core, own_ref[d, 72:80, :], other_ref[d, 72:80, :])
            cols = slice(block * 128, block * 128 + 128)
            out_ref[:, cols] = adam_step(
                data[0:3], out_one_ref[:, cols], out_two_ref[:, cols], scales[1:2, :]
            )

    grid_scale = scales[0:1, :]
    scale = scales[1:2, :]
    for k in range(8 // PARTS):
        for block in range(4):
            d = (step * (8 // PARTS) + k) * 2 + block % 2
            data = jnp.where(block // 2 == core, own_ref[d, 0:72, :], other_ref[d, 0:72, :])
            at = (slice(k * 64, k * 64 + 64), slice(block * 128, block * 128 + 128))
            mid_ref[at] = adam_step(data[0:64], mid_one_ref[at], mid_two_ref[at], scale)
            at = (slice(k * 8, k * 8 + 8), slice(block * 128, block * 128 + 128))
            in_ref[at] = adam_step(data[64:72], in_one_ref[at], in_two_ref[at], scale)
    fine_step_ref[...] = adam_step(
        fine_ref[...], fine_one_ref[...], fine_two_ref[...], grid_scale[:, None, :]
    )
    coarse_step_ref[...] = adam_step(
        coarse_ref[...], coarse_one_ref[...], coarse_two_ref[...], grid_scale[:, None, 0:CC]
    )


def all_steps(own, other, fine, coarse, moments, decoder_entries, grid_entries):
    mid = pl.BlockSpec((512 // PARTS, 512), lambda b: (b, 0))
    inner = pl.BlockSpec((64 // PARTS, 512), lambda b: (b, 0))
    outer = whole((3, 512))
    fine_spec = pl.BlockSpec((CH // PARTS, SR, SC), lambda b: (b, 0, 0))
    coarse_spec = pl.BlockSpec((CH // PARTS, CR, CC), lambda b: (b, 0, 0))
    shapes = ((512, 512), (64, 512), (3, 512), fine.shape, coarse.shape)
    return pl.pallas_call(
        lambda *refs: steps_kernel(
            *refs, decoder_entries=decoder_entries, grid_entries=grid_entries
        ),
        grid=(PARTS,),
        out_shape=tuple(jax.ShapeDtypeStruct(s, F32) for s in shapes),
        in_specs=[whole(own.shape), whole(other.shape), fine_spec, coarse_spec]
        + [mid, mid, inner, inner, outer, outer, fine_spec, fine_spec, coarse_spec, coarse_spec],
        out_specs=(mid, inner, outer, fine_spec, coarse_spec),
        scratch_shapes=[pltpu.VMEM((8, SC), F32)],
        compiler_params=pltpu.CompilerParams(vmem_limit_bytes=16 * MIB),
        name="steps",
    )(own, other, fine, coarse, *moments)


def tally_kernel(one_ref, two_ref, out_ref):
    total = one_ref[...] + two_ref[...]
    grads = total[0:80]
    squares = jnp.sum(grads * grads, axis=0, keepdims=True)
    squares = jnp.broadcast_to(jnp.sum(squares, axis=1, keepdims=True), (1, SC))
    out_ref[...] = total
    out_ref[81:82, :] = squares


def tally(one, two):
    return pl.pallas_call(
        tally_kernel,
        out_shape=jax.ShapeDtypeStruct(one.shape, F32),
        in_specs=[vmem(), vmem()],
        out_specs=vmem(),
        compiler_params=pltpu.CompilerParams(vmem_limit_bytes=4 * MIB),
        name="tally",
    )(one, two)


def reduce_grads(keep, send, fine, coarse, row_out, col_in):
    part = keep + swapped(send, "c", 1)
    part = scatter_sum([part[d * 4 : d * 4 + 4] for d in range(4)], "x")
    part, col_in = lax.optimization_barrier((part, col_in))
    row_in = shifted(turn(row_out, col_in), 1, 0)
    part = scatter_sum([part[d] for d in range(4)], "y")
    fine, coarse, grid_local = join(fine, coarse, row_in, col_in)
    part = exchange_sum(jnp.concatenate([part, grid_local]), "zl")
    across = [(i, i ^ 5) for i in range(axes_size(("zl", "zh")))]
    part = tally(part, lax.ppermute(part, ("zl", "zh"), across))
    own = all_to_all(jnp.broadcast_to(part, (16, *part.shape)))
    return own, swapped(own, "c", 1), fine, coarse


def local_grads(offsets, targets, grid_fine, grid_coarse, weight_in, weight_mid, weight_out):
    row_out, col_out, fine_lines, coarse_lines = edges(grid_fine, grid_coarse)
    corner_in = shifted(col_out, -1, -1)
    col_in = shifted(col_out, 0, -1)
    row_in = shifted(row_out, -1, 0)
    shifts, low_in, low_mid, low_out, floor, ends = prepare(
        offsets, weight_in.T, weight_mid[0], weight_out, targets
    )
    feat, pre, pred, row_one, row_two, col_two, col_one = forward(
        shifts, fine_lines, coarse_lines, row_in, col_in, corner_in, floor, ends, low_in, low_mid, low_out
    )
    late = turned(weight_in.T, weight_mid[0], weight_out, targets, pred)
    in_turned, mid_turned, out_turned, lines = late
    col_one, col_two = meetings(col_one, col_two, COL)
    halos = (*meetings(row_one, row_two, ROW), col_two, col_one)
    keep, send, fine, coarse, row_out, col_out = backward(
        shifts, feat, pre, pred, *halos, lines, low_in, in_turned, mid_turned, out_turned
    )
    return keep, send, fine, coarse, row_out, shifted(col_out, 0, 1)


def shards(
    offsets,
    targets,
    grid_fine,
    grid_coarse,
    weight_in,
    weight_mid,
    weight_out,
    fine_first,
    fine_second,
    coarse_first,
    coarse_second,
    in_first,
    in_second,
    mid_first,
    mid_second,
    out_first,
    out_second,
):
    keep, send, fine, coarse, row_out, col_in = local_grads(
        offsets, targets, grid_fine, grid_coarse, weight_in, weight_mid, weight_out
    )
    own, other, fine_grad, coarse_grad = reduce_grads(keep, send, fine, coarse, row_out, col_in)
    devices = axes_size(ROW) * axes_size(COL)
    grid_entries = (fine_grad.size + coarse_grad.size) * devices
    decoder_entries = weight_in.size + weight_mid.size + weight_out.size
    middle_step, input_step, output_step, fine_step, coarse_step = all_steps(
        own,
        other,
        fine_grad,
        coarse_grad,
        (
            mid_first[0],
            mid_second[0],
            in_first.T,
            in_second.T,
            out_first,
            out_second,
            fine_first,
            fine_second,
            coarse_first,
            coarse_second,
        ),
        decoder_entries,
        grid_entries,
    )
    return (fine_step, coarse_step, input_step.T, middle_step[None], output_step)


def solution(mesh):
    sizes = {"zl": 4, "x": 4, "y": 4, "zh": 2, "c": 2}
    mesh = Mesh(mesh.devices.reshape(tuple(sizes.values())), tuple(sizes))
    placed = (
        P(ROW, COL, None),
        P(None, None, ROW, COL),
        P(None, ROW, COL),
        P(None, ROW, COL),
        P(),
        P(),
        P(),
        P(None, ROW, COL),
        P(None, ROW, COL),
        P(None, ROW, COL),
        P(None, ROW, COL),
        P(),
        P(),
        P(),
        P(),
        P(),
        P(),
    )
    return jax.shard_map(
        shards,
        mesh=mesh,
        in_specs=placed,
        out_specs=(P(None, ROW, COL), P(None, ROW, COL), P(), P(), P()),
        check_vma=False,
    )
```
